32 devices in a mesh: dp: 8 (over z, x), tensor: 4 (over y, core).
Axes of the slice: x: 2, y: 2, z: 4, core: 2. Of those that a mesh axis runs over, the one named last changes fastest.
Arguments:
- text_in: bfloat16 [32, 512, 768], P(('dp', 'tensor')), may hold values from -6 to 6
- layout_in: bfloat16 [32, 512, 192], P(('dp', 'tensor')), may hold values from -6 to 6
- lengths: int32 [32], P('dp'), may hold values from 128 to 512, as said below
- text_mask: int32 [32, 512], P(('dp', 'tensor')), may hold values 0 or 1
- box_mask: int32 [32, 512], P(('dp', 'tensor')), may hold values from 0 to 1, as said below
- text_cot: bfloat16 [32, 512, 768], P(('dp', 'tensor')), may hold values from -6 to 6
- layout_cot: bfloat16 [32, 512, 192], P(('dp', 'tensor')), may hold values from -6 to 6
- master: float32 [4, 8, 235008], P('tensor', 'dp')
- first_moment: float32 [4, 8, 235008], P('tensor', 'dp')
- second_moment: float32 [4, 8, 235008], P('tensor', 'dp'), as said below
- ema_weights: float32 [4, 8, 235008], P('tensor', 'dp')
- vectors: float32 [12480], replicated
- vector_first: float32 [12480], replicated
- vector_second: float32 [12480], replicated
- vector_ema: float32 [12480], replicated
Outputs:
- text_out: bfloat16 [32, 512, 768], P(('dp', 'tensor'))
- layout_out: bfloat16 [32, 512, 192], P(('dp', 'tensor'))
- text_in_grad: float32 [32, 512, 768], P(('dp', 'tensor'))
- layout_in_grad: float32 [32, 512, 192], P(('dp', 'tensor'))
- grad_norm: float32 [], replicated
- new_master: float32 [4, 8, 235008], P('tensor', 'dp')
- new_first: float32 [4, 8, 235008], P('tensor', 'dp')
- new_second: float32 [4, 8, 235008], P('tensor', 'dp')
- master_bf16: bfloat16 [4, 8, 235008], P('tensor', 'dp')
- new_ema: float32 [4, 8, 235008], P('tensor', 'dp')
- new_vectors: float32 [12480], replicated
- new_vector_first: float32 [12480], replicated
- new_vector_second: float32 [12480], replicated
- vectors_bf16: bfloat16 [12480], replicated
- new_vector_ema: float32 [12480], replicated
The draws below stay inside these ranges and needn't reach their ends.
Inputs may be any that keep to these rules, and one draw needn't show every extreme that they name: `lengths`: each page has between 128 and 512 valid positions; some page is full and some has 128. `box_mask`: masked boxes come singly and as whole aligned regions of 8 positions. `second_moment`: second moments are positive.
All inputs are finite; a program needn't handle non-finite values. No bound on the sum of `text_mask` on one device may be relied on, other than what follows from the above.
Results may differ from the reference program's by a relative error of at most 0.012.
The reference program's roundings to bfloat16 on the way count: a program that leaves them out, or rounds other values in their place, can miss the bound.
Values may be sent and summed in bfloat16 or wider, within the bound.
No kernel may reach another device: no remote copies, remote signals or barrier semaphores. Data moves between devices by JAX's collectives and lax.ppermute only.
A program may use at most 192 MiB of HBM per device.

```python
import math
import jax
import jax.numpy as jnp
from jax import lax

D = 768
HEADS = 12
HT = 64
FF = 3072
L = 192
HL = 16
LF = 768
S = 512
PAGES_DEV = 4
STEP = 5
PAGES = 32
MATP = 7520256
NVEC = 12480
NPARAM = 7532736
SPAN = 235008
N_DP = 8
N_TENSOR = 4


def spread_table_drawn():
    text_spread = 1.0 / math.sqrt(D)
    layout_spread = 1.0 / math.sqrt(L)
    table = [(D * D, text_spread), (D * D, text_spread), (D * D, text_spread), (D * D, 8.0 * text_spread), (D * FF, text_spread), (FF * D, 1.0 / math.sqrt(FF)), (L * L, layout_spread), (L * L, layout_spread), (L * L, layout_spread), (L * L, 8.0 * layout_spread), (L * LF, layout_spread), (LF * L, 1.0 / math.sqrt(LF))]
    pieces = [jnp.full((count // N_TENSOR,), spread, jnp.float32) for count, spread in table]
    return jnp.broadcast_to(jnp.concatenate(pieces), (N_TENSOR, MATP // N_TENSOR)).reshape(N_TENSOR, N_DP, SPAN)


def vector_kinds():
    flags = []
    for stream_width, hidden_width in [(D, FF), (L, LF)]:
        for index in range(8):
            flags.append(jnp.full((stream_width,), 1.0 if index in (3, 6) else 0.0, jnp.float32))
        flags.append(jnp.zeros((hidden_width,), jnp.float32))
    flags.append(jnp.full((D,), 2.0, jnp.float32))
    flags.append(jnp.full((L,), 2.0, jnp.float32))
    return jnp.concatenate(flags)


def draw_lengths(key, part):
    drawn = jax.random.randint(jax.random.fold_in(key, 3), (PAGES,), S // 4, S + 1)
    return drawn.at[0].set(S).at[1].set(S // 4)


def draw_box_mask(key, part):
    single = jax.random.randint(jax.random.fold_in(key, 11), (PAGES, S), 0, 40) < 3
    regions = jax.random.randint(jax.random.fold_in(key, 12), (PAGES, S // 8), 0, 40) < 3
    region_rows = jnp.repeat(regions, 8, axis=1)
    return jnp.where(single | region_rows, 1, 0).astype(jnp.int32)


def draw_master(key, part):
    return jax.random.normal(jax.random.fold_in(key, 101), (N_TENSOR, N_DP, SPAN), jnp.float32) * spread_table_drawn()


def draw_ema_weights(key, part):
    return jax.random.normal(jax.random.fold_in(key, 102), (N_TENSOR, N_DP, SPAN), jnp.float32) * spread_table_drawn()


def draw_first_moment(key, part):
    return jax.random.normal(jax.random.fold_in(key, 103), (N_TENSOR, N_DP, SPAN), jnp.float32) / math.sqrt(NPARAM)


def draw_second_moment(key, part):
    factor = jax.random.uniform(jax.random.fold_in(key, 104), (N_TENSOR, N_DP, SPAN), jnp.float32, math.log(0.35), math.log(5.0))
    return jnp.exp(factor) / NPARAM


def vector_draw(key):
    shifts = jax.random.normal(jax.random.fold_in(key, 1), (NVEC,), jnp.float32) * 0.2
    gains = jax.random.uniform(jax.random.fold_in(key, 2), (NVEC,), jnp.float32, 0.6, 1.4)
    embeds = jax.random.normal(jax.random.fold_in(key, 3), (NVEC,), jnp.float32)
    kinds = vector_kinds()
    return jnp.where(kinds > 1.5, embeds, jnp.where(kinds > 0.5, gains, shifts))


def draw_vectors(key, part):
    return vector_draw(jax.random.fold_in(key, 105))


def draw_vector_ema(key, part):
    return vector_draw(jax.random.fold_in(key, 106))


def draw_vector_first(key, part):
    return jax.random.normal(jax.random.fold_in(key, 107), (NVEC,), jnp.float32) / math.sqrt(NPARAM)


def draw_vector_second(key, part):
    factor = jax.random.uniform(jax.random.fold_in(key, 108), (NVEC,), jnp.float32, math.log(0.67), math.log(2.7))
    return jnp.exp(factor) / NPARAM


def plant(values, own_key, smallest, top_value):
    longest = values.shape.index(max(values.shape))
    spots = []
    for shift in (0, 1):
        where = [jax.random.randint(jax.random.fold_in(own_key, axis), (), 0, length) for axis, length in enumerate(values.shape)]
        where[longest] = (where[longest] + shift) % values.shape[longest]
        spots.append(tuple(where))
    return values.at[spots[0]].set(smallest).at[spots[1]].set(top_value)


def shard_levels(rng, shape, cuts, smallest, top_value):
    level, own = 1.0, jax.random.fold_in(rng, 6)
    for axis_at, parts in cuts:
        draws = jnp.exp(jax.random.uniform(jax.random.fold_in(own, axis_at), (parts,), jnp.float32, smallest / len(cuts), top_value / len(cuts)))
        level = level * jnp.repeat(draws, shape[axis_at] // parts).reshape([-1 if axis == axis_at else 1 for axis in range(len(shape))])
    return level


def noise(own_key, dims, scale, limit, cuts=(), kind=jnp.bfloat16):
    array = jax.random.normal(own_key, dims, jnp.float32) * scale
    if len(cuts) > 0:
        array = shard_levels(own_key, dims, cuts, -0.22, 0.18) * array
    return jnp.clip(array, min=-limit, max=limit).astype(kind)


def setup_inputs(seed: int = 0) -> dict:
    arg_keys = jax.random.split(jax.random.key(seed), 16)
    return {
        "text_in": noise(arg_keys[0], (PAGES, S, D), 1.0, 6.0, ((0, 32),)),
        "layout_in": noise(arg_keys[1], (PAGES, S, L), 1.0, 6.0, ((0, 32),)),
        "lengths": draw_lengths(jax.random.fold_in(arg_keys[15], 71), 0),
        "text_mask": plant((jax.random.randint(arg_keys[3], (PAGES, S), 0, 20) < 3).astype(jnp.int32), jax.random.fold_in(arg_keys[3], 1), 0, 1),
        "box_mask": draw_box_mask(jax.random.fold_in(arg_keys[15], 71), 0),
        "text_cot": noise(arg_keys[5], (PAGES, S, D), 1.0, 6.0, ((0, 32),)),
        "layout_cot": noise(arg_keys[6], (PAGES, S, L), 1.0, 6.0, ((0, 32),)),
        "master": draw_master(jax.random.fold_in(arg_keys[15], 71), 0),
        "first_moment": draw_first_moment(jax.random.fold_in(arg_keys[15], 71), 0),
        "second_moment": draw_second_moment(jax.random.fold_in(arg_keys[15], 71), 0),
        "ema_weights": draw_ema_weights(jax.random.fold_in(arg_keys[15], 71), 0),
        "vectors": draw_vectors(jax.random.fold_in(arg_keys[15], 71), 0),
        "vector_first": draw_vector_first(jax.random.fold_in(arg_keys[15], 71), 0),
        "vector_second": draw_vector_second(jax.random.fold_in(arg_keys[15], 71), 0),
        "vector_ema": draw_vector_ema(jax.random.fold_in(arg_keys[15], 71), 0),
    }


norm_eps = 1e-05
clip_bound = 1.0
first_decay = 0.5
second_decay = 0.6
adam_floor = 1e-08
weight_decay = 0.01
vector_rate = 0.5
average_keep = 0.5
masked_score = -1e+30

@jax.custom_vjp
def low(v):
    return lax.optimization_barrier(v.astype(jnp.bfloat16)).astype(jnp.float32)

@jax.custom_vjp
def low_back(v):
    return v

def low_keep(v):
    return (low(v), None)

def low_pass(kept, grad):
    return (grad,)

def back_keep(v):
    return (v, None)

def back_low(kept, grad):
    return (low(grad),)
low.defvjp(low_keep, low_pass)
low_back.defvjp(back_keep, back_low)

def both_ways(value):
    return low_back(low(value))

def matrix_table():
    text_spread = 1.0 / math.sqrt(D)
    layout_spread = 1.0 / math.sqrt(L)
    return [(D, D, 1, text_spread), (D, D, 1, text_spread), (D, D, 1, text_spread), (D, D, 0, 8.0 * text_spread), (D, FF, 1, text_spread), (FF, D, 0, 1.0 / math.sqrt(FF)), (L, L, 1, layout_spread), (L, L, 1, layout_spread), (L, L, 1, layout_spread), (L, L, 0, 8.0 * layout_spread), (L, LF, 1, layout_spread), (LF, L, 0, 1.0 / math.sqrt(LF))]

def unflatten(master):
    shards = master.reshape(N_TENSOR, -1)
    matrices = []
    start = 0
    for height, width, split, spread in matrix_table():
        piece_height = height // N_TENSOR if split == 0 else height
        piece_width = width // N_TENSOR if split == 1 else width
        count = piece_height * piece_width
        pieces = [shards[index, start:start + count].reshape(piece_height, piece_width) for index in range(N_TENSOR)]
        matrices.append(jnp.concatenate(pieces, axis=split))
        start = start + count
    return matrices

def flatten(matrices):
    shards = []
    for index in range(N_TENSOR):
        items = []
        for matrix, entry in zip(matrices, matrix_table()):
            split = entry[2]
            count = matrix.shape[split] // N_TENSOR
            items.append(lax.slice_in_dim(matrix, index * count, (index + 1) * count, axis=split).reshape(-1))
        shards.append(jnp.concatenate(items))
    return jnp.stack(shards).reshape(N_TENSOR, N_DP, SPAN)

def spread_table():
    pieces = [jnp.full((height * width // N_TENSOR,), spread, jnp.float32) for height, width, split, spread in matrix_table()]
    return jnp.broadcast_to(jnp.concatenate(pieces), (N_TENSOR, MATP // N_TENSOR)).reshape(N_TENSOR, N_DP, SPAN)

def split_vector(flat):
    pieces = []
    start = 0
    for width in [D] * 8 + [FF] + [L] * 8 + [LF] + [D, L]:
        pieces.append(flat[start:start + width])
        start = start + width
    return pieces

def dense(acts, weight):
    return jnp.einsum('psd,de->pse', acts, weight, precision=lax.Precision.HIGHEST)

def layer_norm(value, gain, shift):
    mean = lax.optimization_barrier(jnp.mean(value, -1, keepdims=True))
    centred = value - mean
    scale = lax.rsqrt(lax.optimization_barrier(jnp.mean(centred * centred, -1, keepdims=True)) + norm_eps)
    return centred * scale * gain + shift

def heads_of(value, size):
    return value.reshape(value.shape[0], HEADS, size)

def page_attention(items):
    text_query, text_key, text_value, layout_query, layout_key, layout_value, frozen_query, frozen_key, length = items
    positions = text_query.shape[0]
    highest = lax.Precision.HIGHEST
    text_raw = low_back(jnp.einsum('qhd,khd->hqk', heads_of(text_query, HT), heads_of(text_key, HT), precision=highest) * (1.0 / math.sqrt(HT)))
    layout_raw = low_back(jnp.einsum('qhd,khd->hqk', heads_of(layout_query, HL), heads_of(layout_key, HL), precision=highest) * (1.0 / math.sqrt(HL)))
    frozen_raw = jnp.einsum('qhd,khd->hqk', heads_of(frozen_query, HL), heads_of(frozen_key, HL), precision=highest) * (1.0 / math.sqrt(HL))
    valid = jnp.arange(positions) < length
    text_scores = jnp.where(valid, text_raw + frozen_raw, masked_score)
    layout_scores = jnp.where(valid, layout_raw + text_raw, masked_score)
    text_prob = low(jax.nn.softmax(text_scores, axis=-1))
    layout_prob = low(jax.nn.softmax(layout_scores, axis=-1))
    text_context = both_ways(jnp.einsum('hqk,khd->qhd', text_prob, heads_of(text_value, HT), precision=highest).reshape(positions, D))
    layout_context = both_ways(jnp.einsum('hqk,khd->qhd', layout_prob, heads_of(layout_value, HL), precision=highest).reshape(positions, L))
    return (text_context, layout_context)

def layer_forward(params, text_raw_act, layout_raw_act, frozen, page_lengths, text_marks, box_marks):
    matrices, vectors = params
    weights = [low(matrix) for matrix in matrices]
    biases = split_vector(vectors)
    frozen_raw_act, frozen_query_weight, frozen_key_weight, frozen_vectors = frozen
    frozen_split = split_vector(frozen_vectors)
    text_flag = (text_marks > 0)[..., None]
    box_flag = (box_marks > 0)[..., None]
    text_act = jnp.where(text_flag, biases[18], text_raw_act)
    layout_act = jnp.where(box_flag, biases[19], layout_raw_act)
    frozen_act = jnp.where(box_flag, frozen_split[19], frozen_raw_act)
    text_low = low(text_act)
    layout_low = low(layout_act)
    frozen_low = low(frozen_act)
    text_query = both_ways(dense(text_low, weights[0]) + biases[0])
    text_key = both_ways(dense(text_low, weights[1]))
    text_value = both_ways(dense(text_low, weights[2]) + biases[1])
    layout_query = both_ways(dense(layout_low, weights[6]) + biases[9])
    layout_key = both_ways(dense(layout_low, weights[7]))
    layout_value = both_ways(dense(layout_low, weights[8]) + biases[10])
    frozen_query = both_ways(dense(frozen_low, low(frozen_query_weight)) + frozen_split[9])
    frozen_key = both_ways(dense(frozen_low, low(frozen_key_weight)))
    text_context, layout_context = lax.map(jax.checkpoint(page_attention), (text_query, text_key, text_value, layout_query, layout_key, layout_value, frozen_query, frozen_key, page_lengths))
    text_attn = low_back(dense(text_context, weights[3]))
    layout_attn = low_back(dense(layout_context, weights[9]))
    text_mid = layer_norm(text_attn + biases[2] + text_act, biases[3], biases[4])
    layout_mid = layer_norm(layout_attn + biases[11] + layout_act, biases[12], biases[13])
    text_up = low_back(dense(low(text_mid), weights[4]) + biases[8])
    layout_up = low_back(dense(low(layout_mid), weights[10]) + biases[17])
    text_hidden = low(jax.nn.gelu(text_up, approximate=False))
    layout_hidden = low(jax.nn.gelu(layout_up, approximate=False))
    text_down = low_back(dense(text_hidden, weights[5]))
    layout_down = low_back(dense(layout_hidden, weights[11]))
    text_final = layer_norm(text_down + biases[5] + text_mid, biases[6], biases[7])
    layout_final = layer_norm(layout_down + biases[14] + layout_mid, biases[15], biases[16])
    return (text_final, layout_final)

def adam_update(weight, gradient, first, second, average, rate, factor):
    clipped = gradient * factor
    new_first = first_decay * first + (1.0 - first_decay) * clipped
    new_second = second_decay * second + (1.0 - second_decay) * clipped * clipped
    first_hat = new_first / (1.0 - first_decay ** STEP)
    second_hat = new_second / (1.0 - second_decay ** STEP)
    updated = weight - rate * (first_hat / (jnp.sqrt(second_hat) + adam_floor) + weight_decay * weight)
    return (updated, new_first, new_second, updated.astype(jnp.bfloat16), average_keep * average + (1.0 - average_keep) * updated)

def reference(text_in, layout_in, lengths, text_mask, box_mask, text_cot, layout_cot, master, first_moment, second_moment, ema_weights, vectors, vector_first, vector_second, vector_ema):
    matrices = unflatten(master)
    groups = (text_in.astype(jnp.float32).reshape(N_DP, PAGES_DEV, S, D), layout_in.astype(jnp.float32).reshape(N_DP, PAGES_DEV, S, L), lengths.astype(jnp.int32).reshape(N_DP, PAGES_DEV), text_mask.astype(jnp.int32).reshape(N_DP, PAGES_DEV, S), box_mask.astype(jnp.int32).reshape(N_DP, PAGES_DEV, S), text_cot.astype(jnp.float32).reshape(N_DP, PAGES_DEV, S, D), layout_cot.astype(jnp.float32).reshape(N_DP, PAGES_DEV, S, L))
    start_grads = ([jnp.zeros_like(matrix) for matrix in matrices], jnp.zeros_like(vectors))

    def group_step(carry, items):
        text_act, layout_act, page_lengths, text_marks, box_marks, text_back, layout_back = items
        frozen = (layout_act, matrices[6], matrices[7], vectors)

        def run(params, text_value, layout_value, frozen_items):
            return layer_forward(params, text_value, layout_value, frozen_items, page_lengths, text_marks, box_marks)
        outputs, pull = jax.vjp(run, (matrices, vectors), text_act, layout_act, frozen)
        param_grads, text_grad, layout_grad, unused = pull((text_back, layout_back))
        carry = jax.tree.map(jnp.add, carry, param_grads)
        return (carry, (outputs[0].astype(jnp.bfloat16), outputs[1].astype(jnp.bfloat16), text_grad, layout_grad))
    totals, stacked = lax.scan(group_step, start_grads, groups)
    matrix_grads, vector_grad = totals
    flat_grad = flatten(matrix_grads)
    grad_norm = jnp.sqrt(jnp.sum(flat_grad * flat_grad) + jnp.sum(vector_grad * vector_grad))
    factor = clip_bound / jnp.maximum(grad_norm, clip_bound)
    matrix_new = adam_update(master, flat_grad, first_moment, second_moment, ema_weights, spread_table(), factor)
    vector_new = adam_update(vectors, vector_grad, vector_first, vector_second, vector_ema, vector_rate, factor)
    text_out = stacked[0].reshape(PAGES, S, D)
    layout_out = stacked[1].reshape(PAGES, S, L)
    text_in_grad = stacked[2].reshape(PAGES, S, D)
    layout_in_grad = stacked[3].reshape(PAGES, S, L)
    return (text_out, layout_out, text_in_grad, layout_in_grad, grad_norm, matrix_new[0], matrix_new[1], matrix_new[2], matrix_new[3], matrix_new[4], vector_new[0], vector_new[1], vector_new[2], vector_new[3], vector_new[4])
```

```python
from functools import partial
import math

import jax
import jax.numpy as jnp
from jax import lax
from jax.experimental import pallas as pl
from jax.experimental.pallas import tpu as pltpu
from jax.sharding import PartitionSpec as P

D = 768
HT = 64
FF = 3072
L = 192
HL = 16
LF = 768
STEP = 5


norm_eps = 1e-05
clip_bound = 1.0
first_decay = 0.5
second_decay = 0.6
adam_floor = 1e-08
weight_decay = 0.01
vector_rate = 0.5
average_keep = 0.5
masked_score = -1e30


def piece_table(parts):
    text_spread = 1.0 / math.sqrt(D)
    layout_spread = 1.0 / math.sqrt(L)
    return [
        (D, D // parts, text_spread),
        (D, D // parts, text_spread),
        (D, D // parts, text_spread),
        (D // parts, D, 8.0 * text_spread),
        (D, FF // parts, text_spread),
        (FF // parts, D, 1.0 / math.sqrt(FF)),
        (L, L // parts, layout_spread),
        (L, L // parts, layout_spread),
        (L, L // parts, layout_spread),
        (L // parts, L, 8.0 * layout_spread),
        (L, LF // parts, layout_spread),
        (LF // parts, L, 1.0 / math.sqrt(LF)),
    ]


def rate_table(parts):
    return jnp.concatenate(
        [
            jnp.full((height * width,), spread, jnp.float32)
            for height, width, spread in piece_table(parts)
        ]
    )


def split_vector(flat):
    pieces = []
    start = 0
    for width in [D] * 8 + [FF] + [L] * 8 + [LF] + [D, L]:
        pieces.append(flat[start : start + width])
        start = start + width
    return pieces


def project(acts, weight):
    return jnp.einsum("psd,de->pse", acts, weight, preferred_element_type=jnp.float32)


def project_back(incoming, weight):
    return jnp.einsum("pse,de->psd", incoming, weight, preferred_element_type=jnp.float32)


def weight_grad(acts, incoming):
    return jnp.einsum("psd,pse->de", acts, incoming, preferred_element_type=jnp.float32)


def norm_forward(value, gain, shift):
    mean = jnp.mean(value, -1, keepdims=True)
    centred = value - mean
    scale = lax.rsqrt(jnp.mean(centred * centred, -1, keepdims=True) + norm_eps)
    normed = centred * scale
    return (normed * gain + shift, normed, scale)


def norm_backward(incoming, normed, scale, gain):
    scaled = incoming * gain
    result = scale * (
        scaled
        - jnp.mean(scaled, -1, keepdims=True)
        - normed * jnp.mean(scaled * normed, -1, keepdims=True)
    )
    return (result, jnp.sum(incoming * normed, (0, 1)), jnp.sum(incoming, (0, 1)))


def gelu_back(value, incoming):
    unused, pull = jax.vjp(partial(jax.nn.gelu, approximate=False), value)
    return pull(incoming)[0]


def adam_update(weight, gradient, first, second, average, rate, factor):
    clipped = gradient * factor
    new_first = first_decay * first + (1.0 - first_decay) * clipped
    new_second = second_decay * second + (1.0 - second_decay) * clipped * clipped
    first_hat = new_first / (1.0 - first_decay**STEP)
    second_hat = new_second / (1.0 - second_decay**STEP)
    updated = weight - rate * (
        first_hat / (jnp.sqrt(second_hat) + adam_floor) + weight_decay * weight
    )
    return (
        updated,
        new_first,
        new_second,
        updated.astype(jnp.bfloat16),
        average_keep * average + (1.0 - average_keep) * updated,
    )


NT = (((1,), (1,)), ((), ()))
NN = (((1,), (0,)), ((), ()))
TN = (((0,), (0,)), ((), ()))


def dot(left, right, dims):
    return lax.dot_general(left, right, dims, preferred_element_type=jnp.float32)


def lane_of(shape):
    return lax.broadcasted_iota(jnp.int32, shape, len(shape) - 1)


def head_tiles(text_ref, layout_ref, slot, tile, high):
    first = slot * 256 + tile * 128
    text = text_ref[0, :, first : first + 128]
    layout = layout_ref[0, :, first : first + 128]
    low = lane_of(text.shape) < 64
    if high:
        return jnp.where(low, layout, text)
    return jnp.where(low, text, layout)


def own_lanes(shape, high):
    low = lane_of(shape) < 64
    return ~low if high else low


def scaled_query(query, high):
    own = own_lanes(query.shape, high)
    marker = 16 if high else 80
    scale = jnp.where(own, 0.125, 0.25)
    scaled = (query.astype(jnp.float32) * scale).astype(jnp.bfloat16)
    return jnp.where(lane_of(query.shape) == marker, jnp.bfloat16(1.0), scaled)


def masked_key(key, high, length):
    marker = 16 if high else 80
    beyond = lax.broadcasted_iota(jnp.int32, key.shape, 0) >= length
    column = jnp.where(beyond, jnp.float32(-1e30), jnp.float32(0.0)).astype(jnp.bfloat16)
    return jnp.where(lane_of(key.shape) == marker, column, key)


def attend_kernel(length_ref, text_ref, layout_ref, context_ref, layout_context_ref, total_ref):
    length = length_ref[0]
    found = []
    for head in range(3):
        tile, high = head // 2, head % 2 == 1
        query = scaled_query(head_tiles(text_ref, layout_ref, 0, tile, high), high)
        key = masked_key(head_tiles(text_ref, layout_ref, 1, tile, high), high, length)
        value = head_tiles(text_ref, layout_ref, 2, tile, high)
        scores = dot(key, query, NT)
        top = jnp.max(scores, 0, keepdims=True)
        raised = jnp.exp(scores - top)
        total = jnp.sum(raised, 0, keepdims=True)
        probs = (raised * (1.0 / total)).astype(jnp.bfloat16)
        total_ref[0, head : head + 1, :] = top + jnp.log(total)
        context = dot(value, probs, TN)
        found.append(context.T)
    low = lane_of(found[0].shape) < 64
    zero = jnp.zeros_like(found[0])
    context_ref[0, :, 0:128] = jnp.where(low, found[0], found[1]).astype(jnp.bfloat16)
    context_ref[0, :, 128:256] = jnp.where(low, found[2], zero).astype(jnp.bfloat16)
    layout_context_ref[0, :, 0:128] = jnp.where(low, found[1], found[0]).astype(jnp.bfloat16)
    layout_context_ref[0, :, 128:256] = jnp.where(low, zero, found[2]).astype(jnp.bfloat16)


def block(rows, width):
    return pl.BlockSpec((1, rows, width), lambda t: (t, 0, 0))


def attend(length, text, layout):
    parts, positions, _ = text.shape
    return pl.pallas_call(
        attend_kernel,
        grid=(parts,),
        in_specs=[
            pl.BlockSpec(memory_space=pltpu.SMEM),
            block(positions, 768),
            block(positions, 768),
        ],
        out_specs=[block(positions, 256), block(positions, 256), block(8, positions)],
        out_shape=[
            jax.ShapeDtypeStruct((parts, positions, 256), jnp.bfloat16),
            jax.ShapeDtypeStruct((parts, positions, 256), jnp.bfloat16),
            jax.ShapeDtypeStruct((parts, 8, positions), jnp.float32),
        ],
        compiler_params=pltpu.CompilerParams(vmem_limit_bytes=40 << 20),
        cost_estimate=pl.CostEstimate(flops=3 << 30, transcendentals=3 << 20, bytes_accessed=10 << 20),
        name="attend",
    )(length, text, layout)


def attend_back_kernel(
    length_ref,
    text_ref,
    layout_ref,
    total_ref,
    context_ref,
    layout_context_ref,
    context_grad_ref,
    layout_context_grad_ref,
    text_grad_ref,
    layout_grad_ref,
):
    length = length_ref[0]
    grads = ([], [], [])
    for head in range(3):
        tile, high = head // 2, head % 2 == 1
        raw_query = head_tiles(text_ref, layout_ref, 0, tile, high)
        raw_key = head_tiles(text_ref, layout_ref, 1, tile, high)
        value = head_tiles(text_ref, layout_ref, 2, tile, high)
        incoming = head_tiles(context_grad_ref, layout_context_grad_ref, 0, tile, high)
        context = head_tiles(context_ref, layout_context_ref, 0, tile, high)
        own = own_lanes(value.shape, high)
        query = scaled_query(raw_query, high)
        key = masked_key(raw_key, high, length)
        product = (incoming.astype(jnp.float32) * context.astype(jnp.float32)).T
        start = 0 if high else 64
        layout_mean = jnp.sum(product[start : start + 16], 0, keepdims=True)
        joint_mean = jnp.sum(product, 0, keepdims=True)
        zero = jnp.zeros_like(value)
        probs = jnp.exp(dot(key, query, NT) - total_ref[0, head : head + 1, :])
        value_grad = dot(probs.astype(jnp.bfloat16), incoming, NN)
        joint = (probs * (dot(value, incoming, NT) - joint_mean)).astype(jnp.bfloat16)
        alone = (
            probs * (dot(jnp.where(own, zero, value), incoming, NT) - layout_mean)
        ).astype(jnp.bfloat16)
        key_grad = jnp.where(own, dot(joint, raw_query, NN) * 0.125, dot(alone, raw_query, NN) * 0.25)
        rows = lax.broadcasted_iota(jnp.int32, (128, value.shape[0]), 0) < 64
        if high:
            rows = ~rows
        query_grad = jnp.where(
            rows, dot(raw_key, joint, TN) * 0.125, dot(raw_key, alone, TN) * 0.25
        )
        grads[0].append(query_grad.T)
        grads[1].append(key_grad)
        grads[2].append(value_grad)
    low = lane_of(grads[0][0].shape) < 64
    zero = jnp.zeros_like(grads[0][0])
    for slot in range(3):
        first, second, third = grads[slot]
        at = slot * 256
        text_grad_ref[0, :, at : at + 128] = jnp.where(low, first, second).astype(jnp.bfloat16)
        text_grad_ref[0, :, at + 128 : at + 256] = jnp.where(low, third, zero).astype(jnp.bfloat16)
        layout_grad_ref[0, :, at : at + 128] = jnp.where(low, second, first).astype(jnp.bfloat16)
        layout_grad_ref[0, :, at + 128 : at + 256] = jnp.where(low, zero, third).astype(
            jnp.bfloat16
        )


def attend_back(length, text, layout, total, context, layout_context, grad, layout_grad):
    parts, positions, _ = text.shape
    return pl.pallas_call(
        attend_back_kernel,
        grid=(parts,),
        in_specs=[
            pl.BlockSpec(memory_space=pltpu.SMEM),
            block(positions, 768),
            block(positions, 768),
            block(8, positions),
            block(positions, 256),
            block(positions, 256),
            block(positions, 256),
            block(positions, 256),
        ],
        out_specs=[block(positions, 768), block(positions, 768)],
        out_shape=[
            jax.ShapeDtypeStruct((parts, positions, 768), jnp.bfloat16),
            jax.ShapeDtypeStruct((parts, positions, 768), jnp.bfloat16),
        ],
        compiler_params=pltpu.CompilerParams(vmem_limit_bytes=40 << 20),
        cost_estimate=pl.CostEstimate(flops=12 << 30, transcendentals=3 << 20, bytes_accessed=20 << 20),
        name="attend_back",
    )(length, text, layout, total, context, layout_context, grad, layout_grad)


SPAN = 235008
FRAME = 320
UNIT = 768


def cast_kernel(shift_ref, master_ref, frame_ref, flat_ref):
    whole = SPAN // 1024
    for step in range(whole):
        flat_ref[pl.ds(8 * step, 8), :] = master_ref[0, 0, pl.ds(1024 * step, 1024)].reshape(8, 128)
    flat_ref[pl.ds(8 * whole, 4), :] = master_ref[0, 0, pl.ds(1024 * whole, 512)].reshape(4, 128)
    for column in range(6):
        rows = flat_ref[pl.ds(column, 306, stride=6), :]
        rows = jnp.concatenate((rows, jnp.zeros((14, 128), jnp.float32)), 0)
        rows = pltpu.roll(rows, shift_ref[0], 0)
        frame_ref[0, :, column * 128 : column * 128 + 128] = rows.astype(jnp.bfloat16)


def cast_frame(shift, master):
    return pl.pallas_call(
        cast_kernel,
        in_specs=[pl.BlockSpec(memory_space=pltpu.SMEM), pl.BlockSpec(memory_space=pltpu.VMEM)],
        out_specs=pl.BlockSpec(memory_space=pltpu.VMEM),
        out_shape=jax.ShapeDtypeStruct((1, FRAME, UNIT), jnp.bfloat16),
        scratch_shapes=[pltpu.VMEM((1840, 128), jnp.float32)],
        name="cast_frame",
    )(shift, master)


def finish_kernel(shift_ref, keep_ref, other_ref, flat_out_ref, square_ref, flat_ref):
    squares = jnp.zeros((8, 128), jnp.float32)
    for column in range(6):
        at = column * 128
        rows = keep_ref[:, at : at + 128].astype(jnp.float32)
        rows = rows + other_ref[:, at : at + 128].astype(jnp.float32)
        rows = pltpu.roll(rows, FRAME - shift_ref[0], 0)
        flat_ref[pl.ds(column, 306, stride=6), :] = rows[:306]
        inside = lax.broadcasted_iota(jnp.int32, rows.shape, 0) < 306
        masked = jnp.where(inside, rows, 0.0)
        squares = squares + jnp.sum((masked * masked).reshape(40, 8, 128), 0)
    square_ref[...] = squares
    whole = SPAN // 1024
    for step in range(whole):
        flat_out_ref[0, 0, pl.ds(1024 * step, 1024)] = flat_ref[pl.ds(8 * step, 8), :].reshape(1024)
    flat_out_ref[0, 0, pl.ds(1024 * whole, 512)] = flat_ref[pl.ds(8 * whole, 4), :].reshape(512)


def finish(shift, keep, other):
    return pl.pallas_call(
        finish_kernel,
        in_specs=[pl.BlockSpec(memory_space=pltpu.SMEM)]
        + [pl.BlockSpec(memory_space=pltpu.VMEM)] * 2,
        out_specs=[pl.BlockSpec(memory_space=pltpu.VMEM)] * 2,
        out_shape=[
            jax.ShapeDtypeStruct((1, 1, SPAN), jnp.float32),
            jax.ShapeDtypeStruct((8, 128), jnp.float32),
        ],
        scratch_shapes=[pltpu.VMEM((1840, 128), jnp.float32)],
        name="finish",
    )(shift, keep, other)


RATE_STEPS = (
    (0, 768.0**-0.5),
    (576, 8.0 * 768.0**-0.5),
    (768, 768.0**-0.5),
    (1536, 3072.0**-0.5),
    (2304, 192.0**-0.5),
    (2340, 8.0 * 192.0**-0.5),
    (2352, 192.0**-0.5),
    (2400, 768.0**-0.5),
)


def adam_kernel(
    first_index_ref,
    factor_ref,
    weight_ref,
    gradient_ref,
    first_ref,
    second_ref,
    average_ref,
    new_weight_ref,
    new_first_ref,
    new_second_ref,
    low_ref,
    new_average_ref,
):
    width = weight_ref.shape[2]
    start = first_index_ref[0] + pl.program_id(0) * width
    factor = factor_ref[0]
    for at in range(0, width, CHUNK):
        count = min(CHUNK, width - at)
        place = pl.ds(at, count)

        def load(ref):
            return ref[0, 0, place].reshape(count // 128, 128)

        def store(ref, value):
            ref[0, 0, place] = value.reshape(count)

        shape = (count // 128, 128)
        index = lax.broadcasted_iota(jnp.int32, shape, 0) * 128 + start + at
        rate = jnp.full(shape, RATE_STEPS[0][1], jnp.float32)
        for row, value in RATE_STEPS[1:]:
            rate = jnp.where(index >= row * UNIT, jnp.float32(value), rate)
        weight = load(weight_ref)
        clipped = load(gradient_ref) * factor
        new_first = 0.5 * load(first_ref) + 0.5 * clipped
        new_second = 0.6 * load(second_ref) + 0.4 * clipped * clipped
        first_hat = new_first * (1.0 / (1.0 - 0.5**5))
        second_hat = new_second * (1.0 / (1.0 - 0.6**5))
        updated = weight - rate * (first_hat / (jnp.sqrt(second_hat) + 1e-8) + 0.01 * weight)
        store(new_weight_ref, updated)
        store(new_first_ref, new_first)
        store(new_second_ref, new_second)
        low_ref[0, 0, place] = updated.reshape(count).astype(jnp.bfloat16)
        store(new_average_ref, 0.5 * load(average_ref) + 0.5 * updated)


CHUNK = 1024


def adam(first_index, factor, weight, gradient, first, second, average, steps=3):
    span = weight.shape[2]
    spec = pl.BlockSpec((1, 1, span // steps), lambda i: (0, 0, i))
    full = jax.ShapeDtypeStruct(weight.shape, jnp.float32)
    return pl.pallas_call(
        adam_kernel,
        grid=(steps,),
        in_specs=[pl.BlockSpec(memory_space=pltpu.SMEM)] * 2 + [spec] * 5,
        out_specs=[spec] * 5,
        out_shape=[full, full, full, jax.ShapeDtypeStruct(weight.shape, jnp.bfloat16), full],
        name="adam",
    )(first_index, factor, weight, gradient, first, second, average)


def placing(rows, columns, row_axis):
    narrow = lax.broadcasted_iota(jnp.int32, (rows, columns), row_axis)
    wide = lax.broadcasted_iota(jnp.int32, (rows, columns), 1 - row_axis)
    place = jnp.where(narrow < 16, narrow + 64, jnp.where(narrow < 32, narrow - 16, narrow + 160))
    return jnp.where(place == wide, 1.0, 0.0).astype(jnp.bfloat16)


def wide_rows(value):
    return jnp.concatenate((value, jnp.zeros((value.shape[0], 64), value.dtype)), 1)


def unpack_kernel(
    heads_ref, out_ref, small_ref, qkv_ref, wo_ref, lqkv_ref, lwo_ref, lw1_ref, lw2_ref, rows_ref, small_rows_ref
):
    def spread(source_ref, first, count, stride, target_ref):
        for step in range(4):
            piece = wide_rows(source_ref[first : first + count, 192 * step : 192 * step + 192])
            target_ref[0, pl.ds(step, count, stride=stride), :] = piece[:, :128]
            target_ref[1, pl.ds(step, count, stride=stride), :] = piece[:, 128:]

    small_rows_ref[...] = small_ref[0].astype(jnp.float32)
    for slot in range(3):
        for step in range(4):
            piece = heads_ref[0, 192 * slot : 192 * slot + 192, 192 * step : 192 * step + 192]
            piece = wide_rows(piece.astype(jnp.float32))
            rows_ref[0, pl.ds(step, 192, stride=4), :] = piece[:, :128]
            rows_ref[1, pl.ds(step, 192, stride=4), :] = piece[:, 128:]
        qkv_ref[0, :, 256 * slot : 256 * slot + 128] = rows_ref[0].astype(jnp.bfloat16)
        qkv_ref[0, :, 256 * slot + 128 : 256 * slot + 256] = rows_ref[1].astype(jnp.bfloat16)
    wo_ref[0, :192, :] = out_ref[0]
    wo_ref[0, 192:, :] = jnp.zeros((64, 768), jnp.bfloat16)
    place = placing(48, 256, 0)
    narrow = jnp.concatenate(
        [small_rows_ref[0:48, 48 * step : 48 * step + 48] for step in range(16)], 0
    )
    placed = dot(narrow.astype(jnp.bfloat16), place, NN)
    for slot in range(3):
        for step in range(16):
            piece = placed[48 * step + 12 * slot : 48 * step + 12 * slot + 12]
            rows_ref[0, pl.ds(step, 12, stride=16), :] = piece[:, :128]
            rows_ref[1, pl.ds(step, 12, stride=16), :] = piece[:, 128:]
        lqkv_ref[0, :, 256 * slot : 256 * slot + 128] = rows_ref[0, 0:192].astype(jnp.bfloat16)
        lqkv_ref[0, :, 256 * slot + 128 : 256 * slot + 256] = rows_ref[1, 0:192].astype(jnp.bfloat16)
    spread(small_rows_ref, 36, 12, 4, rows_ref)
    lwo_ref[...] = jnp.zeros_like(lwo_ref)
    for head, at in enumerate((64, 0, 192)):
        for half, width in ((0, 128), (1, 64)):
            lwo_ref[0, at : at + 16, 128 * half : 128 * half + width] = rows_ref[
                half, 16 * head : 16 * head + 16, :width
            ].astype(jnp.bfloat16)
    for first, target_ref in ((48, lw1_ref), (96, lw2_ref)):
        spread(small_rows_ref, first, 48, 4, rows_ref)
        target_ref[0, :, 0:128] = rows_ref[0, 0:192].astype(jnp.bfloat16)
        target_ref[0, :, 128:192] = rows_ref[1, 0:192, :64].astype(jnp.bfloat16)


def unpack(stack):
    parts = stack.shape[0]

    def spec(rows, width, at=0):
        return pl.BlockSpec((1, rows, width), lambda t: (t, at, 0))

    shapes = ((768, 768), (256, 768), (192, 768), (256, 192), (192, 192), (192, 192))
    return pl.pallas_call(
        unpack_kernel,
        grid=(parts,),
        in_specs=[spec(576, 768), spec(192, 768, 3), spec(144, 768, 16)],
        out_specs=[spec(*shape) for shape in shapes],
        out_shape=[jax.ShapeDtypeStruct((parts,) + shape, jnp.bfloat16) for shape in shapes],
        scratch_shapes=[pltpu.VMEM((2, 768, 128), jnp.float32), pltpu.VMEM((144, 768), jnp.float32)],
        compiler_params=pltpu.CompilerParams(vmem_limit_bytes=40 << 20),
        name="unpack",
    )(stack, stack, stack)


def pack_kernel(qkv_ref, lqkv_ref, lwo_ref, lw1_ref, lw2_ref, heads_ref, small_ref, slots_ref, small_rows_ref, rows_ref):
    for slot in range(3):
        for half in range(2):
            at = 256 * slot + 128 * half
            rows_ref[half] = qkv_ref[0, :, at : at + 128]
        for step in range(4):
            piece = jnp.concatenate(
                [rows_ref[half, pl.ds(step, 192, stride=4), :] for half in range(2)], 1
            )
            heads_ref[0, 192 * slot : 192 * slot + 192, 192 * step : 192 * step + 192] = piece[
                :, :192
            ].astype(jnp.bfloat16)
    slots_ref[...] = jnp.zeros_like(slots_ref)
    for slot in range(3):
        for half in range(2):
            at = 256 * slot + 128 * half
            rows_ref[half, 0:192] = lqkv_ref[0, :, at : at + 128]
            for step in range(16):
                row = 16 * (3 * step + slot)
                slots_ref[row : row + 12, 128 * half : 128 * half + 128] = rows_ref[
                    half, pl.ds(step, 12, stride=16), :
                ]
    placed = dot(slots_ref[...].astype(jnp.bfloat16), placing(256, 48, 1), NN)
    for slot in range(3):
        for step in range(16):
            at = 16 * (3 * step + slot)
            small_rows_ref[12 * slot : 12 * slot + 12, 48 * step : 48 * step + 48] = placed[at : at + 12]

    def gather(first, count):
        for step in range(4):
            piece = jnp.concatenate([rows_ref[half, pl.ds(step, count, stride=4), :] for half in range(2)], 1)
            small_rows_ref[first : first + count, 192 * step : 192 * step + 192] = piece[:, :192]

    for head, at in enumerate((64, 0, 192)):
        rows_ref[0, 16 * head : 16 * head + 16, :] = lwo_ref[0, at : at + 16, 0:128]
        rows_ref[1, 16 * head : 16 * head + 16, 0:64] = lwo_ref[0, at : at + 16, 128:192]
    gather(36, 12)
    for first, source_ref in ((48, lw1_ref), (96, lw2_ref)):
        rows_ref[0, 0:192, :] = source_ref[0, :, 0:128]
        rows_ref[1, 0:192, 0:64] = source_ref[0, :, 128:192]
        gather(first, 48)
    small_ref[0] = small_rows_ref[...].astype(jnp.bfloat16)


def pack(qkv, lqkv, lwo, lw1, lw2):
    parts = qkv.shape[0]

    def spec(rows, width):
        return pl.BlockSpec((1, rows, width), lambda t: (t, 0, 0))

    return pl.pallas_call(
        pack_kernel,
        grid=(parts,),
        in_specs=[spec(*item.shape[1:]) for item in (qkv, lqkv, lwo, lw1, lw2)],
        out_specs=[spec(576, 768), spec(144, 768)],
        out_shape=[
            jax.ShapeDtypeStruct((parts, 576, 768), jnp.bfloat16),
            jax.ShapeDtypeStruct((parts, 144, 768), jnp.bfloat16),
        ],
        scratch_shapes=[
            pltpu.VMEM((768, 256), jnp.float32),
            pltpu.VMEM((144, 768), jnp.float32),
            pltpu.VMEM((2, 768, 128), jnp.float32),
        ],
        compiler_params=pltpu.CompilerParams(vmem_limit_bytes=40 << 20),
        name="pack",
    )(qkv, lqkv, lwo, lw1, lw2)


def exchange_pairs(flip):
    pairs = []
    for device in range(32):
        z, x, y, core = device // 8, device // 4 % 2, device // 2 % 2, device % 2
        z, x, y, core = flip(z, x, y, core)
        pairs.append((device, z * 8 + x * 4 + y * 2 + core))
    return pairs


ROUNDS = (
    exchange_pairs(lambda z, x, y, core: (z, x, y, 1 - core)),
    exchange_pairs(lambda z, x, y, core: (z, x, 1 - y, core) if core else (z, 1 - x, y, core)),
    exchange_pairs(lambda z, x, y, core: (z, 1 - x, y, core) if core else (z, x, 1 - y, core)),
    exchange_pairs(lambda z, x, y, core: (z ^ 1, x, y, core) if core else (z ^ 2, x, y, core)),
    exchange_pairs(lambda z, x, y, core: (z ^ 2, x, y, core) if core else (z ^ 1, x, y, core)),
)


def swap(value, step):
    return lax.ppermute(value, ("dp", "tensor"), ROUNDS[step])


def total_of(value):
    for step in range(5):
        value = value + swap(value, step)
    return value


def picked(value, index, axis):
    return lax.dynamic_index_in_dim(value, index, axis, keepdims=False)


def added(left, right):
    return (left.astype(jnp.float32) + right.astype(jnp.float32)).astype(jnp.bfloat16)


def core_stage(blocks, core):
    split = blocks.reshape((2, 2) + blocks.shape[1:])
    return picked(split, core, 1), swap(picked(split, 1 - core, 1), 0)


def plane_stages(kept, received, starts, place):
    z, x, y, core = place

    def window(part, across, k):
        at = jnp.where(across == 0, starts[0][k], starts[1][k])
        where = (part, at, 0, 0)
        size = (1, 20, 16, UNIT)
        return added(
            lax.dynamic_slice(kept, where, size), lax.dynamic_slice(received, where, size)
        )

    def side(other):
        rows = []
        for entry in range(2):
            own_x, own_y = (1 - x, 1 - y) if other else (x, y)
            part = jnp.where(core == 0, entry, own_y)
            across = jnp.where(core == 0, own_x, entry)
            rows.append(jnp.concatenate([window(part, across, k) for k in range(2)], 0))
        return jnp.stack(rows)

    second = added(side(False), swap(side(True), 1))
    own = jnp.where(core == 0, y, x)
    return added(picked(second, own, 0), swap(picked(second, 1 - own, 0), 2))


def line_stages(first, second, place):
    z, x, y, core = place
    blocks = jnp.concatenate((second, first), 0)
    order = jnp.where(x == 0, jnp.array([0, 1, 2, 3]), jnp.array([0, 2, 3, 1]))
    high, low = z // 2, z % 2
    lead = jnp.where(core == 0, high, low)
    rest = jnp.where(core == 0, low, high)

    def block(leading, trailing):
        layer = jnp.where(core == 0, 2 * leading + trailing, leading + 2 * trailing)
        return picked(blocks, order[layer], 0)

    kept = jnp.stack([block(lead, entry) for entry in range(2)])
    sent = jnp.stack([block(1 - lead, entry) for entry in range(2)])
    third = added(kept, swap(sent, 3))
    return picked(third, rest, 0), swap(picked(third, 1 - rest, 0), 4)


def spaced(vector):
    gap = jnp.zeros((4, 48), vector.dtype)
    first, second, third = vector[:, 0:16], vector[:, 16:32], vector[:, 32:48]
    return jnp.concatenate((second, gap, first, gap, gap, gap[:, :16], third, gap), 1)


def unspaced(value):
    return jnp.concatenate((value[:, 64:80], value[:, 0:16], value[:, 192:208]), 1).reshape(-1)


def shards(
    text_in,
    layout_in,
    lengths,
    text_mask,
    box_mask,
    text_cot,
    layout_cot,
    master,
    first_moment,
    second_moment,
    ema_weights,
    vectors,
    vector_first,
    vector_second,
    vector_ema,
):
    parts = lax.axis_size("tensor")
    dp_count = lax.axis_size("dp")
    tensor_index = lax.axis_index("tensor")
    dp_index = lax.axis_index("dp")
    span = master.shape[2]
    near = dp_count == 8 and parts == 4
    place = (dp_index // 2, dp_index % 2, tensor_index // 2, tensor_index % 2)
    shift = (2 * dp_index).reshape(1)
    if near:
        frame = cast_frame(shift, master)
        frames = lax.all_gather(frame, ("tensor", "dp"), axis=0, tiled=True)
        frames = frames.reshape(parts, dp_count, FRAME, UNIT)
        before = jnp.pad(frames[:, :-1, 304:], ((0, 0), (1, 0), (0, 0), (0, 0)))
        stack = jnp.concatenate((frames[:, :, :16] + before, frames[:, :, 16:304]), 2)
        stack = jnp.concatenate((stack.reshape(parts, -1, UNIT), frames[:, -1, 304:]), 1)
    else:
        wire = master.reshape(-1, 192).astype(jnp.bfloat16)
        stack = lax.all_gather(wire[None], ("tensor", "dp"), axis=0, tiled=True)
        stack = stack.reshape(parts, -1, UNIT)
    qkv_weight, out_weight, lqkv_weight, lout_weight, lup_weight, ldown_weight = unpack(stack)
    up_weight, down_weight = stack[:, 768:1536], stack[:, 1536:2304]
    biases = split_vector(vectors)
    length = lax.dynamic_slice_in_dim(lengths, tensor_index, 1)

    def product(spec, left, right):
        return jnp.einsum(spec, left, right, preferred_element_type=jnp.float32)

    def over_parts(spec, left, right):
        return sum(product(spec, left[part], right[part]) for part in range(parts))

    def summed(value):
        return jnp.sum(value, 0, dtype=jnp.float32)

    def backward_norm(incoming, normed, scale, gain):
        result, gain_grad, shift_grad = norm_backward(
            incoming[None], normed[None], scale[None], gain
        )
        return result[0], gain_grad, shift_grad

    gap = jnp.zeros((parts, 64), jnp.float32)
    none = jnp.zeros((parts, 256), jnp.float32)
    qkv_bias = jnp.concatenate(
        (biases[0].reshape(parts, 192), gap, none, biases[1].reshape(parts, 192), gap), 1
    )
    lqkv_bias = jnp.concatenate(
        (spaced(biases[9].reshape(parts, 48)), none, spaced(biases[10].reshape(parts, 48))), 1
    )
    text_flag = (text_mask[0] > 0)[:, None]
    box_flag = (box_mask[0] > 0)[:, None]
    text_act = jnp.where(text_flag, biases[18], text_in[0].astype(jnp.float32))
    layout_act = jnp.where(box_flag, biases[19], layout_in[0].astype(jnp.float32))
    text_low = text_act.astype(jnp.bfloat16)
    layout_low = layout_act.astype(jnp.bfloat16)
    qkv = (product("sd,tde->tse", text_low, qkv_weight) + qkv_bias[:, None]).astype(jnp.bfloat16)
    lqkv = (product("sd,tde->tse", layout_low, lqkv_weight) + lqkv_bias[:, None]).astype(
        jnp.bfloat16
    )
    context, lcontext, log_total = attend(length, qkv, lqkv)
    text_attn = over_parts("sc,cd->sd", context, out_weight)
    layout_attn = over_parts("sc,cd->sd", lcontext, lout_weight)
    text_mid, text_normed_one, text_scale_one = norm_forward(
        text_attn + biases[2] + text_act, biases[3], biases[4]
    )
    layout_mid, layout_normed_one, layout_scale_one = norm_forward(
        layout_attn + biases[11] + layout_act, biases[12], biases[13]
    )
    text_mid_low = text_mid.astype(jnp.bfloat16)
    layout_mid_low = layout_mid.astype(jnp.bfloat16)
    text_up = product("sd,tde->tse", text_mid_low, up_weight) + biases[8].reshape(parts, 1, -1)
    layout_up = product("sd,tde->tse", layout_mid_low, lup_weight) + biases[17].reshape(
        parts, 1, -1
    )
    text_hidden = jax.nn.gelu(text_up, approximate=False).astype(jnp.bfloat16)
    layout_hidden = jax.nn.gelu(layout_up, approximate=False).astype(jnp.bfloat16)
    text_down = over_parts("se,ed->sd", text_hidden, down_weight)
    layout_down = over_parts("se,ed->sd", layout_hidden, ldown_weight)
    text_final, text_normed_two, text_scale_two = norm_forward(
        text_down + biases[5] + text_mid, biases[6], biases[7]
    )
    layout_final, layout_normed_two, layout_scale_two = norm_forward(
        layout_down + biases[14] + layout_mid, biases[15], biases[16]
    )
    text_pre_two, text_gain_two, text_shift_two = backward_norm(
        text_cot[0].astype(jnp.float32), text_normed_two, text_scale_two, biases[6]
    )
    layout_pre_two, layout_gain_two, layout_shift_two = backward_norm(
        layout_cot[0].astype(jnp.float32), layout_normed_two, layout_scale_two, biases[15]
    )
    text_down_in = text_pre_two.astype(jnp.bfloat16)
    layout_down_in = layout_pre_two.astype(jnp.bfloat16)
    text_up_grad = gelu_back(text_up, product("sd,ted->tse", text_down_in, down_weight)).astype(
        jnp.bfloat16
    )
    layout_up_grad = gelu_back(
        layout_up, product("sd,ted->tse", layout_down_in, ldown_weight)
    ).astype(jnp.bfloat16)
    down_grad = product("tse,sd->ted", text_hidden, text_down_in).astype(jnp.bfloat16)
    ldown_grad = product("tse,sd->ted", layout_hidden, layout_down_in)
    up_grad = product("sd,tse->tde", text_mid_low, text_up_grad).astype(jnp.bfloat16)
    lup_grad = product("sd,tse->tde", layout_mid_low, layout_up_grad)
    if near:
        early = jnp.concatenate((up_grad[:, 144:], down_grad[:, :608]), 1)
        early = early.reshape(parts, 77, 16, UNIT)
        early_kept, early_received = core_stage(early, place[3])
        early_sum = plane_stages(early_kept, early_received, ((19, 57), (0, 38)), place)
    text_mid_back = over_parts("se,de->sd", text_up_grad, up_weight)
    layout_mid_back = over_parts("se,de->sd", layout_up_grad, lup_weight)
    text_pre_one, text_gain_one, text_shift_one = backward_norm(
        text_pre_two + text_mid_back, text_normed_one, text_scale_one, biases[3]
    )
    layout_pre_one, layout_gain_one, layout_shift_one = backward_norm(
        layout_pre_two + layout_mid_back, layout_normed_one, layout_scale_one, biases[12]
    )
    text_attn_in = text_pre_one.astype(jnp.bfloat16)
    layout_attn_in = layout_pre_one.astype(jnp.bfloat16)
    context_grad = product("sd,tcd->tsc", text_attn_in, out_weight).astype(jnp.bfloat16)
    lcontext_grad = product("sd,tcd->tsc", layout_attn_in, lout_weight).astype(jnp.bfloat16)
    out_grad = product("tsc,sd->tcd", context, text_attn_in)[:, :192].astype(jnp.bfloat16)
    lout_grad = product("tsc,sd->tcd", lcontext, layout_attn_in)
    qkv_in, lqkv_in = attend_back(
        length, qkv, lqkv, log_total, context, lcontext, context_grad, lcontext_grad
    )
    qkv_grad = product("sd,tse->tde", text_low, qkv_in)
    lqkv_grad = product("sd,tse->tde", layout_low, lqkv_in)
    heads_grad, small_grad = pack(qkv_grad, lqkv_grad, lout_grad, lup_grad, ldown_grad)
    if near:
        late = jnp.concatenate(
            (heads_grad, out_grad, up_grad[:, :160], down_grad[:, 592:], small_grad), 1
        )
        late = late.reshape(parts, 78, 16, UNIT)
        late_kept, late_received = core_stage(late, place[3])
        late_sum = plane_stages(late_kept, late_received, ((0, 38), (19, 58)), place)
        kept, received = line_stages(early_sum, late_sum, place)
        span_grad, squares = finish(
            shift, kept.reshape(FRAME, UNIT), received.reshape(FRAME, UNIT)
        )
        local_square = jnp.sum(squares)
    else:
        flat_grad = jnp.concatenate((heads_grad, out_grad, up_grad, down_grad, small_grad), 1)
        flat_grad = flat_grad.reshape(parts * dp_count, -1, 192)
        span_grad = lax.psum_scatter(flat_grad, ("tensor", "dp"), scatter_dimension=0, tiled=True)
        span_grad = span_grad.astype(jnp.float32).reshape(master.shape)
        local_square = jnp.sum(span_grad * span_grad)
    text_full = text_pre_one + over_parts("se,de->sd", qkv_in, qkv_weight)
    layout_full = layout_pre_one + over_parts("se,de->sd", lqkv_in, lqkv_weight)
    text_in_grad = jnp.where(text_flag, 0.0, text_full)
    layout_in_grad = jnp.where(box_flag, 0.0, layout_full)
    text_embed_grad = summed(jnp.where(text_flag, text_full, 0.0))
    layout_embed_grad = summed(jnp.where(box_flag, layout_full, 0.0))
    qkv_sums = jnp.sum(qkv_in, 1, dtype=jnp.float32)
    lqkv_sums = jnp.sum(lqkv_in, 1, dtype=jnp.float32)
    vector_part = jnp.concatenate(
        [
            qkv_sums[:, 0:192].reshape(-1),
            qkv_sums[:, 512:704].reshape(-1),
            summed(text_pre_one),
            text_gain_one,
            text_shift_one,
            summed(text_pre_two),
            text_gain_two,
            text_shift_two,
            jnp.sum(text_up_grad, 1, dtype=jnp.float32).reshape(-1),
            unspaced(lqkv_sums[:, 0:256]),
            unspaced(lqkv_sums[:, 512:768]),
            summed(layout_pre_one),
            layout_gain_one,
            layout_shift_one,
            summed(layout_pre_two),
            layout_gain_two,
            layout_shift_two,
            jnp.sum(layout_up_grad, 1, dtype=jnp.float32).reshape(-1),
            text_embed_grad,
            layout_embed_grad,
        ]
    )
    if near:
        vector_grad = total_of(vector_part)
        matrix_square = total_of(local_square.reshape(1, 1))[0, 0]
    else:
        vector_grad = lax.psum(vector_part, ("dp", "tensor"))
        matrix_square = lax.psum(local_square, ("dp", "tensor"))
    grad_norm = jnp.sqrt(matrix_square + jnp.sum(vector_grad * vector_grad))
    factor = clip_bound / jnp.maximum(grad_norm, clip_bound)
    if near:
        matrix_new = adam(
            (dp_index * span).reshape(1),
            factor.reshape(1),
            master,
            span_grad,
            first_moment,
            second_moment,
            ema_weights,
        )
        matrix_new = tuple(matrix_new)
    else:
        rates = lax.dynamic_slice_in_dim(rate_table(parts), dp_index * span, span)
        matrix_new = adam_update(
            master,
            span_grad,
            first_moment,
            second_moment,
            ema_weights,
            rates.reshape(master.shape),
            factor,
        )
    vector_new = adam_update(
        vectors, vector_grad, vector_first, vector_second, vector_ema, vector_rate, factor
    )
    return (
        (
            text_final.astype(jnp.bfloat16)[None],
            layout_final.astype(jnp.bfloat16)[None],
            text_in_grad[None],
            layout_in_grad[None],
            grad_norm,
        )
        + matrix_new
        + vector_new
    )


def solution(mesh):
    in_specs = (
        P(("dp", "tensor"), None, None),
        P(("dp", "tensor"), None, None),
        P("dp"),
        P(("dp", "tensor"), None),
        P(("dp", "tensor"), None),
        P(("dp", "tensor"), None, None),
        P(("dp", "tensor"), None, None),
        P("tensor", "dp", None),
        P("tensor", "dp", None),
        P("tensor", "dp", None),
        P("tensor", "dp", None),
        P(),
        P(),
        P(),
        P(),
    )
    out_specs = (
        P(("dp", "tensor"), None, None),
        P(("dp", "tensor"), None, None),
        P(("dp", "tensor"), None, None),
        P(("dp", "tensor"), None, None),
        P(),
        P("tensor", "dp", None),
        P("tensor", "dp", None),
        P("tensor", "dp", None),
        P("tensor", "dp", None),
        P("tensor", "dp", None),
        P(),
        P(),
        P(),
        P(),
        P(),
    )
    return jax.shard_map(shards, mesh=mesh, in_specs=in_specs, out_specs=out_specs, check_vma=False)
```

```python
from functools import partial
import math

import jax
import jax.numpy as jnp
from jax import lax
from jax.experimental import pallas as pl
from jax.experimental.pallas import tpu as pltpu
from jax.sharding import PartitionSpec as P

D = 768
HT = 64
FF = 3072
L = 192
HL = 16
LF = 768
STEP = 5


norm_eps = 1e-05
clip_bound = 1.0
first_decay = 0.5
second_decay = 0.6
adam_floor = 1e-08
weight_decay = 0.01
vector_rate = 0.5
average_keep = 0.5
masked_score = -1e30


def piece_table(parts):
    text_spread = 1.0 / math.sqrt(D)
    layout_spread = 1.0 / math.sqrt(L)
    return [
        (D, D // parts, text_spread),
        (D, D // parts, text_spread),
        (D, D // parts, text_spread),
        (D // parts, D, 8.0 * text_spread),
        (D, FF // parts, text_spread),
        (FF // parts, D, 1.0 / math.sqrt(FF)),
        (L, L // parts, layout_spread),
        (L, L // parts, layout_spread),
        (L, L // parts, layout_spread),
        (L // parts, L, 8.0 * layout_spread),
        (L, LF // parts, layout_spread),
        (LF // parts, L, 1.0 / math.sqrt(LF)),
    ]


def rate_table(parts):
    return jnp.concatenate(
        [
            jnp.full((height * width,), spread, jnp.float32)
            for height, width, spread in piece_table(parts)
        ]
    )


def split_vector(flat):
    pieces = []
    start = 0
    for width in [D] * 8 + [FF] + [L] * 8 + [LF] + [D, L]:
        pieces.append(flat[start : start + width])
        start = start + width
    return pieces


def project(acts, weight):
    return jnp.einsum("psd,de->pse", acts, weight, preferred_element_type=jnp.float32)


def project_back(incoming, weight):
    return jnp.einsum("pse,de->psd", incoming, weight, preferred_element_type=jnp.float32)


def weight_grad(acts, incoming):
    return jnp.einsum("psd,pse->de", acts, incoming, preferred_element_type=jnp.float32)


def norm_forward(value, gain, shift):
    mean = jnp.mean(value, -1, keepdims=True)
    centred = value - mean
    scale = lax.rsqrt(jnp.mean(centred * centred, -1, keepdims=True) + norm_eps)
    normed = centred * scale
    return (normed * gain + shift, normed, scale)


def norm_backward(incoming, normed, scale, gain):
    scaled = incoming * gain
    result = scale * (
        scaled
        - jnp.mean(scaled, -1, keepdims=True)
        - normed * jnp.mean(scaled * normed, -1, keepdims=True)
    )
    return (result, jnp.sum(incoming * normed, (0, 1)), jnp.sum(incoming, (0, 1)))


def gelu_back(value, incoming):
    unused, pull = jax.vjp(partial(jax.nn.gelu, approximate=False), value)
    return pull(incoming)[0]


def adam_update(weight, gradient, first, second, average, rate, factor):
    clipped = gradient * factor
    new_first = first_decay * first + (1.0 - first_decay) * clipped
    new_second = second_decay * second + (1.0 - second_decay) * clipped * clipped
    first_hat = new_first / (1.0 - first_decay**STEP)
    second_hat = new_second / (1.0 - second_decay**STEP)
    updated = weight - rate * (
        first_hat / (jnp.sqrt(second_hat) + adam_floor) + weight_decay * weight
    )
    return (
        updated,
        new_first,
        new_second,
        updated.astype(jnp.bfloat16),
        average_keep * average + (1.0 - average_keep) * updated,
    )


NT = (((1,), (1,)), ((), ()))
NN = (((1,), (0,)), ((), ()))
TN = (((0,), (0,)), ((), ()))


def dot(left, right, dims):
    return lax.dot_general(left, right, dims, preferred_element_type=jnp.float32)


def kept_out(*values):
    return [pltpu.with_memory_space_constraint(value, pltpu.HBM) for value in values]


def lane_of(shape):
    return lax.broadcasted_iota(jnp.int32, shape, len(shape) - 1)


def head_tiles(text_ref, layout_ref, slot, tile, high):
    first = slot * 256 + tile * 128
    text = text_ref[0, :, first : first + 128]
    layout = layout_ref[0, :, first : first + 128]
    low = lane_of(text.shape) < 64
    if high:
        return jnp.where(low, layout, text)
    return jnp.where(low, text, layout)


def own_lanes(shape, high):
    low = lane_of(shape) < 64
    return ~low if high else low


def scaled_query(query, high):
    own = own_lanes(query.shape, high)
    marker = 16 if high else 80
    scale = jnp.where(own, 0.125, 0.25)
    scaled = (query.astype(jnp.float32) * scale).astype(jnp.bfloat16)
    return jnp.where(lane_of(query.shape) == marker, jnp.bfloat16(1.0), scaled)


def masked_key(key, high, length):
    marker = 16 if high else 80
    beyond = lax.broadcasted_iota(jnp.int32, key.shape, 0) >= length
    column = jnp.where(beyond, jnp.float32(-1e30), jnp.float32(0.0)).astype(jnp.bfloat16)
    return jnp.where(lane_of(key.shape) == marker, column, key)


def attend_kernel(length_ref, text_ref, layout_ref, context_ref, layout_context_ref, total_ref):
    length = length_ref[0]
    found = []
    for head in range(3):
        tile, high = head // 2, head % 2 == 1
        query = scaled_query(head_tiles(text_ref, layout_ref, 0, tile, high), high)
        key = masked_key(head_tiles(text_ref, layout_ref, 1, tile, high), high, length)
        value = head_tiles(text_ref, layout_ref, 2, tile, high)
        scores = dot(key, query, NT)
        top = jnp.max(scores, 0, keepdims=True)
        raised = jnp.exp(scores - top)
        total = jnp.sum(raised, 0, keepdims=True)
        probs = (raised * (1.0 / total)).astype(jnp.bfloat16)
        total_ref[0, head : head + 1, :] = top + jnp.log(total)
        context = dot(value, probs, TN)
        found.append(context.T)
    low = lane_of(found[0].shape) < 64
    zero = jnp.zeros_like(found[0])
    context_ref[0, :, 0:128] = jnp.where(low, found[0], found[1]).astype(jnp.bfloat16)
    context_ref[0, :, 128:256] = jnp.where(low, found[2], zero).astype(jnp.bfloat16)
    layout_context_ref[0, :, 0:128] = jnp.where(low, found[1], found[0]).astype(jnp.bfloat16)
    layout_context_ref[0, :, 128:256] = jnp.where(low, zero, found[2]).astype(jnp.bfloat16)


def block(rows, width):
    return pl.BlockSpec((1, rows, width), lambda t: (t, 0, 0))


def attend(length, text, layout):
    parts, positions, _ = text.shape
    return pl.pallas_call(
        attend_kernel,
        grid=(parts,),
        in_specs=[
            pl.BlockSpec(memory_space=pltpu.SMEM),
            block(positions, 768),
            block(positions, 768),
        ],
        out_specs=[block(positions, 256), block(positions, 256), block(8, positions)],
        out_shape=[
            jax.ShapeDtypeStruct((parts, positions, 256), jnp.bfloat16),
            jax.ShapeDtypeStruct((parts, positions, 256), jnp.bfloat16),
            jax.ShapeDtypeStruct((parts, 8, positions), jnp.float32),
        ],
        compiler_params=pltpu.CompilerParams(vmem_limit_bytes=24 << 20),
        cost_estimate=pl.CostEstimate(flops=3 << 30, transcendentals=3 << 20, bytes_accessed=10 << 20),
        name="attend",
    )(length, *kept_out(text, layout))


def attend_back_kernel(
    length_ref,
    text_ref,
    layout_ref,
    total_ref,
    context_ref,
    layout_context_ref,
    context_grad_ref,
    layout_context_grad_ref,
    text_grad_ref,
    layout_grad_ref,
):
    length = length_ref[0]
    grads = ([], [], [])
    for head in range(3):
        tile, high = head // 2, head % 2 == 1
        raw_query = head_tiles(text_ref, layout_ref, 0, tile, high)
        raw_key = head_tiles(text_ref, layout_ref, 1, tile, high)
        value = head_tiles(text_ref, layout_ref, 2, tile, high)
        incoming = head_tiles(context_grad_ref, layout_context_grad_ref, 0, tile, high)
        context = head_tiles(context_ref, layout_context_ref, 0, tile, high)
        own = own_lanes(value.shape, high)
        query = scaled_query(raw_query, high)
        key = masked_key(raw_key, high, length)
        product = (incoming.astype(jnp.float32) * context.astype(jnp.float32)).T
        start = 0 if high else 64
        layout_mean = jnp.sum(product[start : start + 16], 0, keepdims=True)
        joint_mean = jnp.sum(product, 0, keepdims=True)
        zero = jnp.zeros_like(value)
        probs = jnp.exp(dot(key, query, NT) - total_ref[0, head : head + 1, :])
        value_grad = dot(probs.astype(jnp.bfloat16), incoming, NN)
        joint = (probs * (dot(value, incoming, NT) - joint_mean)).astype(jnp.bfloat16)
        alone = (
            probs * (dot(jnp.where(own, zero, value), incoming, NT) - layout_mean)
        ).astype(jnp.bfloat16)
        key_grad = jnp.where(own, dot(joint, raw_query, NN) * 0.125, dot(alone, raw_query, NN) * 0.25)
        rows = lax.broadcasted_iota(jnp.int32, (128, value.shape[0]), 0) < 64
        if high:
            rows = ~rows
        query_grad = jnp.where(
            rows, dot(raw_key, joint, TN) * 0.125, dot(raw_key, alone, TN) * 0.25
        )
        grads[0].append(query_grad.T)
        grads[1].append(key_grad)
        grads[2].append(value_grad)
    low = lane_of(grads[0][0].shape) < 64
    zero = jnp.zeros_like(grads[0][0])
    for slot in range(3):
        first, second, third = grads[slot]
        at = slot * 256
        text_grad_ref[0, :, at : at + 128] = jnp.where(low, first, second).astype(jnp.bfloat16)
        text_grad_ref[0, :, at + 128 : at + 256] = jnp.where(low, third, zero).astype(jnp.bfloat16)
        layout_grad_ref[0, :, at : at + 128] = jnp.where(low, second, first).astype(jnp.bfloat16)
        layout_grad_ref[0, :, at + 128 : at + 256] = jnp.where(low, zero, third).astype(
            jnp.bfloat16
        )


def attend_back(length, text, layout, total, context, layout_context, grad, layout_grad):
    parts, positions, _ = text.shape
    return pl.pallas_call(
        attend_back_kernel,
        grid=(parts,),
        in_specs=[
            pl.BlockSpec(memory_space=pltpu.SMEM),
            block(positions, 768),
            block(positions, 768),
            block(8, positions),
            block(positions, 256),
            block(positions, 256),
            block(positions, 256),
            block(positions, 256),
        ],
        out_specs=[block(positions, 768), block(positions, 768)],
        out_shape=[
            jax.ShapeDtypeStruct((parts, positions, 768), jnp.bfloat16),
            jax.ShapeDtypeStruct((parts, positions, 768), jnp.bfloat16),
        ],
        compiler_params=pltpu.CompilerParams(vmem_limit_bytes=30 << 20),
        cost_estimate=pl.CostEstimate(flops=12 << 30, transcendentals=3 << 20, bytes_accessed=20 << 20),
        name="attend_back",
    )(length, *kept_out(text, layout, total, context, layout_context, grad, layout_grad))


SPAN = 235008
FRAME = 320
UNIT = 768


def cast_kernel(shift_ref, master_ref, frame_ref, flat_ref):
    whole = SPAN // 1024
    for step in range(whole):
        flat_ref[pl.ds(8 * step, 8), :] = master_ref[0, 0, pl.ds(1024 * step, 1024)].reshape(8, 128)
    flat_ref[pl.ds(8 * whole, 4), :] = master_ref[0, 0, pl.ds(1024 * whole, 512)].reshape(4, 128)
    for column in range(6):
        rows = flat_ref[pl.ds(column, 306, stride=6), :]
        rows = jnp.concatenate((rows, jnp.zeros((14, 128), jnp.float32)), 0)
        rows = pltpu.roll(rows, shift_ref[0], 0)
        frame_ref[0, :, column * 128 : column * 128 + 128] = rows.astype(jnp.bfloat16)


def cast_frame(shift, master):
    return pl.pallas_call(
        cast_kernel,
        in_specs=[pl.BlockSpec(memory_space=pltpu.SMEM), pl.BlockSpec(memory_space=pltpu.VMEM)],
        out_specs=pl.BlockSpec(memory_space=pltpu.VMEM),
        out_shape=jax.ShapeDtypeStruct((1, FRAME, UNIT), jnp.bfloat16),
        scratch_shapes=[pltpu.VMEM((1840, 128), jnp.float32)],
        name="cast_frame",
    )(shift, master)


def finish_kernel(shift_ref, keep_ref, other_ref, flat_out_ref, square_ref, flat_ref):
    squares = jnp.zeros((8, 128), jnp.float32)
    for column in range(6):
        at = column * 128
        rows = keep_ref[:, at : at + 128].astype(jnp.float32)
        rows = rows + other_ref[:, at : at + 128].astype(jnp.float32)
        rows = pltpu.roll(rows, FRAME - shift_ref[0], 0)
        flat_ref[pl.ds(column, 306, stride=6), :] = rows[:306]
        inside = lax.broadcasted_iota(jnp.int32, rows.shape, 0) < 306
        masked = jnp.where(inside, rows, 0.0)
        squares = squares + jnp.sum((masked * masked).reshape(40, 8, 128), 0)
    square_ref[...] = jnp.broadcast_to(jnp.sum(squares, 0, keepdims=True), square_ref.shape)
    whole = SPAN // 1024
    for step in range(whole):
        flat_out_ref[0, 0, pl.ds(1024 * step, 1024)] = flat_ref[pl.ds(8 * step, 8), :].reshape(1024)
    flat_out_ref[0, 0, pl.ds(1024 * whole, 512)] = flat_ref[pl.ds(8 * whole, 4), :].reshape(512)


def finish(shift, keep, other):
    return pl.pallas_call(
        finish_kernel,
        in_specs=[pl.BlockSpec(memory_space=pltpu.SMEM)]
        + [pl.BlockSpec(memory_space=pltpu.VMEM)] * 2,
        out_specs=[pl.BlockSpec(memory_space=pltpu.VMEM)] * 2,
        out_shape=[
            jax.ShapeDtypeStruct((1, 1, SPAN), jnp.float32),
            jax.ShapeDtypeStruct((32, 128), jnp.float32),
        ],
        scratch_shapes=[pltpu.VMEM((1840, 128), jnp.float32)],
        name="finish",
    )(shift, keep, other)


RATE_STEPS = (
    (0, 768.0**-0.5),
    (576, 8.0 * 768.0**-0.5),
    (768, 768.0**-0.5),
    (1536, 3072.0**-0.5),
    (2304, 192.0**-0.5),
    (2340, 8.0 * 192.0**-0.5),
    (2352, 192.0**-0.5),
    (2400, 768.0**-0.5),
)


def adam_kernel(
    first_index_ref,
    factor_ref,
    weight_ref,
    gradient_ref,
    first_ref,
    second_ref,
    average_ref,
    new_weight_ref,
    new_first_ref,
    new_second_ref,
    low_ref,
    new_average_ref,
):
    width = weight_ref.shape[2]
    start = first_index_ref[0] + pl.program_id(0) * width
    factor = factor_ref[0]
    for at in range(0, width, CHUNK):
        count = min(CHUNK, width - at)
        place = pl.ds(at, count)

        def load(ref):
            return ref[0, 0, place].reshape(count // 128, 128)

        def store(ref, value):
            ref[0, 0, place] = value.reshape(count)

        shape = (count // 128, 128)
        index = lax.broadcasted_iota(jnp.int32, shape, 0) * 128 + start + at
        rate = jnp.full(shape, RATE_STEPS[0][1], jnp.float32)
        for row, value in RATE_STEPS[1:]:
            rate = jnp.where(index >= row * UNIT, jnp.float32(value), rate)
        weight = load(weight_ref)
        clipped = load(gradient_ref) * factor
        new_first = 0.5 * load(first_ref) + 0.5 * clipped
        new_second = 0.6 * load(second_ref) + 0.4 * clipped * clipped
        first_hat = new_first * (1.0 / (1.0 - 0.5**5))
        second_hat = new_second * (1.0 / (1.0 - 0.6**5))
        updated = weight - rate * (first_hat / (jnp.sqrt(second_hat) + 1e-8) + 0.01 * weight)
        store(new_weight_ref, updated)
        store(new_first_ref, new_first)
        store(new_second_ref, new_second)
        low_ref[0, 0, place] = updated.reshape(count).astype(jnp.bfloat16)
        store(new_average_ref, 0.5 * load(average_ref) + 0.5 * updated)


CHUNK = 1024


def adam(first_index, factor, weight, gradient, first, second, average, steps=3):
    span = weight.shape[2]
    spec = pl.BlockSpec((1, 1, span // steps), lambda i: (0, 0, i))
    full = jax.ShapeDtypeStruct(weight.shape, jnp.float32)
    return pl.pallas_call(
        adam_kernel,
        grid=(steps,),
        in_specs=[pl.BlockSpec(memory_space=pltpu.SMEM)] * 2 + [spec] * 5,
        out_specs=[spec] * 5,
        out_shape=[full, full, full, jax.ShapeDtypeStruct(weight.shape, jnp.bfloat16), full],
        name="adam",
    )(first_index, factor, weight, gradient, first, second, average)


def placing(rows, columns, row_axis):
    narrow = lax.broadcasted_iota(jnp.int32, (rows, columns), row_axis)
    wide = lax.broadcasted_iota(jnp.int32, (rows, columns), 1 - row_axis)
    place = jnp.where(narrow < 16, narrow + 64, jnp.where(narrow < 32, narrow - 16, narrow + 160))
    return jnp.where(place == wide, 1.0, 0.0).astype(jnp.bfloat16)


def wide_rows(value):
    return jnp.concatenate((value, jnp.zeros((value.shape[0], 64), value.dtype)), 1)


def early_kernel(parts_ref, mid_ref, up_in_ref, hidden_ref, down_in_ref, early_ref, rest_ref):
    up_grad = dot(mid_ref[...], up_in_ref[0], TN)
    early_ref[0, 0:624] = up_grad[144:].astype(jnp.bfloat16)
    rest_ref[0, 0:160] = up_grad[:160].astype(jnp.bfloat16)
    down_grad = dot(hidden_ref[0], down_in_ref[...], TN)
    early_ref[0, 624:1232] = down_grad[:608].astype(jnp.bfloat16)
    rest_ref[0, 160:336] = down_grad[592:].astype(jnp.bfloat16)


def early_grads(parts, mid, up_in, hidden, down_in):
    positions = mid.shape[0]
    count = parts.shape[0]
    fixed = pl.BlockSpec((positions, 768), lambda i, p: (0, 0))
    chosen = pl.BlockSpec((1, positions, 768), lambda i, p: (p[i], 0, 0))
    return pl.pallas_call(
        early_kernel,
        grid_spec=pltpu.PrefetchScalarGridSpec(
            num_scalar_prefetch=1,
            grid=(count,),
            in_specs=[fixed, chosen, chosen, fixed],
            out_specs=[
                pl.BlockSpec((1, 1232, 768), lambda i, p: (i, 0, 0)),
                pl.BlockSpec((1, 336, 768), lambda i, p: (i, 0, 0)),
            ],
        ),
        out_shape=[
            jax.ShapeDtypeStruct((count, 1232, 768), jnp.bfloat16),
            jax.ShapeDtypeStruct((count, 336, 768), jnp.bfloat16),
        ],
        compiler_params=pltpu.CompilerParams(vmem_limit_bytes=20 << 20),
        cost_estimate=pl.CostEstimate(flops=count * 1208 << 20, transcendentals=0, bytes_accessed=count * 5 << 20),
        name="early_grads",
    )(parts, *kept_out(mid, up_in, hidden, down_in))


def late_kernel(
    parts_ref,
    text_ref,
    qkv_in_ref,
    layout_ref,
    lqkv_in_ref,
    context_ref,
    attn_in_ref,
    lcontext_ref,
    lattn_in_ref,
    lmid_ref,
    lup_in_ref,
    lhidden_ref,
    ldown_in_ref,
    rest_ref,
    late_ref,
    heads_ref,
    rows_ref,
    slots_ref,
    small_ref,
):
    heads_grad = dot(text_ref[...], qkv_in_ref[0], TN)
    for tile in range(6):
        heads_ref[tile] = heads_grad[:, 128 * tile : 128 * tile + 128]
    for slot in range(3):
        for step in range(4):
            piece = jnp.concatenate(
                [heads_ref[2 * slot + half, pl.ds(step, 192, stride=4), :] for half in range(2)], 1
            )
            late_ref[0, 192 * slot : 192 * slot + 192, 192 * step : 192 * step + 192] = piece[
                :, :192
            ].astype(jnp.bfloat16)
    late_ref[0, 576:768] = dot(context_ref[0], attn_in_ref[...], TN)[:192].astype(jnp.bfloat16)
    late_ref[0, 768:1104] = rest_ref[0]

    slots_ref[...] = jnp.zeros_like(slots_ref)
    lqkv_grad = dot(layout_ref[...], lqkv_in_ref[0], TN)
    for slot in range(3):
        for half in range(2):
            at = 256 * slot + 128 * half
            rows_ref[half, 0:192] = lqkv_grad[:, at : at + 128]
            for step in range(16):
                row = 16 * (3 * step + slot)
                slots_ref[row : row + 12, 128 * half : 128 * half + 128] = rows_ref[
                    half, pl.ds(step, 12, stride=16), :
                ]
    placed = dot(slots_ref[...].astype(jnp.bfloat16), placing(256, 48, 1), NN)
    for slot in range(3):
        for step in range(16):
            at = 16 * (3 * step + slot)
            small_ref[12 * slot : 12 * slot + 12, 48 * step : 48 * step + 48] = placed[at : at + 12]

    def gather(first, count):
        for step in range(4):
            piece = jnp.concatenate(
                [rows_ref[half, pl.ds(step, count, stride=4), :] for half in range(2)], 1
            )
            small_ref[first : first + count, 192 * step : 192 * step + 192] = piece[:, :192]

    lout_grad = dot(lcontext_ref[0], lattn_in_ref[...], TN)
    for head, at in enumerate((64, 0, 192)):
        rows_ref[0, 16 * head : 16 * head + 16, :] = lout_grad[at : at + 16, 0:128]
        rows_ref[1, 16 * head : 16 * head + 16, 0:64] = lout_grad[at : at + 16, 128:192]
    gather(36, 12)
    for first, left, right in (
        (48, lmid_ref[...], lup_in_ref[0]),
        (96, lhidden_ref[0], ldown_in_ref[...]),
    ):
        grad = dot(left, right, TN)
        rows_ref[0, 0:192, :] = grad[:, 0:128]
        rows_ref[1, 0:192, 0:64] = grad[:, 128:192]
        gather(first, 48)
    late_ref[0, 1104:1248] = small_ref[...].astype(jnp.bfloat16)


def late_grads(parts, text, qkv_in, layout, lqkv_in, context, attn_in, lcontext, lattn_in, lmid, lup_in, lhidden, ldown_in, rest):
    positions = text.shape[0]
    count = parts.shape[0]

    def fixed(width):
        return pl.BlockSpec((positions, width), lambda i, p: (0, 0))

    def chosen(width):
        return pl.BlockSpec((1, positions, width), lambda i, p: (p[i], 0, 0))

    return pl.pallas_call(
        late_kernel,
        grid_spec=pltpu.PrefetchScalarGridSpec(
            num_scalar_prefetch=1,
            grid=(count,),
            in_specs=[
                fixed(768),
                chosen(768),
                fixed(192),
                chosen(768),
                chosen(256),
                fixed(768),
                chosen(256),
                fixed(192),
                fixed(192),
                chosen(192),
                chosen(192),
                fixed(192),
                pl.BlockSpec((1, 336, 768), lambda i, p: (i, 0, 0)),
            ],
            out_specs=pl.BlockSpec((1, 1248, 768), lambda i, p: (i, 0, 0)),
            scratch_shapes=[
                pltpu.VMEM((6, 768, 128), jnp.float32),
                pltpu.VMEM((2, 192, 128), jnp.float32),
                pltpu.VMEM((768, 256), jnp.float32),
                pltpu.VMEM((144, 768), jnp.float32),
            ],
        ),
        out_shape=jax.ShapeDtypeStruct((count, 1248, 768), jnp.bfloat16),
        compiler_params=pltpu.CompilerParams(vmem_limit_bytes=26 << 20),
        cost_estimate=pl.CostEstimate(flops=count * 1208 << 20, transcendentals=0, bytes_accessed=count * 6 << 20),
        name="late_grads",
    )(parts, *kept_out(text, qkv_in, layout, lqkv_in, context, attn_in, lcontext, lattn_in, lmid, lup_in, lhidden, ldown_in, rest))


TILES = 20
HEAD_PIECES = ((0, 0, 20, 0), (1, 1, 16, 20), (1, 0, 1, 36), (7, 11, 9, 37))
OUT_PIECES = ((1, 17, 3, 0), (2, 1, 9, 3))
UP_PIECES = ((2, 10, 10, 0), (3, 1, 19, 10), (4, 1, 19, 29))
DOWN_PIECES = ((5, 1, 19, 0), (6, 1, 19, 19), (7, 1, 10, 38))
OUT_SEAMS = ((2, 2),)
UP_SEAMS = ((3, 9), (4, 28), (5, 47))
DOWN_SEAMS = ((6, 18), (7, 37))


def start_piece(table_ref, sources, part, window, first, count, target, semaphore):
    row = part * 8 + window
    for index, source in enumerate(sources):

        @pl.when(table_ref[0, row] == index)
        def start():
            place = source.at[table_ref[1, row], pl.ds(first, count)]
            pltpu.make_async_copy(place, target, semaphore).start()


def wait_piece(table_ref, sources, part, window, first, count, target, semaphore):
    pltpu.make_async_copy(sources[0].at[0, pl.ds(first, count)], target, semaphore).wait()


def unpack_kernel(
    table_ref, *refs
):
    sources = refs[:4]
    qkv_ref, lqkv_ref, lwo_ref, lw1_ref, lw2_ref, frames_ref, rows_ref, small_ref, semaphores = refs[4:]
    part = pl.program_id(0)

    def each(act, number):
        for index, (window, first, count, at) in enumerate(HEAD_PIECES):
            target = frames_ref.at[number, pl.ds(at, count)]
            act(table_ref, sources, number, window, first, count, target, semaphores.at[number, index])

    @pl.when(part == 0)
    def begin():
        for number in range(4):
            each(start_piece, number)

    each(wait_piece, part)
    frames_ref[part, 19] = frames_ref[part, 19] + frames_ref[part, 36]

    def spread(source_ref, first, count, stride, target_ref):
        for step in range(4):
            piece = wide_rows(source_ref[first : first + count, 192 * step : 192 * step + 192])
            target_ref[0, pl.ds(step, count, stride=stride), :] = piece[:, :128]
            target_ref[1, pl.ds(step, count, stride=stride), :] = piece[:, 128:]

    small_ref[...] = frames_ref[part, 37:46].reshape(144, 768).astype(jnp.float32)
    for slot in range(3):
        for step in range(4):
            piece = frames_ref[part, 12 * slot : 12 * slot + 12, :, 192 * step : 192 * step + 192]
            piece = wide_rows(piece.reshape(192, 192).astype(jnp.float32))
            rows_ref[0, pl.ds(step, 192, stride=4), :] = piece[:, :128]
            rows_ref[1, pl.ds(step, 192, stride=4), :] = piece[:, 128:]
        qkv_ref[0, :, 256 * slot : 256 * slot + 128] = rows_ref[0].astype(jnp.bfloat16)
        qkv_ref[0, :, 256 * slot + 128 : 256 * slot + 256] = rows_ref[1].astype(jnp.bfloat16)
    place = placing(48, 256, 0)
    narrow = jnp.concatenate(
        [small_ref[0:48, 48 * step : 48 * step + 48] for step in range(16)], 0
    )
    placed = dot(narrow.astype(jnp.bfloat16), place, NN)
    for slot in range(3):
        for step in range(16):
            piece = placed[48 * step + 12 * slot : 48 * step + 12 * slot + 12]
            rows_ref[0, pl.ds(step, 12, stride=16), :] = piece[:, :128]
            rows_ref[1, pl.ds(step, 12, stride=16), :] = piece[:, 128:]
        lqkv_ref[0, :, 256 * slot : 256 * slot + 128] = rows_ref[0, 0:192].astype(jnp.bfloat16)
        lqkv_ref[0, :, 256 * slot + 128 : 256 * slot + 256] = rows_ref[1, 0:192].astype(jnp.bfloat16)
    spread(small_ref, 36, 12, 4, rows_ref)
    lwo_ref[...] = jnp.zeros_like(lwo_ref)
    for head, at in enumerate((64, 0, 192)):
        for half, width in ((0, 128), (1, 64)):
            lwo_ref[0, at : at + 16, 128 * half : 128 * half + width] = rows_ref[
                half, 16 * head : 16 * head + 16, :width
            ].astype(jnp.bfloat16)
    for first, target_ref in ((48, lw1_ref), (96, lw2_ref)):
        spread(small_ref, first, 48, 4, rows_ref)
        target_ref[0, :, 0:128] = rows_ref[0, 0:192].astype(jnp.bfloat16)
        target_ref[0, :, 128:192] = rows_ref[1, 0:192, :64].astype(jnp.bfloat16)


def unpack(table, sources):
    shapes = ((768, 768), (192, 768), (256, 192), (192, 192), (192, 192))
    return pl.pallas_call(
        unpack_kernel,
        grid=(4,),
        in_specs=[pl.BlockSpec(memory_space=pltpu.SMEM)] + [pl.BlockSpec(memory_space=pl.ANY)] * 4,
        out_specs=[pl.BlockSpec((1,) + shape, lambda t: (t, 0, 0)) for shape in shapes],
        out_shape=[jax.ShapeDtypeStruct((4,) + shape, jnp.bfloat16) for shape in shapes],
        scratch_shapes=[
            pltpu.VMEM((4, 46, 16, 768), jnp.bfloat16),
            pltpu.VMEM((2, 768, 128), jnp.float32),
            pltpu.VMEM((144, 768), jnp.float32),
            pltpu.SemaphoreType.DMA((4, 4)),
        ],
        compiler_params=pltpu.CompilerParams(vmem_limit_bytes=20 << 20),
        cost_estimate=pl.CostEstimate(flops=1 << 30, transcendentals=0, bytes_accessed=14 << 20),
        name="unpack",
    )(table, *sources)


def assemble_kernel(early_table_ref, late_table_ref, *refs):
    early, late = refs[0:4], refs[4:8]
    out_ref, up_ref, down_ref, seams_ref, semaphores = refs[8:]
    matrices = (
        (OUT_PIECES, OUT_SEAMS, out_ref),
        (UP_PIECES, UP_SEAMS, up_ref),
        (DOWN_PIECES, DOWN_SEAMS, down_ref),
    )

    def each(act, part):
        index = 0
        seam = 0
        for pieces, seams, target_ref in matrices:
            for window, first, count, at in pieces + tuple((w, 0, 1, None) for w, _ in seams):
                if at is None:
                    target = seams_ref.at[part, pl.ds(seam, 1)]
                    seam += 1
                else:
                    target = target_ref.at[part, pl.ds(at, count)]
                table_ref, sources = (
                    (early_table_ref, early) if window // 2 in (0, 3) else (late_table_ref, late)
                )
                act(table_ref, sources, part, window, first, count, target, semaphores.at[part, index])
                index += 1

    def begin(part, carry):
        each(start_piece, part)
        return carry

    def end(part, carry):
        each(wait_piece, part)
        seam = 0
        for _, seams, target_ref in matrices:
            for _, at in seams:
                target_ref[part, at] = target_ref[part, at] + seams_ref[part, seam]
                seam += 1
        return carry

    lax.fori_loop(0, 4, begin, 0)
    out_ref[:, 12:16] = jnp.zeros((4, 4, 16, 768), jnp.bfloat16)
    lax.fori_loop(0, 4, end, 0)


def assemble(early_table, late_table, early, late):
    shapes = ((4, 16, 16, 768), (4, 48, 16, 768), (4, 48, 16, 768))
    results = pl.pallas_call(
        assemble_kernel,
        in_specs=[pl.BlockSpec(memory_space=pltpu.SMEM)] * 2
        + [pl.BlockSpec(memory_space=pl.ANY)] * 8,
        out_specs=[pl.BlockSpec(memory_space=pltpu.VMEM)] * 3,
        out_shape=[jax.ShapeDtypeStruct(shape, jnp.bfloat16) for shape in shapes],
        scratch_shapes=[
            pltpu.VMEM((4, 6, 16, 768), jnp.bfloat16),
            pltpu.SemaphoreType.DMA((4, 14)),
        ],
        compiler_params=pltpu.CompilerParams(vmem_limit_bytes=20 << 20),
        cost_estimate=pl.CostEstimate(flops=1 << 20, transcendentals=0, bytes_accessed=22 << 20),
        name="assemble",
    )(early_table, late_table, *early, *late)
    return [item.reshape(4, -1, 768) for item in results]


def gelu_parts(value):
    below = 0.5 + 0.5 * lax.erf(value * 0.5**0.5)
    decay = jnp.exp(value * value * -0.5)
    return value * below, below + value * decay * 0.3989422804014327


def normed_rows(value):
    mean = jnp.mean(value, -1, keepdims=True)
    centred = value - mean
    scale = lax.rsqrt(jnp.mean(centred * centred, -1, keepdims=True) + 1e-5)
    return centred * scale, scale


def norm_pull(incoming, normed, scale, gain):
    scaled = incoming * gain
    return scale * (
        scaled
        - jnp.mean(scaled, -1, keepdims=True)
        - normed * jnp.mean(scaled * normed, -1, keepdims=True)
    )


def column_sums(target_ref, *values):
    for row, value in enumerate(values):
        target_ref[row : row + 1] = jnp.sum(value, 0, keepdims=True)


def forward_kernel(*refs):
    streams = (refs[0:7] + refs[14:20] + refs[26:27], refs[7:14] + refs[20:26] + refs[27:28])
    part = pl.program_id(0)
    for (
        mid_ref,
        mid_low_ref,
        up_ref,
        up_bias_ref,
        down_ref,
        rows_ref,
        cotangent_ref,
        hidden_ref,
        slope_ref,
        final_ref,
        pre_ref,
        pre_low_ref,
        sums_ref,
        total_ref,
    ) in streams:
        hidden, slope = gelu_parts(dot(mid_low_ref[...], up_ref[0], NN) + up_bias_ref[0])
        hidden = hidden.astype(jnp.bfloat16)
        hidden_ref[0] = hidden
        slope_ref[0] = slope.astype(jnp.bfloat16)
        down = dot(hidden, down_ref[0], NN)

        @pl.when(part == 0)
        def first():
            total_ref[...] = down

        @pl.when(part > 0)
        def later():
            total_ref[...] = total_ref[...] + down

        @pl.when(part == pl.num_programs(0) - 1)
        def last():
            gain = rows_ref[6:7]
            normed, scale = normed_rows(total_ref[...] + rows_ref[5:6] + mid_ref[...])
            final_ref[0] = (normed * gain + rows_ref[7:8]).astype(jnp.bfloat16)
            incoming = cotangent_ref[0].astype(jnp.float32)
            pre = norm_pull(incoming, normed, scale, gain)
            pre_ref[...] = pre
            pre_low_ref[...] = pre.astype(jnp.bfloat16)
            column_sums(sums_ref, pre, incoming * normed, incoming)


def backward_kernel(*refs):
    streams = (refs[0:8] + refs[16:21] + refs[26:27], refs[8:16] + refs[21:26] + refs[27:28])
    part = pl.program_id(0)
    for (
        pre_ref,
        pre_low_ref,
        down_ref,
        slope_ref,
        up_ref,
        normed_ref,
        scale_ref,
        rows_ref,
        up_in_ref,
        up_sum_ref,
        attn_ref,
        attn_low_ref,
        sums_ref,
        total_ref,
    ) in streams:
        up_in = dot(pre_low_ref[...], down_ref[0], NT) * slope_ref[0].astype(jnp.float32)
        up_in = up_in.astype(jnp.bfloat16)
        up_in_ref[0] = up_in
        up_sum_ref[0] = jnp.sum(up_in.astype(jnp.float32), 0, keepdims=True)
        back = dot(up_in, up_ref[0], NT)

        @pl.when(part == 0)
        def first():
            total_ref[...] = back

        @pl.when(part > 0)
        def later():
            total_ref[...] = total_ref[...] + back

        @pl.when(part == pl.num_programs(0) - 1)
        def last():
            incoming = total_ref[...] + pre_ref[...]
            normed = normed_ref[...]
            attn = norm_pull(incoming, normed, scale_ref[...], rows_ref[3:4])
            attn_ref[...] = attn
            attn_low_ref[...] = attn.astype(jnp.bfloat16)
            column_sums(sums_ref, attn, incoming * normed, incoming)


def whole(*shape):
    return pl.BlockSpec(shape, lambda t: (0,) * len(shape))


def by_part(*shape):
    return pl.BlockSpec((1,) + shape, lambda t: (t,) + (0,) * len(shape))


def feed_forward(text, layout):
    parts, positions = text[2].shape[0], text[0].shape[0]
    in_specs, out_specs, out_shape, scratch = [], [], [], []
    for stream in (text, layout):
        width, hidden = stream[2].shape[1:]
        in_specs += [
            whole(positions, width),
            whole(positions, width),
            by_part(width, hidden),
            by_part(1, hidden),
            by_part(hidden, width),
            whole(8, width),
            whole(1, positions, width),
        ]
        out_specs += [
            by_part(positions, hidden),
            by_part(positions, hidden),
            whole(1, positions, width),
            whole(positions, width),
            whole(positions, width),
            whole(8, width),
        ]
        out_shape += [
            jax.ShapeDtypeStruct((parts, positions, hidden), jnp.bfloat16),
            jax.ShapeDtypeStruct((parts, positions, hidden), jnp.bfloat16),
            jax.ShapeDtypeStruct((1, positions, width), jnp.bfloat16),
            jax.ShapeDtypeStruct((positions, width), jnp.float32),
            jax.ShapeDtypeStruct((positions, width), jnp.bfloat16),
            jax.ShapeDtypeStruct((8, width), jnp.float32),
        ]
        scratch.append(pltpu.VMEM((positions, width), jnp.float32))
    results = pl.pallas_call(
        forward_kernel,
        grid=(parts,),
        in_specs=in_specs,
        out_specs=out_specs,
        out_shape=out_shape,
        scratch_shapes=scratch,
        compiler_params=pltpu.CompilerParams(vmem_limit_bytes=36 << 20),
        cost_estimate=pl.CostEstimate(flops=6 << 30, transcendentals=4 << 20, bytes_accessed=28 << 20),
        name="feed_forward",
    )(*kept_out(*text, *layout))
    return results[:6], results[6:]


def feed_back(text, layout):
    parts, positions = text[2].shape[0], text[0].shape[0]
    in_specs, out_specs, out_shape, scratch = [], [], [], []
    for stream in (text, layout):
        width, hidden = stream[4].shape[1:]
        in_specs += [
            whole(positions, width),
            whole(positions, width),
            by_part(hidden, width),
            by_part(positions, hidden),
            by_part(width, hidden),
            whole(positions, width),
            whole(positions, 1),
            whole(8, width),
        ]
        out_specs += [
            by_part(positions, hidden),
            by_part(1, hidden),
            whole(positions, width),
            whole(positions, width),
            whole(8, width),
        ]
        out_shape += [
            jax.ShapeDtypeStruct((parts, positions, hidden), jnp.bfloat16),
            jax.ShapeDtypeStruct((parts, 1, hidden), jnp.float32),
            jax.ShapeDtypeStruct((positions, width), jnp.float32),
            jax.ShapeDtypeStruct((positions, width), jnp.bfloat16),
            jax.ShapeDtypeStruct((8, width), jnp.float32),
        ]
        scratch.append(pltpu.VMEM((positions, width), jnp.float32))
    results = pl.pallas_call(
        backward_kernel,
        grid=(parts,),
        in_specs=in_specs,
        out_specs=out_specs,
        out_shape=out_shape,
        scratch_shapes=scratch,
        compiler_params=pltpu.CompilerParams(vmem_limit_bytes=36 << 20),
        cost_estimate=pl.CostEstimate(flops=6 << 30, transcendentals=0, bytes_accessed=28 << 20),
        name="feed_back",
    )(*kept_out(*text, *layout))
    return results[:5], results[5:]


EARLY_STARTS = ((19, 57), (0, 38))
LATE_STARTS = ((0, 38), (19, 58))


def exchange_pairs(flip):
    pairs = []
    for device in range(32):
        z, x, y, core = device // 8, device // 4 % 2, device // 2 % 2, device % 2
        z, x, y, core = flip(z, x, y, core)
        pairs.append((device, z * 8 + x * 4 + y * 2 + core))
    return pairs


ROUNDS = (
    exchange_pairs(lambda z, x, y, core: (z, x, y, 1 - core)),
    exchange_pairs(lambda z, x, y, core: (z, x, 1 - y, core) if core else (z, 1 - x, y, core)),
    exchange_pairs(lambda z, x, y, core: (z, 1 - x, y, core) if core else (z, x, 1 - y, core)),
    exchange_pairs(lambda z, x, y, core: (z ^ 1, x, y, core) if core else (z ^ 2, x, y, core)),
    exchange_pairs(lambda z, x, y, core: (z ^ 2, x, y, core) if core else (z ^ 1, x, y, core)),
)


def swap(value, step):
    return lax.ppermute(value, ("dp", "tensor"), ROUNDS[step])


def after(value, *others):
    return lax.optimization_barrier((value, others))[0]


def picked(value, index, axis):
    return lax.dynamic_index_in_dim(value, index, axis, keepdims=False)


def total_low(*values):
    return sum(value.astype(jnp.float32) for value in values).astype(jnp.bfloat16)


def windows(value, starts, place, entry, other):
    z, x, y, core = place
    own_x, own_y = (1 - x, 1 - y) if other else (x, y)
    part = jnp.where(core == 0, entry, own_y)
    across = jnp.where(core == 0, own_x, entry)
    value = value.reshape(2, -1, 16, UNIT)
    size = (1, 20, 16, UNIT)
    pieces = []
    for k in range(2):
        at = jnp.where(across == 0, starts[0][k], starts[1][k])
        pieces.append(lax.dynamic_slice(value, (part, at, 0, 0), size))
    return jnp.concatenate(pieces, 0)


def first_sent(kept, received, starts, place):
    return jnp.stack(
        [
            total_low(*(windows(item, starts, place, entry, True) for item in (kept, received)))
            for entry in range(2)
        ]
    )


def second_part(kept, received, second, starts, place, own):
    z, x, y, core = place
    entry = jnp.where(core == 0, y, x)
    entry = entry if own else 1 - entry
    return (
        windows(kept, starts, place, entry, False),
        windows(received, starts, place, entry, False),
        picked(second, entry, 0),
    )


def line_stages(early, late, earlier, place):
    z, x, y, core = place
    blocks = jnp.concatenate((late, early), 0)
    order = jnp.where(x == 0, jnp.array([0, 1, 2, 3]), jnp.array([0, 2, 3, 1]))
    high, low = z // 2, z % 2
    lead = jnp.where(core == 0, high, low)
    rest = jnp.where(core == 0, low, high)

    def block(leading, trailing):
        layer = jnp.where(core == 0, 2 * leading + trailing, leading + 2 * trailing)
        return picked(blocks, order[layer], 0)

    sent = jnp.stack([block(1 - lead, entry) for entry in range(2)])
    third = swap(after(sent, earlier), 3)
    last = swap(total_low(block(lead, 1 - rest), picked(third, 1 - rest, 0)), 4)
    return total_low(block(lead, rest), picked(third, rest, 0)), last


def gather_pieces(frame, place):
    z, x, y, core = place
    own = frame.reshape(TILES, 16, UNIT)
    near = swap(own, 4)
    lead = jnp.where(core == 0, z // 2, z % 2)
    outer = (z == 0) | (z == 3)
    groups = []
    for first in (True, False):
        sent = jnp.where(outer == first, own, near)
        if groups:
            sent = after(sent, groups[0][1])
        groups.append((sent, swap(sent, 3)))
    part = jnp.arange(32) // 8
    window = jnp.arange(32) % 8
    its_z, its_x, its_y, its_core = window // 2, window % 2, part // 2, part % 2
    off_x, off_y = its_x != x, its_y != y
    which = 2 * (its_core != core) + jnp.where(its_core == 0, off_y, off_x)
    its_lead = jnp.where(its_core == 0, z // 2, z % 2)
    pairs = [jnp.stack(group) for group in groups]
    outer_four = jnp.concatenate((pairs[0], swap(pairs[0], 1)), 0)
    outer_rest = swap(after(outer_four, pairs[1]), 2)
    inner_four = jnp.concatenate((pairs[1], swap(after(pairs[1], outer_four), 1)), 0)
    outer_other = (swap(outer_four, 0), swap(after(outer_rest, inner_four), 0))
    inner_rest = swap(inner_four, 2)
    tables = []
    for first in (True, False):
        if first:
            sent_z = 3 * its_lead
        else:
            sent_z = jnp.where(its_core == 0, 1 + its_lead, 2 - its_lead)
        slot = 2 * jnp.where(its_core == 0, off_x, off_y) + (its_z != sent_z)
        tables.append(jnp.stack((which, slot)).astype(jnp.int32))
    return tables, (outer_four, outer_rest) + outer_other, (inner_four, inner_rest)


def rearranged(stack):
    def matrix(first, count, height):
        return stack[:, first : first + count].reshape(4, height, -1)

    gap = jnp.zeros((4, 768, 64), stack.dtype)
    heads = []
    for slot in range(3):
        heads += [matrix(192 * slot, 192, 768), gap]
    small = []
    for slot in range(3):
        columns = matrix(2304 + 12 * slot, 12, 192)
        small.append(spaced(columns.reshape(768, 48)).reshape(4, 192, 256))
    rows = matrix(2340, 12, 48).transpose(0, 2, 1)
    return (
        jnp.concatenate(heads, 2),
        jnp.pad(stack[:, 576:768], ((0, 0), (0, 64), (0, 0))),
        jnp.concatenate(small, 2),
        spaced(rows.reshape(768, 48)).reshape(4, 192, 256).transpose(0, 2, 1),
        matrix(2352, 48, 192),
        matrix(2400, 48, 192),
    )


def spaced(vector):
    gap = jnp.zeros((vector.shape[0], 48), vector.dtype)
    first, second, third = vector[:, 0:16], vector[:, 16:32], vector[:, 32:48]
    return jnp.concatenate((second, gap, first, gap, gap, gap[:, :16], third, gap), 1)


def unspaced(value):
    return jnp.concatenate((value[:, 64:80], value[:, 0:16], value[:, 192:208]), 1).reshape(-1)


def shards(
    text_in,
    layout_in,
    lengths,
    text_mask,
    box_mask,
    text_cot,
    layout_cot,
    master,
    first_moment,
    second_moment,
    ema_weights,
    vectors,
    vector_first,
    vector_second,
    vector_ema,
):
    parts = lax.axis_size("tensor")
    dp_count = lax.axis_size("dp")
    tensor_index = lax.axis_index("tensor")
    dp_index = lax.axis_index("dp")
    span = master.shape[2]
    near = dp_count == 8 and parts == 4
    place = (dp_index // 2, dp_index % 2, tensor_index // 2, tensor_index % 2)
    shift = (2 * dp_index).reshape(1)
    all_parts = jnp.arange(parts, dtype=jnp.int32)
    own_parts = all_parts[::2] + place[3]
    other_parts = all_parts[::2] + 1 - place[3]
    if near:
        tables, outer, inner = gather_pieces(cast_frame(shift, master), place)
        qkv_weight, lqkv_weight, lout_weight, lup_weight, ldown_weight = unpack(tables[0], outer)
    else:
        wire = master.reshape(-1, 192).astype(jnp.bfloat16)
        stack = lax.all_gather(wire[None], ("tensor", "dp"), axis=0, tiled=True)
        stack = stack.reshape(parts, -1, UNIT)
        qkv_weight, out_weight, lqkv_weight, lout_weight, lup_weight, ldown_weight = rearranged(stack)
        up_weight, down_weight = stack[:, 768:1536], stack[:, 1536:2304]
    biases = split_vector(vectors)
    length = lax.dynamic_slice_in_dim(lengths, tensor_index, 1)

    def product(spec, left, right):
        return jnp.einsum(spec, left, right, preferred_element_type=jnp.float32)

    def over_parts(spec, left, right):
        return sum(product(spec, left[part], right[part]) for part in range(parts))

    def summed(value):
        return jnp.sum(value, 0, dtype=jnp.float32)

    gap = jnp.zeros((parts, 64), jnp.float32)
    none = jnp.zeros((parts, 256), jnp.float32)
    qkv_bias = jnp.concatenate(
        (biases[0].reshape(parts, 192), gap, none, biases[1].reshape(parts, 192), gap), 1
    )
    lqkv_bias = jnp.concatenate(
        (spaced(biases[9].reshape(parts, 48)), none, spaced(biases[10].reshape(parts, 48))), 1
    )
    text_flag = (text_mask[0] > 0)[:, None]
    box_flag = (box_mask[0] > 0)[:, None]
    text_act = jnp.where(text_flag, biases[18], text_in[0].astype(jnp.float32))
    layout_act = jnp.where(box_flag, biases[19], layout_in[0].astype(jnp.float32))
    text_low = text_act.astype(jnp.bfloat16)
    layout_low = layout_act.astype(jnp.bfloat16)
    qkv = (product("sd,tde->tse", text_low, qkv_weight) + qkv_bias[:, None]).astype(jnp.bfloat16)
    lqkv = (product("sd,tde->tse", layout_low, lqkv_weight) + lqkv_bias[:, None]).astype(
        jnp.bfloat16
    )
    context, lcontext, log_total = attend(length, qkv, lqkv)
    if near:
        inner = inner + (swap(inner[0], 0), swap(after(inner[1], context), 0))
        out_weight, up_weight, down_weight = assemble(*tables, outer, inner)
    text_attn = over_parts("sc,cd->sd", context, out_weight)
    layout_attn = over_parts("sc,cd->sd", lcontext, lout_weight)
    text_mid, text_normed_one, text_scale_one = norm_forward(
        text_attn + biases[2] + text_act, biases[3], biases[4]
    )
    layout_mid, layout_normed_one, layout_scale_one = norm_forward(
        layout_attn + biases[11] + layout_act, biases[12], biases[13]
    )
    text_mid_low = text_mid.astype(jnp.bfloat16)
    layout_mid_low = layout_mid.astype(jnp.bfloat16)
    text_rows, layout_rows = vectors[:6144].reshape(8, D), vectors[9216:10752].reshape(8, L)
    text_ahead, layout_ahead = feed_forward(
        (
            text_mid,
            text_mid_low,
            up_weight,
            biases[8].reshape(parts, 1, -1),
            down_weight,
            text_rows,
            text_cot,
        ),
        (
            layout_mid,
            layout_mid_low,
            lup_weight,
            biases[17].reshape(parts, 1, -1),
            ldown_weight,
            layout_rows,
            layout_cot,
        ),
    )
    text_hidden, text_slope, text_out, text_pre_two, text_down_in, text_sums_two = text_ahead
    layout_hidden, layout_slope, layout_out, layout_pre_two, layout_down_in, layout_sums_two = (
        layout_ahead
    )
    text_behind, layout_behind = feed_back(
        (
            text_pre_two,
            text_down_in,
            down_weight,
            text_slope,
            up_weight,
            text_normed_one,
            text_scale_one,
            text_rows,
        ),
        (
            layout_pre_two,
            layout_down_in,
            ldown_weight,
            layout_slope,
            lup_weight,
            layout_normed_one,
            layout_scale_one,
            layout_rows,
        ),
    )
    text_up_grad, text_up_sums, text_pre_one, text_attn_in, text_sums_one = text_behind
    layout_up_grad, layout_up_sums, layout_pre_one, layout_attn_in, layout_sums_one = layout_behind
    early_of = (text_mid_low, text_up_grad, text_hidden, text_down_in)
    if near:
        early_sent, rest_sent = early_grads(other_parts, *early_of)
        early_received = swap(early_sent, 0)
        early_kept, rest_kept = early_grads(own_parts, *early_of)
        text_attn_in, layout_attn_in = after((text_attn_in, layout_attn_in), early_sent, early_kept)
    else:
        early_all, rest_all = early_grads(all_parts, *early_of)
    context_grad = product("sd,tcd->tsc", text_attn_in, out_weight).astype(jnp.bfloat16)
    lcontext_grad = product("sd,tcd->tsc", layout_attn_in, lout_weight).astype(jnp.bfloat16)
    if near:
        early_sent = first_sent(early_kept, early_received, EARLY_STARTS, place)
        early_second = swap(early_sent, 1)
        context_grad = after(context_grad, early_sent)
    qkv_in, lqkv_in = attend_back(
        length, qkv, lqkv, log_total, context, lcontext, context_grad, lcontext_grad
    )
    late_of = [
        text_low,
        qkv_in,
        layout_low,
        lqkv_in,
        context,
        text_attn_in,
        lcontext,
        layout_attn_in,
        layout_mid_low,
        layout_up_grad,
        layout_hidden,
        layout_down_in,
    ]
    if near:
        early_of = (early_kept, early_received, early_second, EARLY_STARTS, place)
        early_sent = total_low(*second_part(*early_of, False))
        early_third = swap(early_sent, 2)
        late_of[1] = after(qkv_in, early_sent)
        late_sent = late_grads(other_parts, *late_of, rest_sent)
        late_received = swap(late_sent, 0)
        late_kept = late_grads(own_parts, *late_of, rest_kept)
        qkv_in, lqkv_in = after((qkv_in, lqkv_in), late_sent, late_kept, early_third)
        late_sent = first_sent(late_kept, late_received, LATE_STARTS, place)
        late_second = swap(late_sent, 1)
        early_sum = total_low(*second_part(*early_of, True), early_third)
    else:
        late_all = late_grads(all_parts, *late_of, rest_all)
    text_full = text_pre_one + over_parts("se,de->sd", qkv_in, qkv_weight)
    layout_full = layout_pre_one + over_parts("se,de->sd", lqkv_in, lqkv_weight)
    text_in_grad = jnp.where(text_flag, 0.0, text_full)
    layout_in_grad = jnp.where(box_flag, 0.0, layout_full)
    text_embed_grad = summed(jnp.where(text_flag, text_full, 0.0))
    layout_embed_grad = summed(jnp.where(box_flag, layout_full, 0.0))
    qkv_sums = jnp.sum(qkv_in, 1, dtype=jnp.float32)
    lqkv_sums = jnp.sum(lqkv_in, 1, dtype=jnp.float32)
    vector_part = jnp.concatenate(
        [
            qkv_sums[:, 0:192].reshape(-1),
            qkv_sums[:, 512:704].reshape(-1),
            text_sums_one[:3].reshape(-1),
            text_sums_two[:3].reshape(-1),
            text_up_sums.reshape(-1),
            unspaced(lqkv_sums[:, 0:256]),
            unspaced(lqkv_sums[:, 512:768]),
            layout_sums_one[:3].reshape(-1),
            layout_sums_two[:3].reshape(-1),
            layout_up_sums.reshape(-1),
            text_embed_grad,
            layout_embed_grad,
        ]
    )
    if near:
        vector_grad = vector_part
        for step in range(3):
            vector_grad = vector_grad + swap(vector_grad, step)
        late_of = (late_kept, late_received, late_second, LATE_STARTS, place)
        late_sent = total_low(*second_part(*late_of, False))
        late_third = swap(after(late_sent, vector_grad), 2)
        for step in range(3, 5):
            vector_grad = vector_grad + swap(vector_grad, step)
        late_sum = total_low(*second_part(*late_of, True), late_third)
        kept, received = line_stages(early_sum, late_sum, vector_grad, place)
        span_grad, squares = finish(shift, kept.reshape(FRAME, UNIT), received.reshape(FRAME, UNIT))
        squares = lax.all_to_all(squares, ("dp", "tensor"), 0, 0, tiled=True)
        matrix_square = jnp.sum(squares)
    else:
        flat_grad = jnp.concatenate(
            (late_all[:, :912], early_all, late_all[:, 944:]), 1
        ).reshape(parts * dp_count, -1, 192)
        span_grad = lax.psum_scatter(flat_grad, ("tensor", "dp"), scatter_dimension=0, tiled=True)
        span_grad = span_grad.astype(jnp.float32).reshape(master.shape)
        vector_grad = lax.psum(vector_part, ("dp", "tensor"))
        matrix_square = lax.psum(jnp.sum(span_grad * span_grad), ("dp", "tensor"))
    grad_norm = jnp.sqrt(matrix_square + jnp.sum(vector_grad * vector_grad))
    factor = clip_bound / jnp.maximum(grad_norm, clip_bound)
    if near:
        matrix_new = adam(
            (dp_index * span).reshape(1),
            factor.reshape(1),
            master,
            span_grad,
            first_moment,
            second_moment,
            ema_weights,
        )
        matrix_new = tuple(matrix_new)
    else:
        rates = lax.dynamic_slice_in_dim(rate_table(parts), dp_index * span, span)
        matrix_new = adam_update(
            master,
            span_grad,
            first_moment,
            second_moment,
            ema_weights,
            rates.reshape(master.shape),
            factor,
        )
    vector_new = adam_update(
        vectors, vector_grad, vector_first, vector_second, vector_ema, vector_rate, factor
    )
    return (
        (
            text_out,
            layout_out,
            text_in_grad[None],
            layout_in_grad[None],
            grad_norm,
        )
        + matrix_new
        + vector_new
    )


def solution(mesh):
    in_specs = (
        P(("dp", "tensor"), None, None),
        P(("dp", "tensor"), None, None),
        P("dp"),
        P(("dp", "tensor"), None),
        P(("dp", "tensor"), None),
        P(("dp", "tensor"), None, None),
        P(("dp", "tensor"), None, None),
        P("tensor", "dp", None),
        P("tensor", "dp", None),
        P("tensor", "dp", None),
        P("tensor", "dp", None),
        P(),
        P(),
        P(),
        P(),
    )
    out_specs = (
        P(("dp", "tensor"), None, None),
        P(("dp", "tensor"), None, None),
        P(("dp", "tensor"), None, None),
        P(("dp", "tensor"), None, None),
        P(),
        P("tensor", "dp", None),
        P("tensor", "dp", None),
        P("tensor", "dp", None),
        P("tensor", "dp", None),
        P("tensor", "dp", None),
        P(),
        P(),
        P(),
        P(),
        P(),
    )
    return jax.shard_map(shards, mesh=mesh, in_specs=in_specs, out_specs=out_specs, check_vma=False)
```

```python
from functools import partial
import math

import jax
import jax.numpy as jnp
from jax import lax
from jax.experimental import pallas as pl
from jax.experimental.pallas import tpu as pltpu
from jax.sharding import PartitionSpec as P

D = 768
HT = 64
FF = 3072
L = 192
HL = 16
LF = 768
STEP = 5


norm_eps = 1e-05
clip_bound = 1.0
first_decay = 0.5
second_decay = 0.6
adam_floor = 1e-08
weight_decay = 0.01
vector_rate = 0.5
average_keep = 0.5
masked_score = -1e30


def piece_table(parts):
    text_spread = 1.0 / math.sqrt(D)
    layout_spread = 1.0 / math.sqrt(L)
    return [
        (D, D // parts, text_spread),
        (D, D // parts, text_spread),
        (D, D // parts, text_spread),
        (D // parts, D, 8.0 * text_spread),
        (D, FF // parts, text_spread),
        (FF // parts, D, 1.0 / math.sqrt(FF)),
        (L, L // parts, layout_spread),
        (L, L // parts, layout_spread),
        (L, L // parts, layout_spread),
        (L // parts, L, 8.0 * layout_spread),
        (L, LF // parts, layout_spread),
        (LF // parts, L, 1.0 / math.sqrt(LF)),
    ]


def rate_table(parts):
    return jnp.concatenate(
        [
            jnp.full((height * width,), spread, jnp.float32)
            for height, width, spread in piece_table(parts)
        ]
    )


def split_vector(flat):
    pieces = []
    start = 0
    for width in [D] * 8 + [FF] + [L] * 8 + [LF] + [D, L]:
        pieces.append(flat[start : start + width])
        start = start + width
    return pieces


def project(acts, weight):
    return jnp.einsum("psd,de->pse", acts, weight, preferred_element_type=jnp.float32)


def project_back(incoming, weight):
    return jnp.einsum("pse,de->psd", incoming, weight, preferred_element_type=jnp.float32)


def weight_grad(acts, incoming):
    return jnp.einsum("psd,pse->de", acts, incoming, preferred_element_type=jnp.float32)


def norm_forward(value, gain, shift):
    mean = jnp.mean(value, -1, keepdims=True)
    centred = value - mean
    scale = lax.rsqrt(jnp.mean(centred * centred, -1, keepdims=True) + norm_eps)
    normed = centred * scale
    return (normed * gain + shift, normed, scale)


def norm_backward(incoming, normed, scale, gain):
    scaled = incoming * gain
    result = scale * (
        scaled
        - jnp.mean(scaled, -1, keepdims=True)
        - normed * jnp.mean(scaled * normed, -1, keepdims=True)
    )
    return (result, jnp.sum(incoming * normed, (0, 1)), jnp.sum(incoming, (0, 1)))


def gelu_back(value, incoming):
    unused, pull = jax.vjp(partial(jax.nn.gelu, approximate=False), value)
    return pull(incoming)[0]


def adam_update(weight, gradient, first, second, average, rate, factor):
    clipped = gradient * factor
    new_first = first_decay * first + (1.0 - first_decay) * clipped
    new_second = second_decay * second + (1.0 - second_decay) * clipped * clipped
    first_hat = new_first / (1.0 - first_decay**STEP)
    second_hat = new_second / (1.0 - second_decay**STEP)
    updated = weight - rate * (
        first_hat / (jnp.sqrt(second_hat) + adam_floor) + weight_decay * weight
    )
    return (
        updated,
        new_first,
        new_second,
        updated.astype(jnp.bfloat16),
        average_keep * average + (1.0 - average_keep) * updated,
    )


NT = (((1,), (1,)), ((), ()))
NN = (((1,), (0,)), ((), ()))
TN = (((0,), (0,)), ((), ()))


def dot(left, right, dims):
    return lax.dot_general(left, right, dims, preferred_element_type=jnp.float32)


def kept_out(*values):
    return [pltpu.with_memory_space_constraint(value, pltpu.HBM) for value in values]


def outside(shape, dtype):
    return pltpu.HBM(shape, dtype)


def lane_of(shape):
    return lax.broadcasted_iota(jnp.int32, shape, len(shape) - 1)


def head_tiles(text_ref, layout_ref, slot, tile, high):
    first = slot * 256 + tile * 128
    text = text_ref[0, :, first : first + 128]
    layout = layout_ref[0, :, first : first + 128]
    low = lane_of(text.shape) < 64
    if high:
        return jnp.where(low, layout, text)
    return jnp.where(low, text, layout)


def own_lanes(shape, high):
    low = lane_of(shape) < 64
    return ~low if high else low


def scaled_query(query, high):
    own = own_lanes(query.shape, high)
    marker = 16 if high else 80
    scale = jnp.where(own, 0.125, 0.25)
    scaled = (query.astype(jnp.float32) * scale).astype(jnp.bfloat16)
    return jnp.where(lane_of(query.shape) == marker, jnp.bfloat16(1.0), scaled)


def masked_key(key, high, length):
    marker = 16 if high else 80
    beyond = lax.broadcasted_iota(jnp.int32, key.shape, 0) >= length
    column = jnp.where(beyond, jnp.float32(-1e30), jnp.float32(0.0)).astype(jnp.bfloat16)
    return jnp.where(lane_of(key.shape) == marker, column, key)


def attend_kernel(length_ref, text_ref, layout_ref, context_ref, layout_context_ref, total_ref):
    length = length_ref[0]
    found = []
    for head in range(3):
        tile, high = head // 2, head % 2 == 1
        query = scaled_query(head_tiles(text_ref, layout_ref, 0, tile, high), high)
        key = masked_key(head_tiles(text_ref, layout_ref, 1, tile, high), high, length)
        value = head_tiles(text_ref, layout_ref, 2, tile, high)
        scores = dot(key, query, NT)
        top = jnp.max(scores, 0, keepdims=True)
        raised = jnp.exp(scores - top)
        total = jnp.sum(raised, 0, keepdims=True)
        probs = (raised * (1.0 / total)).astype(jnp.bfloat16)
        total_ref[0, head : head + 1, :] = top + jnp.log(total)
        context = dot(value, probs, TN)
        found.append(context.T)
    low = lane_of(found[0].shape) < 64
    zero = jnp.zeros_like(found[0])
    context_ref[0, :, 0:128] = jnp.where(low, found[0], found[1]).astype(jnp.bfloat16)
    context_ref[0, :, 128:256] = jnp.where(low, found[2], zero).astype(jnp.bfloat16)
    layout_context_ref[0, :, 0:128] = jnp.where(low, found[1], found[0]).astype(jnp.bfloat16)
    layout_context_ref[0, :, 128:256] = jnp.where(low, zero, found[2]).astype(jnp.bfloat16)


def block(rows, width):
    return pl.BlockSpec((1, rows, width), lambda t: (t, 0, 0))


def attend(length, text, layout):
    parts, positions, _ = text.shape
    return pl.pallas_call(
        attend_kernel,
        grid=(parts,),
        in_specs=[
            pl.BlockSpec(memory_space=pltpu.SMEM),
            block(positions, 768),
            block(positions, 768),
        ],
        out_specs=[block(positions, 256), block(positions, 256), block(8, positions)],
        out_shape=[
            outside((parts, positions, 256), jnp.bfloat16),
            outside((parts, positions, 256), jnp.bfloat16),
            outside((parts, 8, positions), jnp.float32),
        ],
        compiler_params=pltpu.CompilerParams(vmem_limit_bytes=24 << 20),
        cost_estimate=pl.CostEstimate(flops=3 << 30, transcendentals=3 << 20, bytes_accessed=10 << 20),
        name="attend",
    )(length, *kept_out(text, layout))


def attend_back_kernel(
    length_ref,
    text_ref,
    layout_ref,
    total_ref,
    context_ref,
    layout_context_ref,
    context_grad_ref,
    layout_context_grad_ref,
    text_grad_ref,
    layout_grad_ref,
):
    length = length_ref[0]
    grads = ([], [], [])
    for head in range(3):
        tile, high = head // 2, head % 2 == 1
        raw_query = head_tiles(text_ref, layout_ref, 0, tile, high)
        raw_key = head_tiles(text_ref, layout_ref, 1, tile, high)
        value = head_tiles(text_ref, layout_ref, 2, tile, high)
        incoming = head_tiles(context_grad_ref, layout_context_grad_ref, 0, tile, high)
        context = head_tiles(context_ref, layout_context_ref, 0, tile, high)
        own = own_lanes(value.shape, high)
        query = scaled_query(raw_query, high)
        key = masked_key(raw_key, high, length)
        product = (incoming.astype(jnp.float32) * context.astype(jnp.float32)).T
        start = 0 if high else 64
        layout_mean = jnp.sum(product[start : start + 16], 0, keepdims=True)
        joint_mean = jnp.sum(product, 0, keepdims=True)
        zero = jnp.zeros_like(value)
        probs = jnp.exp(dot(key, query, NT) - total_ref[0, head : head + 1, :])
        value_grad = dot(probs.astype(jnp.bfloat16), incoming, NN)
        joint = (probs * (dot(value, incoming, NT) - joint_mean)).astype(jnp.bfloat16)
        alone = (
            probs * (dot(jnp.where(own, zero, value), incoming, NT) - layout_mean)
        ).astype(jnp.bfloat16)
        key_grad = jnp.where(own, dot(joint, raw_query, NN) * 0.125, dot(alone, raw_query, NN) * 0.25)
        rows = lax.broadcasted_iota(jnp.int32, (128, value.shape[0]), 0) < 64
        if high:
            rows = ~rows
        query_grad = jnp.where(
            rows, dot(raw_key, joint, TN) * 0.125, dot(raw_key, alone, TN) * 0.25
        )
        grads[0].append(query_grad.T)
        grads[1].append(key_grad)
        grads[2].append(value_grad)
    low = lane_of(grads[0][0].shape) < 64
    zero = jnp.zeros_like(grads[0][0])
    for slot in range(3):
        first, second, third = grads[slot]
        at = slot * 256
        text_grad_ref[0, :, at : at + 128] = jnp.where(low, first, second).astype(jnp.bfloat16)
        text_grad_ref[0, :, at + 128 : at + 256] = jnp.where(low, third, zero).astype(jnp.bfloat16)
        layout_grad_ref[0, :, at : at + 128] = jnp.where(low, second, first).astype(jnp.bfloat16)
        layout_grad_ref[0, :, at + 128 : at + 256] = jnp.where(low, zero, third).astype(
            jnp.bfloat16
        )


def attend_back(length, text, layout, total, context, layout_context, grad, layout_grad):
    parts, positions, _ = text.shape
    return pl.pallas_call(
        attend_back_kernel,
        grid=(parts,),
        in_specs=[
            pl.BlockSpec(memory_space=pltpu.SMEM),
            block(positions, 768),
            block(positions, 768),
            block(8, positions),
            block(positions, 256),
            block(positions, 256),
            block(positions, 256),
            block(positions, 256),
        ],
        out_specs=[block(positions, 768), block(positions, 768)],
        out_shape=[
            outside((parts, positions, 768), jnp.bfloat16),
            outside((parts, positions, 768), jnp.bfloat16),
        ],
        compiler_params=pltpu.CompilerParams(vmem_limit_bytes=30 << 20),
        cost_estimate=pl.CostEstimate(flops=12 << 30, transcendentals=3 << 20, bytes_accessed=20 << 20),
        name="attend_back",
    )(length, *kept_out(text, layout, total, context, layout_context, grad, layout_grad))


SPAN = 235008
FRAME = 320
UNIT = 768


def cast_kernel(shift_ref, master_ref, frame_ref, flat_ref):
    whole = SPAN // 1024
    for step in range(whole):
        flat_ref[pl.ds(8 * step, 8), :] = master_ref[0, 0, pl.ds(1024 * step, 1024)].reshape(8, 128)
    flat_ref[pl.ds(8 * whole, 4), :] = master_ref[0, 0, pl.ds(1024 * whole, 512)].reshape(4, 128)
    for column in range(6):
        rows = flat_ref[pl.ds(column, 306, stride=6), :]
        rows = jnp.concatenate((rows, jnp.zeros((14, 128), jnp.float32)), 0)
        rows = pltpu.roll(rows, shift_ref[0], 0)
        frame_ref[0, :, column * 128 : column * 128 + 128] = rows.astype(jnp.bfloat16)


def cast_frame(shift, master):
    return pl.pallas_call(
        cast_kernel,
        in_specs=[pl.BlockSpec(memory_space=pltpu.SMEM), pl.BlockSpec(memory_space=pltpu.VMEM)],
        out_specs=pl.BlockSpec(memory_space=pltpu.VMEM),
        out_shape=jax.ShapeDtypeStruct((1, FRAME, UNIT), jnp.bfloat16),
        scratch_shapes=[pltpu.VMEM((1840, 128), jnp.float32)],
        name="cast_frame",
    )(shift, master)


def finish_kernel(
    place_ref, early_ref, early_last_ref, late_ref, late_last_ref, flat_out_ref, square_ref, flat_ref
):
    shift, window = place_ref[0], place_ref[1]
    row = lax.broadcasted_iota(jnp.int32, (FRAME, 128), 0)
    first = jnp.where(window == 7, 176, 0)
    last = jnp.where(window == 0, 320, jnp.where(window == 1, 272, jnp.where(window == 7, 320, 0)))
    late = (row >= first) & (row < last)
    squares = jnp.zeros((8, 128), jnp.float32)
    for column in range(6):
        at = slice(column * 128, column * 128 + 128)
        rows = jnp.where(
            late,
            late_ref[:, at].astype(jnp.float32) + late_last_ref[:, at].astype(jnp.float32),
            early_ref[:, at].astype(jnp.float32) + early_last_ref[:, at].astype(jnp.float32),
        )
        rows = pltpu.roll(rows, FRAME - shift, 0)
        flat_ref[pl.ds(column, 306, stride=6), :] = rows[:306]
        masked = jnp.where(row < 306, rows, 0.0)
        squares = squares + jnp.sum((masked * masked).reshape(40, 8, 128), 0)
    square_ref[...] = jnp.broadcast_to(jnp.sum(squares, 0, keepdims=True), square_ref.shape)
    whole = SPAN // 1024
    for step in range(whole):
        flat_out_ref[0, 0, pl.ds(1024 * step, 1024)] = flat_ref[pl.ds(8 * step, 8), :].reshape(1024)
    flat_out_ref[0, 0, pl.ds(1024 * whole, 512)] = flat_ref[pl.ds(8 * whole, 4), :].reshape(512)


def finish(place, *sums):
    return pl.pallas_call(
        finish_kernel,
        in_specs=[pl.BlockSpec(memory_space=pltpu.SMEM)]
        + [pl.BlockSpec(memory_space=pltpu.VMEM)] * 4,
        out_specs=[pl.BlockSpec(memory_space=pltpu.VMEM)] * 2,
        out_shape=[
            jax.ShapeDtypeStruct((1, 1, SPAN), jnp.float32),
            jax.ShapeDtypeStruct((32, 128), jnp.float32),
        ],
        scratch_shapes=[pltpu.VMEM((1840, 128), jnp.float32)],
        name="finish",
    )(place, *sums)


RATE_STEPS = (
    (0, 768.0**-0.5),
    (576, 8.0 * 768.0**-0.5),
    (768, 768.0**-0.5),
    (1536, 3072.0**-0.5),
    (2304, 192.0**-0.5),
    (2340, 8.0 * 192.0**-0.5),
    (2352, 192.0**-0.5),
    (2400, 768.0**-0.5),
)


def adam_kernel(
    first_index_ref,
    factor_ref,
    weight_ref,
    gradient_ref,
    first_ref,
    second_ref,
    average_ref,
    new_weight_ref,
    new_first_ref,
    new_second_ref,
    low_ref,
    new_average_ref,
):
    width = weight_ref.shape[2]
    start = first_index_ref[0] + pl.program_id(0) * width
    factor = factor_ref[0]
    for at in range(0, width, CHUNK):
        count = min(CHUNK, width - at)
        place = pl.ds(at, count)

        def load(ref):
            return ref[0, 0, place].reshape(count // 128, 128)

        def store(ref, value):
            ref[0, 0, place] = value.reshape(count)

        shape = (count // 128, 128)
        index = lax.broadcasted_iota(jnp.int32, shape, 0) * 128 + start + at
        rate = jnp.full(shape, RATE_STEPS[0][1], jnp.float32)
        for row, value in RATE_STEPS[1:]:
            rate = jnp.where(index >= row * UNIT, jnp.float32(value), rate)
        weight = load(weight_ref)
        clipped = load(gradient_ref) * factor
        new_first = 0.5 * load(first_ref) + 0.5 * clipped
        new_second = 0.6 * load(second_ref) + 0.4 * clipped * clipped
        first_hat = new_first * (1.0 / (1.0 - 0.5**5))
        second_hat = new_second * (1.0 / (1.0 - 0.6**5))
        updated = weight - rate * (first_hat / (jnp.sqrt(second_hat) + 1e-8) + 0.01 * weight)
        store(new_weight_ref, updated)
        store(new_first_ref, new_first)
        store(new_second_ref, new_second)
        low_ref[0, 0, place] = updated.reshape(count).astype(jnp.bfloat16)
        store(new_average_ref, 0.5 * load(average_ref) + 0.5 * updated)


CHUNK = 1024


def adam(first_index, factor, weight, gradient, first, second, average, steps=3):
    span = weight.shape[2]
    spec = pl.BlockSpec((1, 1, span // steps), lambda i: (0, 0, i))
    full = jax.ShapeDtypeStruct(weight.shape, jnp.float32)
    return pl.pallas_call(
        adam_kernel,
        grid=(steps,),
        in_specs=[pl.BlockSpec(memory_space=pltpu.SMEM)] * 2 + [spec] * 5,
        out_specs=[spec] * 5,
        out_shape=[full, full, full, jax.ShapeDtypeStruct(weight.shape, jnp.bfloat16), full],
        name="adam",
    )(first_index, factor, weight, gradient, first, second, average)


def placing(rows, columns, row_axis):
    narrow = lax.broadcasted_iota(jnp.int32, (rows, columns), row_axis)
    wide = lax.broadcasted_iota(jnp.int32, (rows, columns), 1 - row_axis)
    place = jnp.where(narrow < 16, narrow + 64, jnp.where(narrow < 32, narrow - 16, narrow + 160))
    return jnp.where(place == wide, 1.0, 0.0).astype(jnp.bfloat16)


def wide_rows(value):
    return jnp.concatenate((value, jnp.zeros((value.shape[0], 64), value.dtype)), 1)


def early_kernel(
    parts_ref, mid_ref, up_in_ref, hidden_ref, down_in_ref, context_ref, attn_in_ref, early_ref
):
    early_ref[0, 0:192] = dot(context_ref[0], attn_in_ref[...], TN)[:192].astype(jnp.bfloat16)
    early_ref[0, 192:960] = dot(mid_ref[...], up_in_ref[0], TN).astype(jnp.bfloat16)
    early_ref[0, 960:1728] = dot(hidden_ref[0], down_in_ref[...], TN).astype(jnp.bfloat16)
    early_ref[0, 1728:] = jnp.zeros((96, 768), jnp.bfloat16)


def early_grads(parts, mid, up_in, hidden, down_in, context, attn_in):
    positions = mid.shape[0]
    count = parts.shape[0]
    fixed = pl.BlockSpec((positions, 768), lambda i, p: (0, 0))
    chosen = pl.BlockSpec((1, positions, 768), lambda i, p: (p[i], 0, 0))
    return pl.pallas_call(
        early_kernel,
        grid_spec=pltpu.PrefetchScalarGridSpec(
            num_scalar_prefetch=1,
            grid=(count,),
            in_specs=[
                fixed,
                chosen,
                chosen,
                fixed,
                pl.BlockSpec((1, positions, 256), lambda i, p: (p[i], 0, 0)),
                fixed,
            ],
            out_specs=pl.BlockSpec((1, 1824, 768), lambda i, p: (i, 0, 0)),
        ),
        out_shape=outside((count, 1824, 768), jnp.bfloat16),
        compiler_params=pltpu.CompilerParams(vmem_limit_bytes=24 << 20),
        cost_estimate=pl.CostEstimate(flops=count * 1408 << 20, transcendentals=0, bytes_accessed=count * 6 << 20),
        name="early_grads",
    )(parts, *kept_out(mid, up_in, hidden, down_in, context, attn_in))


def late_kernel(
    parts_ref,
    text_ref,
    qkv_in_ref,
    layout_ref,
    lqkv_in_ref,
    lcontext_ref,
    lattn_in_ref,
    lmid_ref,
    lup_in_ref,
    lhidden_ref,
    ldown_in_ref,
    late_ref,
    heads_ref,
    rows_ref,
    slots_ref,
    small_ref,
):
    heads_grad = dot(text_ref[...], qkv_in_ref[0], TN)
    for tile in range(6):
        heads_ref[tile] = heads_grad[:, 128 * tile : 128 * tile + 128]
    for slot in range(3):
        for step in range(4):
            piece = jnp.concatenate(
                [heads_ref[2 * slot + half, pl.ds(step, 192, stride=4), :] for half in range(2)], 1
            )
            late_ref[0, 192 * slot : 192 * slot + 192, 192 * step : 192 * step + 192] = piece[
                :, :192
            ].astype(jnp.bfloat16)

    slots_ref[...] = jnp.zeros_like(slots_ref)
    lqkv_grad = dot(layout_ref[...], lqkv_in_ref[0], TN)
    for slot in range(3):
        for half in range(2):
            at = 256 * slot + 128 * half
            rows_ref[half, 0:192] = lqkv_grad[:, at : at + 128]
            for step in range(16):
                row = 16 * (3 * step + slot)
                slots_ref[row : row + 12, 128 * half : 128 * half + 128] = rows_ref[
                    half, pl.ds(step, 12, stride=16), :
                ]
    placed = dot(slots_ref[...].astype(jnp.bfloat16), placing(256, 48, 1), NN)
    for slot in range(3):
        for step in range(16):
            at = 16 * (3 * step + slot)
            small_ref[12 * slot : 12 * slot + 12, 48 * step : 48 * step + 48] = placed[at : at + 12]

    def gather(first, count):
        for step in range(4):
            piece = jnp.concatenate(
                [rows_ref[half, pl.ds(step, count, stride=4), :] for half in range(2)], 1
            )
            small_ref[first : first + count, 192 * step : 192 * step + 192] = piece[:, :192]

    lout_grad = dot(lcontext_ref[0], lattn_in_ref[...], TN)
    for head, at in enumerate((64, 0, 192)):
        rows_ref[0, 16 * head : 16 * head + 16, :] = lout_grad[at : at + 16, 0:128]
        rows_ref[1, 16 * head : 16 * head + 16, 0:64] = lout_grad[at : at + 16, 128:192]
    gather(36, 12)
    for first, left, right in (
        (48, lmid_ref[...], lup_in_ref[0]),
        (96, lhidden_ref[0], ldown_in_ref[...]),
    ):
        grad = dot(left, right, TN)
        rows_ref[0, 0:192, :] = grad[:, 0:128]
        rows_ref[1, 0:192, 0:64] = grad[:, 128:192]
        gather(first, 48)
    late_ref[0, 576:720] = small_ref[...].astype(jnp.bfloat16)


def late_grads(parts, text, qkv_in, layout, lqkv_in, lcontext, lattn_in, lmid, lup_in, lhidden, ldown_in):
    positions = text.shape[0]
    count = parts.shape[0]

    def fixed(width):
        return pl.BlockSpec((positions, width), lambda i, p: (0, 0))

    def chosen(width):
        return pl.BlockSpec((1, positions, width), lambda i, p: (p[i], 0, 0))

    return pl.pallas_call(
        late_kernel,
        grid_spec=pltpu.PrefetchScalarGridSpec(
            num_scalar_prefetch=1,
            grid=(count,),
            in_specs=[
                fixed(768),
                chosen(768),
                fixed(192),
                chosen(768),
                chosen(256),
                fixed(192),
                fixed(192),
                chosen(192),
                chosen(192),
                fixed(192),
            ],
            out_specs=pl.BlockSpec((1, 720, 768), lambda i, p: (i, 0, 0)),
            scratch_shapes=[
                pltpu.VMEM((6, 768, 128), jnp.float32),
                pltpu.VMEM((2, 192, 128), jnp.float32),
                pltpu.VMEM((768, 256), jnp.float32),
                pltpu.VMEM((144, 768), jnp.float32),
            ],
        ),
        out_shape=outside((count, 720, 768), jnp.bfloat16),
        compiler_params=pltpu.CompilerParams(vmem_limit_bytes=26 << 20),
        cost_estimate=pl.CostEstimate(flops=count * 1208 << 20, transcendentals=0, bytes_accessed=count * 6 << 20),
        name="late_grads",
    )(parts, *kept_out(text, qkv_in, layout, lqkv_in, lcontext, lattn_in, lmid, lup_in, lhidden, ldown_in))


TILES = 20
HEAD_PIECES = ((0, 0, 20, 0), (1, 1, 16, 20), (1, 0, 1, 36), (7, 11, 9, 37))
OUT_PIECES = ((1, 17, 3, 0), (2, 1, 9, 3))
UP_PIECES = ((2, 10, 10, 0), (3, 1, 19, 10), (4, 1, 19, 29))
DOWN_PIECES = ((5, 1, 19, 0), (6, 1, 19, 19), (7, 1, 10, 38))
OUT_SEAMS = ((2, 2),)
UP_SEAMS = ((3, 9), (4, 28), (5, 47))
DOWN_SEAMS = ((6, 18), (7, 37))


def start_piece(table_ref, sources, part, window, first, count, target, semaphore):
    row = part * 8 + window
    for index, source in enumerate(sources):

        @pl.when(table_ref[0, row] == index)
        def start():
            place = source.at[table_ref[1, row], pl.ds(first, count)]
            pltpu.make_async_copy(place, target, semaphore).start()


def wait_piece(table_ref, sources, part, window, first, count, target, semaphore):
    pltpu.make_async_copy(sources[0].at[0, pl.ds(first, count)], target, semaphore).wait()


def unpack_kernel(
    table_ref, *refs
):
    sources = refs[:4]
    qkv_ref, lqkv_ref, lwo_ref, lw1_ref, lw2_ref, frames_ref, rows_ref, small_ref, semaphores = refs[4:]
    part = pl.program_id(0)

    def each(act, number):
        for index, (window, first, count, at) in enumerate(HEAD_PIECES):
            target = frames_ref.at[number, pl.ds(at, count)]
            act(table_ref, sources, number, window, first, count, target, semaphores.at[number, index])

    @pl.when(part == 0)
    def begin():
        for number in range(4):
            each(start_piece, number)

    each(wait_piece, part)
    frames_ref[part, 19] = frames_ref[part, 19] + frames_ref[part, 36]

    def spread(source_ref, first, count, stride, target_ref):
        for step in range(4):
            piece = wide_rows(source_ref[first : first + count, 192 * step : 192 * step + 192])
            target_ref[0, pl.ds(step, count, stride=stride), :] = piece[:, :128]
            target_ref[1, pl.ds(step, count, stride=stride), :] = piece[:, 128:]

    small_ref[...] = frames_ref[part, 37:46].reshape(144, 768).astype(jnp.float32)
    for slot in range(3):
        for step in range(4):
            piece = frames_ref[part, 12 * slot : 12 * slot + 12, :, 192 * step : 192 * step + 192]
            piece = wide_rows(piece.reshape(192, 192).astype(jnp.float32))
            rows_ref[0, pl.ds(step, 192, stride=4), :] = piece[:, :128]
            rows_ref[1, pl.ds(step, 192, stride=4), :] = piece[:, 128:]
        qkv_ref[0, :, 256 * slot : 256 * slot + 128] = rows_ref[0].astype(jnp.bfloat16)
        qkv_ref[0, :, 256 * slot + 128 : 256 * slot + 256] = rows_ref[1].astype(jnp.bfloat16)
    place = placing(48, 256, 0)
    narrow = jnp.concatenate(
        [small_ref[0:48, 48 * step : 48 * step + 48] for step in range(16)], 0
    )
    placed = dot(narrow.astype(jnp.bfloat16), place, NN)
    for slot in range(3):
        for step in range(16):
            piece = placed[48 * step + 12 * slot : 48 * step + 12 * slot + 12]
            rows_ref[0, pl.ds(step, 12, stride=16), :] = piece[:, :128]
            rows_ref[1, pl.ds(step, 12, stride=16), :] = piece[:, 128:]
        lqkv_ref[0, :, 256 * slot : 256 * slot + 128] = rows_ref[0, 0:192].astype(jnp.bfloat16)
        lqkv_ref[0, :, 256 * slot + 128 : 256 * slot + 256] = rows_ref[1, 0:192].astype(jnp.bfloat16)
    spread(small_ref, 36, 12, 4, rows_ref)
    lwo_ref[...] = jnp.zeros_like(lwo_ref)
    for head, at in enumerate((64, 0, 192)):
        for half, width in ((0, 128), (1, 64)):
            lwo_ref[0, at : at + 16, 128 * half : 128 * half + width] = rows_ref[
                half, 16 * head : 16 * head + 16, :width
            ].astype(jnp.bfloat16)
    for first, target_ref in ((48, lw1_ref), (96, lw2_ref)):
        spread(small_ref, first, 48, 4, rows_ref)
        target_ref[0, :, 0:128] = rows_ref[0, 0:192].astype(jnp.bfloat16)
        target_ref[0, :, 128:192] = rows_ref[1, 0:192, :64].astype(jnp.bfloat16)


def unpack(table, sources):
    shapes = ((768, 768), (192, 768), (256, 192), (192, 192), (192, 192))
    return pl.pallas_call(
        unpack_kernel,
        grid=(4,),
        in_specs=[pl.BlockSpec(memory_space=pltpu.SMEM)] + [pl.BlockSpec(memory_space=pl.ANY)] * 4,
        out_specs=[pl.BlockSpec((1,) + shape, lambda t: (t, 0, 0)) for shape in shapes],
        out_shape=[outside((4,) + shape, jnp.bfloat16) for shape in shapes],
        scratch_shapes=[
            pltpu.VMEM((4, 46, 16, 768), jnp.bfloat16),
            pltpu.VMEM((2, 768, 128), jnp.float32),
            pltpu.VMEM((144, 768), jnp.float32),
            pltpu.SemaphoreType.DMA((4, 4)),
        ],
        compiler_params=pltpu.CompilerParams(vmem_limit_bytes=20 << 20),
        cost_estimate=pl.CostEstimate(flops=1 << 30, transcendentals=0, bytes_accessed=14 << 20),
        name="unpack",
    )(table, *kept_out(*sources))


def gelu_parts(value):
    below = 0.5 + 0.5 * lax.erf(value * 0.5**0.5)
    decay = jnp.exp(value * value * -0.5)
    return value * below, below + value * decay * 0.3989422804014327


def normed_rows(value):
    mean = jnp.mean(value, -1, keepdims=True)
    centred = value - mean
    scale = lax.rsqrt(jnp.mean(centred * centred, -1, keepdims=True) + 1e-5)
    return centred * scale, scale


def norm_pull(incoming, normed, scale, gain):
    scaled = incoming * gain
    return scale * (
        scaled
        - jnp.mean(scaled, -1, keepdims=True)
        - normed * jnp.mean(scaled * normed, -1, keepdims=True)
    )


def column_sums(target_ref, *values):
    for row, value in enumerate(values):
        target_ref[row : row + 1] = jnp.sum(value, 0, keepdims=True)


def each_piece(act, tables, pieces_refs, matrix, part, target_ref, seams_ref, semaphores):
    index = matrix[2]
    for window, first, count, at in matrix[0]:
        group = 0 if window // 2 in (0, 3) else 1
        target = target_ref.at[part, pl.ds(at, count)]
        sources = pieces_refs[4 * group : 4 * group + 4]
        act(tables[group], sources, part, window, first, count, target, semaphores.at[part, index])
        index += 1
    for number, (window, _) in enumerate(matrix[1]):
        group = 0 if window // 2 in (0, 3) else 1
        target = seams_ref.at[part, pl.ds(matrix[3] + number, 1)]
        sources = pieces_refs[4 * group : 4 * group + 4]
        act(tables[group], sources, part, window, 0, 1, target, semaphores.at[part, index])
        index += 1


OUT_MATRIX = (OUT_PIECES, OUT_SEAMS, 0, 0)
UP_MATRIX = (UP_PIECES, UP_SEAMS, 3, 1)
DOWN_MATRIX = (DOWN_PIECES, DOWN_SEAMS, 9, 4)


def started(*args):
    def begin(part, carry):
        each_piece(start_piece, *args[:3], part, *args[3:])
        return carry

    lax.fori_loop(0, 4, begin, 0)


def awaited(tables, pieces_refs, matrix, part, target_ref, seams_ref, semaphores):
    each_piece(wait_piece, tables, pieces_refs, matrix, part, target_ref, seams_ref, semaphores)
    for number, (_, at) in enumerate(matrix[1]):
        target_ref[part, at] = target_ref[part, at] + seams_ref[part, matrix[3] + number]


def forward_kernel(*refs):
    tables, pieces_refs, refs = refs[0:2], refs[2:10], refs[10:]
    inputs, outputs, scratch = refs[:18], refs[18:37], refs[37:]
    out_ref = outputs[18]
    out_scratch, up_scratch, down_scratch, seams_ref, semaphores = scratch[6:]
    part = pl.program_id(0)

    @pl.when(part == 0)
    def begin():
        for matrix, target_ref in (
            (OUT_MATRIX, out_scratch),
            (UP_MATRIX, up_scratch),
            (DOWN_MATRIX, down_scratch),
        ):
            started(tables, pieces_refs, matrix, target_ref, seams_ref, semaphores)
        out_scratch[:, 12:16] = jnp.zeros((4, 4, 16, 768), jnp.bfloat16)
        for number in range(4):
            awaited(tables, pieces_refs, OUT_MATRIX, number, out_scratch, seams_ref, semaphores)
        out_ref[...] = out_scratch[...].reshape(4, 256, 768)

    awaited(tables, pieces_refs, UP_MATRIX, part, up_scratch, seams_ref, semaphores)
    awaited(tables, pieces_refs, DOWN_MATRIX, part, down_scratch, seams_ref, semaphores)
    for stream in range(2):
        act_ref, context_ref, own_out_ref, own_up_ref, up_bias_ref, own_down_ref, rows_ref, cotangent_ref, _ = inputs[
            9 * stream : 9 * stream + 9
        ]
        (
            mid_low_ref,
            normed_ref,
            scale_ref,
            hidden_ref,
            slope_ref,
            final_ref,
            pre_ref,
            pre_low_ref,
            sums_ref,
        ) = outputs[9 * stream : 9 * stream + 9]
        mid_ref, total_ref, low_ref = scratch[3 * stream : 3 * stream + 3]

        @pl.when(part == 0)
        def attention_out():
            weights = out_ref if stream == 0 else own_out_ref
            attn = sum(dot(context_ref[number], weights[number], NN) for number in range(4))
            normed, scale = normed_rows(attn + rows_ref[2:3] + act_ref[...])
            mid = normed * rows_ref[3:4] + rows_ref[4:5]
            normed_ref[...] = normed
            scale_ref[...] = scale
            mid_ref[...] = mid
            low_ref[...] = mid.astype(jnp.bfloat16)
            mid_low_ref[...] = low_ref[...]

        if stream == 0:
            up, down = up_scratch[part].reshape(768, 768), down_scratch[part].reshape(768, 768)
        else:
            up, down = own_up_ref[0], own_down_ref[0]
        hidden, slope = gelu_parts(dot(low_ref[...], up, NN) + up_bias_ref[0])
        hidden = hidden.astype(jnp.bfloat16)
        hidden_ref[0] = hidden
        slope_ref[0] = slope.astype(jnp.bfloat16)
        product = dot(hidden, down, NN)

        @pl.when(part == 0)
        def first():
            total_ref[...] = product

        @pl.when(part > 0)
        def later():
            total_ref[...] = total_ref[...] + product

        @pl.when(part == 3)
        def last():
            gain = rows_ref[6:7]
            normed, scale = normed_rows(total_ref[...] + rows_ref[5:6] + mid_ref[...])
            final_ref[0] = (normed * gain + rows_ref[7:8]).astype(jnp.bfloat16)
            incoming = cotangent_ref[0].astype(jnp.float32)
            pre = norm_pull(incoming, normed, scale, gain)
            pre_ref[...] = pre
            pre_low_ref[...] = pre.astype(jnp.bfloat16)
            column_sums(sums_ref, pre, incoming * normed, incoming)


def backward_kernel(*refs):
    tables, pieces_refs, refs = refs[0:2], refs[2:10], refs[10:]
    inputs, outputs, scratch = refs[:18], refs[18:30], refs[30:]
    up_scratch, down_scratch, seams_ref, semaphores = scratch[2:]
    part = pl.program_id(0)

    @pl.when(part == 0)
    def begin():
        for matrix, target_ref in ((DOWN_MATRIX, down_scratch), (UP_MATRIX, up_scratch)):
            started(tables, pieces_refs, matrix, target_ref, seams_ref, semaphores)

    awaited(tables, pieces_refs, DOWN_MATRIX, part, down_scratch, seams_ref, semaphores)
    awaited(tables, pieces_refs, UP_MATRIX, part, up_scratch, seams_ref, semaphores)
    for stream in range(2):
        pre_ref, pre_low_ref, slope_ref, normed_ref, scale_ref, rows_ref, out_ref, own_down_ref, own_up_ref = inputs[
            9 * stream : 9 * stream + 9
        ]
        up_in_ref, up_sum_ref, attn_ref, attn_low_ref, sums_ref, context_grad_ref = outputs[
            6 * stream : 6 * stream + 6
        ]
        total_ref = scratch[stream]
        if stream == 0:
            up, down = up_scratch[part].reshape(768, 768), down_scratch[part].reshape(768, 768)
        else:
            up, down = own_up_ref[0], own_down_ref[0]
        up_in = dot(pre_low_ref[...], down, NT) * slope_ref[0].astype(jnp.float32)
        up_in = up_in.astype(jnp.bfloat16)
        up_in_ref[0] = up_in
        up_sum_ref[0] = jnp.sum(up_in.astype(jnp.float32), 0, keepdims=True)
        back = dot(up_in, up, NT)

        @pl.when(part == 0)
        def first():
            total_ref[...] = back

        @pl.when(part > 0)
        def later():
            total_ref[...] = total_ref[...] + back

        @pl.when(part == 3)
        def last():
            incoming = total_ref[...] + pre_ref[...]
            normed = normed_ref[...]
            attn = norm_pull(incoming, normed, scale_ref[...], rows_ref[3:4])
            attn_low = attn.astype(jnp.bfloat16)
            attn_ref[...] = attn
            attn_low_ref[...] = attn_low
            column_sums(sums_ref, attn, incoming * normed, incoming)
            for number in range(4):
                context_grad_ref[number] = dot(attn_low, out_ref[number], NT).astype(jnp.bfloat16)


def whole(*shape):
    return pl.BlockSpec(shape, lambda t: (0,) * len(shape), pipeline_mode=pl.Buffered(1))


def result(*shape):
    return pl.BlockSpec(shape, lambda t: (0,) * len(shape))


def by_part(*shape):
    return pl.BlockSpec((1,) + shape, lambda t: (t,) + (0,) * len(shape))


PIECES_SPECS = [pl.BlockSpec(memory_space=pltpu.SMEM)] * 2 + [
    pl.BlockSpec(memory_space=pl.ANY)
] * 8


def feed_forward(tables, pieces, text, layout):
    positions = text[0].shape[0]
    small = jnp.zeros((8, 128), jnp.float32)
    in_specs, operands, out_specs, out_shape, scratch = [], [], [], [], []
    for number, stream in enumerate((text, layout)):
        act, context, out, up, up_bias, down, rows, cotangent = stream
        width, hidden = act.shape[1], up_bias.shape[2]
        matrices = (out, up, down)
        specs = (whole(4, 256, width), by_part(width, hidden), by_part(hidden, width))
        if number == 0:
            matrices, specs = (small,) * 3, (whole(8, 128),) * 3
        in_specs += [
            whole(positions, width),
            whole(4, positions, 256),
            specs[0],
            specs[1],
            by_part(1, hidden),
            specs[2],
            whole(8, width),
            whole(1, positions, width),
            whole(8, 128),
        ]
        operands += [act, context, matrices[0], matrices[1], up_bias, matrices[2], rows, cotangent, small]
        out_specs += [
            result(positions, width),
            result(positions, width),
            result(positions, 1),
            by_part(positions, hidden),
            by_part(positions, hidden),
            result(1, positions, width),
            result(positions, width),
            result(positions, width),
            result(8, width),
        ]
        out_shape += [
            outside((positions, width), jnp.bfloat16),
            outside((positions, width), jnp.float32),
            outside((positions, 1), jnp.float32),
            outside((4, positions, hidden), jnp.bfloat16),
            outside((4, positions, hidden), jnp.bfloat16),
            outside((1, positions, width), jnp.bfloat16),
            outside((positions, width), jnp.float32),
            outside((positions, width), jnp.bfloat16),
            outside((8, width), jnp.float32),
        ]
        scratch += [
            pltpu.VMEM((positions, width), jnp.float32),
            pltpu.VMEM((positions, width), jnp.float32),
            pltpu.VMEM((positions, width), jnp.bfloat16),
        ]
    results = pl.pallas_call(
        forward_kernel,
        grid=(4,),
        in_specs=PIECES_SPECS + in_specs,
        out_specs=out_specs + [result(4, 256, 768)],
        out_shape=out_shape + [outside((4, 256, 768), jnp.bfloat16)],
        scratch_shapes=scratch
        + [
            pltpu.VMEM((4, 16, 16, 768), jnp.bfloat16),
            pltpu.VMEM((4, 48, 16, 768), jnp.bfloat16),
            pltpu.VMEM((4, 48, 16, 768), jnp.bfloat16),
            pltpu.VMEM((4, 6, 16, 768), jnp.bfloat16),
            pltpu.SemaphoreType.DMA((4, 14)),
        ],
        compiler_params=pltpu.CompilerParams(vmem_limit_bytes=56 << 20),
        cost_estimate=pl.CostEstimate(flops=7 << 30, transcendentals=4 << 20, bytes_accessed=36 << 20),
        name="feed_forward",
    )(*tables, *kept_out(*pieces), *kept_out(*operands))
    return results[:9], results[9:18], results[18]


def feed_back(tables, pieces, text, layout):
    positions = text[0].shape[0]
    small = jnp.zeros((8, 128), jnp.float32)
    in_specs, operands, out_specs, out_shape, scratch = [], [], [], [], []
    for number, stream in enumerate((text, layout)):
        pre, pre_low, slope, normed, scale, rows, out, down, up = stream
        width, hidden = pre.shape[1], slope.shape[2]
        matrices, specs = (down, up), (by_part(hidden, width), by_part(width, hidden))
        if number == 0:
            matrices, specs = (small,) * 2, (whole(8, 128),) * 2
        in_specs += [
            whole(positions, width),
            whole(positions, width),
            by_part(positions, hidden),
            whole(positions, width),
            whole(positions, 1),
            whole(8, width),
            whole(4, 256, width),
            specs[0],
            specs[1],
        ]
        operands += [pre, pre_low, slope, normed, scale, rows, out, *matrices]
        out_specs += [
            by_part(positions, hidden),
            by_part(1, hidden),
            result(positions, width),
            result(positions, width),
            result(8, width),
            result(4, positions, 256),
        ]
        out_shape += [
            outside((4, positions, hidden), jnp.bfloat16),
            outside((4, 1, hidden), jnp.float32),
            outside((positions, width), jnp.float32),
            outside((positions, width), jnp.bfloat16),
            outside((8, width), jnp.float32),
            outside((4, positions, 256), jnp.bfloat16),
        ]
        scratch.append(pltpu.VMEM((positions, width), jnp.float32))
    results = pl.pallas_call(
        backward_kernel,
        grid=(4,),
        in_specs=PIECES_SPECS + in_specs,
        out_specs=out_specs,
        out_shape=out_shape,
        scratch_shapes=scratch
        + [
            pltpu.VMEM((4, 48, 16, 768), jnp.bfloat16),
            pltpu.VMEM((4, 48, 16, 768), jnp.bfloat16),
            pltpu.VMEM((4, 6, 16, 768), jnp.bfloat16),
            pltpu.SemaphoreType.DMA((4, 14)),
        ],
        compiler_params=pltpu.CompilerParams(vmem_limit_bytes=56 << 20),
        cost_estimate=pl.CostEstimate(flops=7 << 30, transcendentals=0, bytes_accessed=36 << 20),
        name="feed_back",
    )(*tables, *kept_out(*pieces), *kept_out(*operands))
    return results[:6], results[6:]


def sum_kernel(counts, table_ref, *refs):
    total = len(counts)
    sources, out_ref = refs[:total], refs[total]
    buffers, semaphores = refs[total + 1 : -1], refs[-1]
    entries = out_ref.shape[0]

    def copies(entry):
        found = []
        for number, (source, buffer) in enumerate(zip(sources, buffers)):
            at = 0
            for piece, count in enumerate(counts[number]):
                part, first = (table_ref[number, entry, piece, item] for item in range(2))
                found.append(
                    pltpu.make_async_copy(
                        source.at[part, pl.ds(first, count)],
                        buffer.at[entry, pl.ds(at, count)],
                        semaphores.at[number, entry, piece],
                    )
                )
                at += count
        return found

    pending = [copies(entry) for entry in range(entries)]
    for copy in sum(pending, []):
        copy.start()
    for entry in range(entries):
        for copy in pending[entry]:
            copy.wait()
        total_value = sum(buffer[entry].astype(jnp.float32) for buffer in buffers)
        out_ref[entry] = total_value.astype(jnp.bfloat16)


def sum_windows(*sources):
    entries = len(sources[0][1])
    counts = tuple(tuple(count for _, _, count in places[0]) for _, places in sources)
    widest = max(len(item) for item in counts)
    length = sum(counts[0])
    rows = []
    for _, places in sources:
        for entry in places:
            for index, first, _ in entry + [(0, 0, 0)] * (widest - len(entry)):
                rows += [jnp.asarray(index, jnp.int32), jnp.asarray(first, jnp.int32)]
    table = jnp.stack(rows).reshape(len(sources), entries, widest, 2)
    shape = (entries, length, 16, 768)
    size = entries * length * 16 * 768 * 2
    return pl.pallas_call(
        lambda *refs: sum_kernel(counts, *refs),
        in_specs=[pl.BlockSpec(memory_space=pltpu.SMEM)]
        + [pl.BlockSpec(memory_space=pl.ANY)] * len(sources),
        out_specs=pl.BlockSpec(memory_space=pltpu.VMEM),
        out_shape=outside(shape, jnp.bfloat16),
        scratch_shapes=[pltpu.VMEM(shape, jnp.bfloat16)] * len(sources)
        + [pltpu.SemaphoreType.DMA((len(sources), entries, widest))],
        compiler_params=pltpu.CompilerParams(vmem_limit_bytes=24 << 20),
        cost_estimate=pl.CostEstimate(
            flops=size, transcendentals=0, bytes_accessed=size * (len(sources) + 1)
        ),
        name="sum_windows",
    )(table, *(pltpu.with_memory_space_constraint(array, pltpu.HBM) for array, _ in sources))


EARLY_PIECES = ((2, 21, 20), (40, 59, 20), (78, 97, 17), (95, 0, 3))
LATE_PIECES = ((0, 19, 26),)


def exchange_pairs(flip):
    pairs = []
    for device in range(32):
        z, x, y, core = device // 8, device // 4 % 2, device // 2 % 2, device % 2
        z, x, y, core = flip(z, x, y, core)
        pairs.append((device, z * 8 + x * 4 + y * 2 + core))
    return pairs


ROUNDS = (
    exchange_pairs(lambda z, x, y, core: (z, x, y, 1 - core)),
    exchange_pairs(lambda z, x, y, core: (z, x, 1 - y, core) if core else (z, 1 - x, y, core)),
    exchange_pairs(lambda z, x, y, core: (z, 1 - x, y, core) if core else (z, x, 1 - y, core)),
    exchange_pairs(lambda z, x, y, core: (z ^ 1, x, y, core) if core else (z ^ 2, x, y, core)),
    exchange_pairs(lambda z, x, y, core: (z ^ 2, x, y, core) if core else (z ^ 1, x, y, core)),
)


LAST_PAIRS = [
    (z * 8 + rest * 2 + core, to * 8 + rest * 2 + core)
    for core, pairs in enumerate((((1, 0), (2, 3)), ((2, 0), (1, 3))))
    for z, to in pairs
    for rest in range(4)
]


def swap(value, step):
    return lax.ppermute(value, ("dp", "tensor"), ROUNDS[step])


def after(value, *others):
    return lax.optimization_barrier((value, others))[0]


def picked(value, index, axis):
    return lax.dynamic_index_in_dim(value, index, axis, keepdims=False)


def total_low(*values):
    return sum(value.astype(jnp.float32) for value in values).astype(jnp.bfloat16)


def tiled(value):
    return value.reshape(2, -1, 16, UNIT)


def window_places(pieces, place, entry, other):
    z, x, y, core = place
    own_x, own_y = (1 - x, 1 - y) if other else (x, y)
    part = jnp.where(core == 0, entry, own_y)
    across = jnp.where(core == 0, own_x, entry)
    return [(part, jnp.where(across == 0, first, second), n) for first, second, n in pieces]


def first_sent(kept, received, pieces, place):
    places = [window_places(pieces, place, entry, True) for entry in range(2)]
    return sum_windows((tiled(kept), places), (tiled(received), places))


def second_part(kept, received, second, pieces, place, own, *third):
    z, x, y, core = place
    entry = jnp.where(core == 0, y, x)
    entry = entry if own else 1 - entry
    places = [window_places(pieces, place, entry, False)]
    whole_entry = [[(entry, 0, second.shape[1])]]
    return sum_windows(
        (tiled(kept), places),
        (tiled(received), places),
        (second, whole_entry),
        *((value[None], [[(0, 0, second.shape[1])]]) for value in third),
    )[0]


def total_low(*values):
    return sum(value.astype(jnp.float32) for value in values).astype(jnp.bfloat16)


def line_blocks(value, place):
    z, x, y, core = place
    blocks = value.reshape(3, TILES, 16, UNIT)
    order = jnp.array([2, 0, 1, 2])
    high, low = z // 2, z % 2
    lead = jnp.where(core == 0, high, low)
    rest = jnp.where(core == 0, low, high)

    def block(leading, trailing):
        layer = jnp.where(core == 0, 2 * leading + trailing, leading + 2 * trailing)
        return order[layer], 0, TILES

    sent = sum_windows((blocks, [[block(1 - lead, entry)] for entry in range(2)]))
    return sent, (blocks, block(lead, 1 - rest), block(lead, rest), rest)


def late_line(value, place):
    z, x, y, core = place
    upper = jnp.where(core == 0, z // 2, z % 2)
    sent = lax.dynamic_slice_in_dim(value, 6 * (1 - upper), TILES)
    kept = lax.dynamic_slice_in_dim(value, 6 * upper, TILES)
    kept = total_low(kept, swap(sent, 3))
    return kept, lax.ppermute(kept, ("dp", "tensor"), LAST_PAIRS)


def gather_pieces(frame, place, prepared):
    z, x, y, core = place
    own = frame.reshape(TILES, 16, UNIT)
    near = swap(own, 4)
    lead = jnp.where(core == 0, z // 2, z % 2)
    outer = (z == 0) | (z == 3)
    groups = []
    for first in (True, False):
        sent = jnp.where(outer == first, own, near)
        if groups:
            sent = after(sent, groups[0][1])
        groups.append((sent, swap(sent, 3)))
    part = jnp.arange(32) // 8
    window = jnp.arange(32) % 8
    its_z, its_x, its_y, its_core = window // 2, window % 2, part // 2, part % 2
    off_x, off_y = its_x != x, its_y != y
    which = 2 * (its_core != core) + jnp.where(its_core == 0, off_y, off_x)
    its_lead = jnp.where(its_core == 0, z // 2, z % 2)
    pairs = [jnp.stack(group) for group in groups]
    outer_four = jnp.concatenate((pairs[0], swap(pairs[0], 1)), 0)
    prepared = lax.optimization_barrier(prepared)
    outer_rest = swap(after(outer_four, pairs[1], prepared), 2)
    inner_four = jnp.concatenate((pairs[1], swap(after(pairs[1], outer_four), 1)), 0)
    outer_other = (swap(outer_four, 0), swap(after(outer_rest, inner_four), 0))
    inner_rest = swap(inner_four, 2)
    tables = []
    for first in (True, False):
        if first:
            sent_z = 3 * its_lead
        else:
            sent_z = jnp.where(its_core == 0, 1 + its_lead, 2 - its_lead)
        slot = 2 * jnp.where(its_core == 0, off_x, off_y) + (its_z != sent_z)
        tables.append(jnp.stack((which, slot)).astype(jnp.int32))
    return tables, (outer_four, outer_rest) + outer_other, (inner_four, inner_rest), prepared


def rearranged(stack):
    def matrix(first, count, height):
        return stack[:, first : first + count].reshape(4, height, -1)

    gap = jnp.zeros((4, 768, 64), stack.dtype)
    heads = []
    for slot in range(3):
        heads += [matrix(192 * slot, 192, 768), gap]
    small = []
    for slot in range(3):
        columns = matrix(2304 + 12 * slot, 12, 192)
        small.append(spaced(columns.reshape(768, 48)).reshape(4, 192, 256))
    rows = matrix(2340, 12, 48).transpose(0, 2, 1)
    return (
        jnp.concatenate(heads, 2),
        jnp.concatenate(small, 2),
        spaced(rows.reshape(768, 48)).reshape(4, 192, 256).transpose(0, 2, 1),
        matrix(2352, 48, 192),
        matrix(2400, 48, 192),
    )


def stack_pieces(stack):
    frames = jnp.stack([stack[:, 304 * window : 304 * window + FRAME] for window in range(8)], 1)
    seam = (jnp.arange(FRAME)[:, None] >= 304) & (jnp.arange(8) < 7)[:, None, None]
    frames = jnp.where(seam, 0.0, frames).astype(stack.dtype).reshape(32, TILES, 16, UNIT)
    number = jnp.arange(32)
    tables, groups = [], []
    for chosen in ((0, 1, 6, 7), (2, 3, 4, 5)):
        slot = sum(jnp.where(number % 8 == window, k, 0) for k, window in enumerate(chosen))
        tables.append(jnp.stack((number // 8, slot)).astype(jnp.int32))
        groups.append(
            tuple(jnp.stack([frames[part * 8 + w] for w in chosen]) for part in range(4))
        )
    return tables, groups[0], groups[1]


def spaced(vector):
    gap = jnp.zeros((vector.shape[0], 48), vector.dtype)
    first, second, third = vector[:, 0:16], vector[:, 16:32], vector[:, 32:48]
    return jnp.concatenate((second, gap, first, gap, gap, gap[:, :16], third, gap), 1)


def unspaced(value):
    return jnp.concatenate((value[:, 64:80], value[:, 0:16], value[:, 192:208]), 1).reshape(-1)


def shards(
    text_in,
    layout_in,
    lengths,
    text_mask,
    box_mask,
    text_cot,
    layout_cot,
    master,
    first_moment,
    second_moment,
    ema_weights,
    vectors,
    vector_first,
    vector_second,
    vector_ema,
):
    parts = lax.axis_size("tensor")
    dp_count = lax.axis_size("dp")
    tensor_index = lax.axis_index("tensor")
    dp_index = lax.axis_index("dp")
    span = master.shape[2]
    near = dp_count == 8 and parts == 4
    place = (dp_index // 2, dp_index % 2, tensor_index // 2, tensor_index % 2)
    shift = (2 * dp_index).reshape(1)
    all_parts = jnp.arange(parts, dtype=jnp.int32)
    own_parts = all_parts[::2] + place[3]
    other_parts = all_parts[::2] + 1 - place[3]
    biases = split_vector(vectors)
    length = lax.dynamic_slice_in_dim(lengths, tensor_index, 1)

    def product(spec, left, right):
        return jnp.einsum(spec, left, right, preferred_element_type=jnp.float32)

    def over_parts(spec, left, right):
        return sum(product(spec, left[part], right[part]) for part in range(parts))

    def summed(value):
        return jnp.sum(value, 0, dtype=jnp.float32)

    gap = jnp.zeros((parts, 64), jnp.float32)
    none = jnp.zeros((parts, 256), jnp.float32)
    qkv_bias = jnp.concatenate(
        (biases[0].reshape(parts, 192), gap, none, biases[1].reshape(parts, 192), gap), 1
    )
    lqkv_bias = jnp.concatenate(
        (spaced(biases[9].reshape(parts, 48)), none, spaced(biases[10].reshape(parts, 48))), 1
    )
    text_flag = (text_mask[0] > 0)[:, None]
    box_flag = (box_mask[0] > 0)[:, None]
    text_act = jnp.where(text_flag, biases[18], text_in[0].astype(jnp.float32))
    layout_act = jnp.where(box_flag, biases[19], layout_in[0].astype(jnp.float32))
    text_low = text_act.astype(jnp.bfloat16)
    layout_low = layout_act.astype(jnp.bfloat16)
    text_rows, layout_rows = vectors[:6144].reshape(8, D), vectors[9216:10752].reshape(8, L)
    up_bias, lup_bias = biases[8].reshape(parts, 1, -1), biases[17].reshape(parts, 1, -1)
    prepared = (
        length,
        qkv_bias,
        lqkv_bias,
        text_act,
        layout_act,
        text_low,
        layout_low,
        text_rows,
        layout_rows,
        up_bias,
        lup_bias,
        layout_cot,
    )
    if near:
        tables, outer, inner, prepared = gather_pieces(
            cast_frame(shift, master), place, prepared
        )
        qkv_weight, lqkv_weight, lout_weight, lup_weight, ldown_weight = unpack(tables[0], outer)
    else:
        wire = master.reshape(-1, 192).astype(jnp.bfloat16)
        stack = lax.all_gather(wire[None], ("tensor", "dp"), axis=0, tiled=True)
        stack = stack.reshape(parts, -1, UNIT)
        qkv_weight, lqkv_weight, lout_weight, lup_weight, ldown_weight = rearranged(stack)
        tables, outer, inner = stack_pieces(stack)
    (
        length,
        qkv_bias,
        lqkv_bias,
        text_act,
        layout_act,
        text_low,
        layout_low,
        text_rows,
        layout_rows,
        up_bias,
        lup_bias,
        layout_cot,
    ) = prepared
    qkv = (product("sd,tde->tse", text_low, qkv_weight) + qkv_bias[:, None]).astype(jnp.bfloat16)
    lqkv = (product("sd,tde->tse", layout_low, lqkv_weight) + lqkv_bias[:, None]).astype(
        jnp.bfloat16
    )
    context, lcontext, log_total = attend(length, qkv, lqkv)
    if near:
        inner = inner + (swap(inner[0], 0), swap(after(inner[1], context), 0))
    pieces = outer + inner
    text_ahead, layout_ahead, out_weight = feed_forward(
        tables,
        pieces,
        (text_act, context, None, None, up_bias, None, text_rows, text_cot),
        (
            layout_act,
            lcontext,
            lout_weight,
            lup_weight,
            lup_bias,
            ldown_weight,
            layout_rows,
            layout_cot,
        ),
    )
    text_mid_low, text_normed, text_scale, text_hidden, text_slope, text_out = text_ahead[:6]
    text_pre, text_down_in, text_sums_two = text_ahead[6:]
    layout_mid_low, layout_normed, layout_scale, layout_hidden, layout_slope = layout_ahead[:5]
    layout_out, layout_pre, layout_down_in, layout_sums_two = layout_ahead[5:]
    text_behind, layout_behind = feed_back(
        tables,
        pieces,
        (
            text_pre,
            text_down_in,
            text_slope,
            text_normed,
            text_scale,
            text_rows,
            out_weight,
            None,
            None,
        ),
        (
            layout_pre,
            layout_down_in,
            layout_slope,
            layout_normed,
            layout_scale,
            layout_rows,
            lout_weight,
            ldown_weight,
            lup_weight,
        ),
    )
    text_up_grad, text_up_sums, text_pre_one, text_attn_in, text_sums_one, context_grad = text_behind
    layout_up_grad, layout_up_sums, layout_pre_one = layout_behind[:3]
    layout_attn_in, layout_sums_one, lcontext_grad = layout_behind[3:]
    early_of = (text_mid_low, text_up_grad, text_hidden, text_down_in, context, text_attn_in)
    if near:
        early_sent = early_grads(other_parts, *early_of)
        early_received = swap(early_sent, 0)
        early_kept = early_grads(after(own_parts, early_sent), *early_of)
    else:
        early_all = early_grads(all_parts, *early_of)
    if near:
        early_received = after(early_received, early_kept)
        early_sent = first_sent(early_kept, early_received, EARLY_PIECES, place)
        early_second = swap(early_sent, 1)
        context_grad = after(context_grad, early_sent)
    qkv_in, lqkv_in = attend_back(
        length, qkv, lqkv, log_total, context, lcontext, context_grad, lcontext_grad
    )
    late_of = [
        text_low,
        qkv_in,
        layout_low,
        lqkv_in,
        lcontext,
        layout_attn_in,
        layout_mid_low,
        layout_up_grad,
        layout_hidden,
        layout_down_in,
    ]
    if near:
        late_sent = late_grads(other_parts, *late_of)
        late_received = swap(late_sent, 0)
        late_kept = late_grads(after(own_parts, late_sent), *late_of)
        late_received = after(late_received, late_kept)
        late_sent = first_sent(late_kept, late_received, LATE_PIECES, place)
        late_second = swap(late_sent, 1)
        early_second = after(early_second, late_sent)
        early_of = (early_kept, early_received, early_second, EARLY_PIECES, place)
        early_sent = second_part(*early_of, False)
        early_third = swap(early_sent, 2)
        qkv_in, lqkv_in = after((qkv_in, lqkv_in), early_sent)
    else:
        late_all = late_grads(all_parts, *late_of)
    text_full = text_pre_one + over_parts("se,de->sd", qkv_in, qkv_weight)
    layout_full = layout_pre_one + over_parts("se,de->sd", lqkv_in, lqkv_weight)
    text_in_grad = jnp.where(text_flag, 0.0, text_full)
    layout_in_grad = jnp.where(box_flag, 0.0, layout_full)
    text_embed_grad = summed(jnp.where(text_flag, text_full, 0.0))
    layout_embed_grad = summed(jnp.where(box_flag, layout_full, 0.0))
    qkv_sums = jnp.sum(qkv_in, 1, dtype=jnp.float32)
    lqkv_sums = jnp.sum(lqkv_in, 1, dtype=jnp.float32)
    vector_part = jnp.concatenate(
        [
            qkv_sums[:, 0:192].reshape(-1),
            qkv_sums[:, 512:704].reshape(-1),
            text_sums_one[:3].reshape(-1),
            text_sums_two[:3].reshape(-1),
            text_up_sums.reshape(-1),
            unspaced(lqkv_sums[:, 0:256]),
            unspaced(lqkv_sums[:, 512:768]),
            layout_sums_one[:3].reshape(-1),
            layout_sums_two[:3].reshape(-1),
            layout_up_sums.reshape(-1),
            text_embed_grad,
            layout_embed_grad,
        ]
    )
    if near:
        vector_grad = vector_part + swap(vector_part, 0)
        early_third = after(early_third, vector_grad)
        early_sum = second_part(*early_of, True, early_third)
        early_sent, (blocks, next_place, own_place, rest) = line_blocks(early_sum, place)
        early_fourth = swap(early_sent, 3)
        vector_next = swap(vector_grad, 1)
        late_second = after(late_second, early_sent)
        late_of = (late_kept, late_received, late_second, LATE_PIECES, place)
        late_sent = second_part(*late_of, False)
        late_third = swap(late_sent, 2)
        vector_grad = vector_grad + after(vector_next, late_sent)
        vector_next = swap(vector_grad, 2)
        late_third = after(late_third, vector_grad)
        late_sum = second_part(*late_of, True, late_third)
        vector_grad = vector_grad + after(vector_next, late_sum)
        vector_next = swap(vector_grad, 3)
        early_fourth = after(early_fourth, late_sum)

        def early_block(block_place, entry):
            return sum_windows(
                (blocks, [[block_place]]), (early_fourth, [[(entry, 0, TILES)]])
            )[0]

        early_sent = early_block(next_place, 1 - rest)
        early_last = swap(early_sent, 4)
        late_kept, late_last = late_line(after(late_sum, early_sent), place)
        early_kept = early_block(own_place, rest)
        vector_grad = vector_grad + after(vector_next, early_kept)
        vector_grad = vector_grad + swap(vector_grad, 4)
        span_grad, squares = finish(
            jnp.stack((2 * dp_index, dp_index)),
            *(item.reshape(FRAME, UNIT) for item in (early_kept, early_last, late_kept, late_last)),
        )
        squares = lax.all_to_all(squares, ("dp", "tensor"), 0, 0, tiled=True)
        matrix_square = jnp.sum(squares)
    else:
        flat_grad = jnp.concatenate(
            (late_all[:, :576], early_all[:, :1728], late_all[:, 576:]), 1
        ).reshape(parts * dp_count, -1, 192)
        span_grad = lax.psum_scatter(flat_grad, ("tensor", "dp"), scatter_dimension=0, tiled=True)
        span_grad = span_grad.astype(jnp.float32).reshape(master.shape)
        vector_grad = lax.psum(vector_part, ("dp", "tensor"))
        matrix_square = lax.psum(jnp.sum(span_grad * span_grad), ("dp", "tensor"))
    grad_norm = jnp.sqrt(matrix_square + jnp.sum(vector_grad * vector_grad))
    factor = clip_bound / jnp.maximum(grad_norm, clip_bound)
    if near:
        matrix_new = adam(
            (dp_index * span).reshape(1),
            factor.reshape(1),
            master,
            span_grad,
            first_moment,
            second_moment,
            ema_weights,
        )
        matrix_new = tuple(matrix_new)
    else:
        rates = lax.dynamic_slice_in_dim(rate_table(parts), dp_index * span, span)
        matrix_new = adam_update(
            master,
            span_grad,
            first_moment,
            second_moment,
            ema_weights,
            rates.reshape(master.shape),
            factor,
        )
    vector_new = adam_update(
        vectors, vector_grad, vector_first, vector_second, vector_ema, vector_rate, factor
    )
    return (
        (
            text_out,
            layout_out,
            text_in_grad[None],
            layout_in_grad[None],
            grad_norm,
        )
        + matrix_new
        + vector_new
    )


def solution(mesh):
    in_specs = (
        P(("dp", "tensor"), None, None),
        P(("dp", "tensor"), None, None),
        P("dp"),
        P(("dp", "tensor"), None),
        P(("dp", "tensor"), None),
        P(("dp", "tensor"), None, None),
        P(("dp", "tensor"), None, None),
        P("tensor", "dp", None),
        P("tensor", "dp", None),
        P("tensor", "dp", None),
        P("tensor", "dp", None),
        P(),
        P(),
        P(),
        P(),
    )
    out_specs = (
        P(("dp", "tensor"), None, None),
        P(("dp", "tensor"), None, None),
        P(("dp", "tensor"), None, None),
        P(("dp", "tensor"), None, None),
        P(),
        P("tensor", "dp", None),
        P("tensor", "dp", None),
        P("tensor", "dp", None),
        P("tensor", "dp", None),
        P("tensor", "dp", None),
        P(),
        P(),
        P(),
        P(),
        P(),
    )
    return jax.shard_map(shards, mesh=mesh, in_specs=in_specs, out_specs=out_specs, check_vma=False)
```

```python
from functools import partial
import math

import jax
import jax.numpy as jnp
from jax import lax
from jax.experimental import pallas as pl
from jax.experimental.pallas import tpu as pltpu
from jax.sharding import PartitionSpec as P

D = 768
HT = 64
FF = 3072
L = 192
HL = 16
LF = 768
STEP = 5


norm_eps = 1e-05
clip_bound = 1.0
first_decay = 0.5
second_decay = 0.6
adam_floor = 1e-08
weight_decay = 0.01
vector_rate = 0.5
average_keep = 0.5
masked_score = -1e30


def piece_table(parts):
    text_spread = 1.0 / math.sqrt(D)
    layout_spread = 1.0 / math.sqrt(L)
    return [
        (D, D // parts, text_spread),
        (D, D // parts, text_spread),
        (D, D // parts, text_spread),
        (D // parts, D, 8.0 * text_spread),
        (D, FF // parts, text_spread),
        (FF // parts, D, 1.0 / math.sqrt(FF)),
        (L, L // parts, layout_spread),
        (L, L // parts, layout_spread),
        (L, L // parts, layout_spread),
        (L // parts, L, 8.0 * layout_spread),
        (L, LF // parts, layout_spread),
        (LF // parts, L, 1.0 / math.sqrt(LF)),
    ]


def rate_table(parts):
    return jnp.concatenate(
        [
            jnp.full((height * width,), spread, jnp.float32)
            for height, width, spread in piece_table(parts)
        ]
    )


def split_vector(flat):
    pieces = []
    start = 0
    for width in [D] * 8 + [FF] + [L] * 8 + [LF] + [D, L]:
        pieces.append(flat[start : start + width])
        start = start + width
    return pieces


def project(acts, weight):
    return jnp.einsum("psd,de->pse", acts, weight, preferred_element_type=jnp.float32)


def project_back(incoming, weight):
    return jnp.einsum("pse,de->psd", incoming, weight, preferred_element_type=jnp.float32)


def weight_grad(acts, incoming):
    return jnp.einsum("psd,pse->de", acts, incoming, preferred_element_type=jnp.float32)


def norm_forward(value, gain, shift):
    mean = jnp.mean(value, -1, keepdims=True)
    centred = value - mean
    scale = lax.rsqrt(jnp.mean(centred * centred, -1, keepdims=True) + norm_eps)
    normed = centred * scale
    return (normed * gain + shift, normed, scale)


def norm_backward(incoming, normed, scale, gain):
    scaled = incoming * gain
    result = scale * (
        scaled
        - jnp.mean(scaled, -1, keepdims=True)
        - normed * jnp.mean(scaled * normed, -1, keepdims=True)
    )
    return (result, jnp.sum(incoming * normed, (0, 1)), jnp.sum(incoming, (0, 1)))


def gelu_back(value, incoming):
    unused, pull = jax.vjp(partial(jax.nn.gelu, approximate=False), value)
    return pull(incoming)[0]


def adam_update(weight, gradient, first, second, average, rate, factor):
    clipped = gradient * factor
    new_first = first_decay * first + (1.0 - first_decay) * clipped
    new_second = second_decay * second + (1.0 - second_decay) * clipped * clipped
    first_hat = new_first / (1.0 - first_decay**STEP)
    second_hat = new_second / (1.0 - second_decay**STEP)
    updated = weight - rate * (
        first_hat / (jnp.sqrt(second_hat) + adam_floor) + weight_decay * weight
    )
    return (
        updated,
        new_first,
        new_second,
        updated.astype(jnp.bfloat16),
        average_keep * average + (1.0 - average_keep) * updated,
    )


COST = pl.CostEstimate(flops=5 << 30, transcendentals=0, bytes_accessed=10 << 20)
NT = (((1,), (1,)), ((), ()))
NN = (((1,), (0,)), ((), ()))
TN = (((0,), (0,)), ((), ()))


def dot(left, right, dims):
    return lax.dot_general(left, right, dims, preferred_element_type=jnp.float32)


def kept_out(*values):
    return [pltpu.with_memory_space_constraint(value, pltpu.HBM) for value in values]


def outside(shape, dtype):
    return pltpu.HBM(shape, dtype)


def lane_of(shape):
    return lax.broadcasted_iota(jnp.int32, shape, len(shape) - 1)


def head_tiles(text_ref, layout_ref, slot, tile, high):
    first = slot * 256 + tile * 128
    text = text_ref[0, :, first : first + 128]
    layout = layout_ref[0, :, first : first + 128]
    low = lane_of(text.shape) < 64
    if high:
        return jnp.where(low, layout, text)
    return jnp.where(low, text, layout)


def own_lanes(shape, high):
    low = lane_of(shape) < 64
    return ~low if high else low


def scaled_query(query, high):
    own = own_lanes(query.shape, high)
    marker = 16 if high else 80
    scale = jnp.where(own, 0.125, 0.25)
    scaled = (query.astype(jnp.float32) * scale).astype(jnp.bfloat16)
    return jnp.where(lane_of(query.shape) == marker, jnp.bfloat16(1.0), scaled)


def masked_key(key, high, length):
    marker = 16 if high else 80
    beyond = lax.broadcasted_iota(jnp.int32, key.shape, 0) >= length
    column = jnp.where(beyond, jnp.float32(-1e30), jnp.float32(0.0)).astype(jnp.bfloat16)
    return jnp.where(lane_of(key.shape) == marker, column, key)


def attend_kernel(length_ref, text_ref, layout_ref, context_ref, layout_context_ref, total_ref):
    length = length_ref[0]
    found = []
    for head in range(3):
        tile, high = head // 2, head % 2 == 1
        query = scaled_query(head_tiles(text_ref, layout_ref, 0, tile, high), high)
        key = masked_key(head_tiles(text_ref, layout_ref, 1, tile, high), high, length)
        value = head_tiles(text_ref, layout_ref, 2, tile, high)
        scores = dot(key, query, NT)
        top = jnp.max(scores, 0, keepdims=True)
        raised = jnp.exp(scores - top)
        total = jnp.sum(raised, 0, keepdims=True)
        probs = (raised * (1.0 / total)).astype(jnp.bfloat16)
        total_ref[0, head : head + 1, :] = top + jnp.log(total)
        context = dot(value, probs, TN)
        found.append(context.T)
    low = lane_of(found[0].shape) < 64
    zero = jnp.zeros_like(found[0])
    context_ref[0, :, 0:128] = jnp.where(low, found[0], found[1]).astype(jnp.bfloat16)
    context_ref[0, :, 128:256] = jnp.where(low, found[2], zero).astype(jnp.bfloat16)
    layout_context_ref[0, :, 0:128] = jnp.where(low, found[1], found[0]).astype(jnp.bfloat16)
    layout_context_ref[0, :, 128:256] = jnp.where(low, zero, found[2]).astype(jnp.bfloat16)


def block(rows, width):
    return pl.BlockSpec((1, rows, width), lambda t: (t, 0, 0))


def attend(length, text, layout):
    parts, positions, _ = text.shape
    return pl.pallas_call(
        attend_kernel,
        grid=(parts,),
        in_specs=[
            pl.BlockSpec(memory_space=pltpu.SMEM),
            block(positions, 768),
            block(positions, 768),
        ],
        out_specs=[block(positions, 256), block(positions, 256), block(8, positions)],
        out_shape=[
            outside((parts, positions, 256), jnp.bfloat16),
            outside((parts, positions, 256), jnp.bfloat16),
            outside((parts, 8, positions), jnp.float32),
        ],
        compiler_params=pltpu.CompilerParams(vmem_limit_bytes=24 << 20),
        cost_estimate=COST,
        name="attend",
    )(length, *kept_out(text, layout))


def attend_back_kernel(
    length_ref,
    text_ref,
    layout_ref,
    total_ref,
    context_ref,
    layout_context_ref,
    context_grad_ref,
    layout_context_grad_ref,
    text_grad_ref,
    layout_grad_ref,
):
    length = length_ref[0]
    grads = ([], [], [])
    for head in range(3):
        tile, high = head // 2, head % 2 == 1
        raw_query = head_tiles(text_ref, layout_ref, 0, tile, high)
        raw_key = head_tiles(text_ref, layout_ref, 1, tile, high)
        value = head_tiles(text_ref, layout_ref, 2, tile, high)
        incoming = head_tiles(context_grad_ref, layout_context_grad_ref, 0, tile, high)
        context = head_tiles(context_ref, layout_context_ref, 0, tile, high)
        own = own_lanes(value.shape, high)
        query = scaled_query(raw_query, high)
        key = masked_key(raw_key, high, length)
        product = (incoming.astype(jnp.float32) * context.astype(jnp.float32)).T
        start = 0 if high else 64
        layout_mean = jnp.sum(product[start : start + 16], 0, keepdims=True)
        joint_mean = jnp.sum(product, 0, keepdims=True)
        zero = jnp.zeros_like(value)
        probs = jnp.exp(dot(key, query, NT) - total_ref[0, head : head + 1, :])
        value_grad = dot(probs.astype(jnp.bfloat16), incoming, NN)
        joint = (probs * (dot(value, incoming, NT) - joint_mean)).astype(jnp.bfloat16)
        alone = (
            probs * (dot(jnp.where(own, zero, value), incoming, NT) - layout_mean)
        ).astype(jnp.bfloat16)
        key_grad = jnp.where(own, dot(joint, raw_query, NN) * 0.125, dot(alone, raw_query, NN) * 0.25)
        rows = lax.broadcasted_iota(jnp.int32, (128, value.shape[0]), 0) < 64
        if high:
            rows = ~rows
        query_grad = jnp.where(
            rows, dot(raw_key, joint, TN) * 0.125, dot(raw_key, alone, TN) * 0.25
        )
        grads[0].append(query_grad.T)
        grads[1].append(key_grad)
        grads[2].append(value_grad)
    low = lane_of(grads[0][0].shape) < 64
    zero = jnp.zeros_like(grads[0][0])
    for slot in range(3):
        first, second, third = grads[slot]
        at = slot * 256
        text_grad_ref[0, :, at : at + 128] = jnp.where(low, first, second).astype(jnp.bfloat16)
        text_grad_ref[0, :, at + 128 : at + 256] = jnp.where(low, third, zero).astype(jnp.bfloat16)
        layout_grad_ref[0, :, at : at + 128] = jnp.where(low, second, first).astype(jnp.bfloat16)
        layout_grad_ref[0, :, at + 128 : at + 256] = jnp.where(low, zero, third).astype(
            jnp.bfloat16
        )


def attend_back(length, text, layout, total, context, layout_context, grad, layout_grad):
    parts, positions, _ = text.shape
    return pl.pallas_call(
        attend_back_kernel,
        grid=(parts,),
        in_specs=[
            pl.BlockSpec(memory_space=pltpu.SMEM),
            block(positions, 768),
            block(positions, 768),
            block(8, positions),
            block(positions, 256),
            block(positions, 256),
            block(positions, 256),
            block(positions, 256),
        ],
        out_specs=[block(positions, 768), block(positions, 768)],
        out_shape=[
            outside((parts, positions, 768), jnp.bfloat16),
            outside((parts, positions, 768), jnp.bfloat16),
        ],
        compiler_params=pltpu.CompilerParams(vmem_limit_bytes=30 << 20),
        cost_estimate=COST,
        name="attend_back",
    )(length, *kept_out(text, layout, total, context, layout_context, grad, layout_grad))


SPAN = 235008
FRAME = 320
UNIT = 768


def cast_kernel(shift_ref, master_ref, frame_ref, flat_ref):
    whole = SPAN // 1024
    for step in range(whole):
        flat_ref[pl.ds(8 * step, 8), :] = master_ref[0, 0, pl.ds(1024 * step, 1024)].reshape(8, 128)
    flat_ref[pl.ds(8 * whole, 4), :] = master_ref[0, 0, pl.ds(1024 * whole, 512)].reshape(4, 128)
    for column in range(6):
        rows = flat_ref[pl.ds(column, 306, stride=6), :]
        rows = jnp.concatenate((rows, jnp.zeros((14, 128), jnp.float32)), 0)
        rows = pltpu.roll(rows, shift_ref[0], 0)
        frame_ref[0, :, column * 128 : column * 128 + 128] = rows.astype(jnp.bfloat16)


def cast_frame(shift, master):
    return pl.pallas_call(
        cast_kernel,
        in_specs=[pl.BlockSpec(memory_space=pltpu.SMEM), pl.BlockSpec(memory_space=pltpu.VMEM)],
        out_specs=pl.BlockSpec(memory_space=pltpu.VMEM),
        out_shape=jax.ShapeDtypeStruct((1, FRAME, UNIT), jnp.bfloat16),
        scratch_shapes=[pltpu.VMEM((1840, 128), jnp.float32)],
        name="cast_frame",
    )(shift, master)


def finish_kernel(
    place_ref,
    slice_ref,
    inner_ref,
    inner_last_ref,
    outer_ref,
    outer_last_ref,
    late_ref,
    late_last_ref,
    flat_out_ref,
    square_ref,
    flat_ref,
):
    shift, window = place_ref[0], place_ref[1]
    row = lax.broadcasted_iota(jnp.int32, (FRAME, 128), 0)
    first = jnp.where(window == 7, 176, 0)
    last = jnp.where(window == 0, 320, jnp.where(window == 1, 272, jnp.where(window == 7, 320, 0)))
    late = (row >= first) & (row < last)
    inner = (window >= 2) & (window < 6)
    squares = jnp.zeros((8, 128), jnp.float32)
    for column in range(6):
        at = slice(column * 128, column * 128 + 128)
        rows = jnp.where(
            late,
            late_ref[:, at].astype(jnp.float32) + late_last_ref[:, at].astype(jnp.float32),
            jnp.where(
                inner,
                inner_ref[:, at].astype(jnp.float32) + inner_last_ref[:, at].astype(jnp.float32),
                outer_ref[:, at].astype(jnp.float32) + outer_last_ref[:, at].astype(jnp.float32),
            ),
        )
        rows = pltpu.roll(rows, FRAME - shift, 0)
        flat_ref[pl.ds(column, 306, stride=6), :] = rows[:306]
        masked = jnp.where(row < 306, rows, 0.0)
        squares = squares + jnp.sum((masked * masked).reshape(40, 8, 128), 0)
    square_ref[:, :512] = jnp.broadcast_to(slice_ref[...], (32, 512))
    square_ref[:, 512:] = jnp.broadcast_to(jnp.sum(squares, 0, keepdims=True), (32, 128))
    whole = SPAN // 1024
    for step in range(whole):
        flat_out_ref[0, 0, pl.ds(1024 * step, 1024)] = flat_ref[pl.ds(8 * step, 8), :].reshape(1024)
    flat_out_ref[0, 0, pl.ds(1024 * whole, 512)] = flat_ref[pl.ds(8 * whole, 4), :].reshape(512)


def finish(place, *values):
    return pl.pallas_call(
        finish_kernel,
        in_specs=[pl.BlockSpec(memory_space=pltpu.SMEM)]
        + [pl.BlockSpec(memory_space=pltpu.VMEM)] * 7,
        out_specs=[pl.BlockSpec(memory_space=pltpu.VMEM)] * 2,
        out_shape=[
            jax.ShapeDtypeStruct((1, 1, SPAN), jnp.float32),
            jax.ShapeDtypeStruct((32, 640), jnp.float32),
        ],
        scratch_shapes=[pltpu.VMEM((1840, 128), jnp.float32)],
        name="finish",
    )(place, *values)


RATE_STEPS = (
    (0, 768.0**-0.5),
    (576, 8.0 * 768.0**-0.5),
    (768, 768.0**-0.5),
    (1536, 3072.0**-0.5),
    (2304, 192.0**-0.5),
    (2340, 8.0 * 192.0**-0.5),
    (2352, 192.0**-0.5),
    (2400, 768.0**-0.5),
)


def adam_kernel(
    first_index_ref,
    shared_ref,
    weight_ref,
    gradient_ref,
    first_ref,
    second_ref,
    average_ref,
    new_weight_ref,
    new_first_ref,
    new_second_ref,
    low_ref,
    new_average_ref,
):
    width = weight_ref.shape[2]
    start = first_index_ref[0] + pl.program_id(0) * width
    shared = shared_ref[...]
    squares = jnp.where(lax.broadcasted_iota(jnp.int32, shared.shape, 1) < 512, shared * shared, shared)
    squares = jnp.sum(jnp.sum(squares, 0, keepdims=True), 1, keepdims=True)
    factor = 1.0 / jnp.maximum(jnp.sqrt(squares), 1.0)
    for at in range(0, width, CHUNK):
        count = min(CHUNK, width - at)
        place = pl.ds(at, count)

        def load(ref):
            return ref[0, 0, place].reshape(count // 128, 128)

        def store(ref, value):
            ref[0, 0, place] = value.reshape(count)

        shape = (count // 128, 128)
        index = lax.broadcasted_iota(jnp.int32, shape, 0) * 128 + start + at
        rate = jnp.full(shape, RATE_STEPS[0][1], jnp.float32)
        for row, value in RATE_STEPS[1:]:
            rate = jnp.where(index >= row * UNIT, jnp.float32(value), rate)
        weight = load(weight_ref)
        clipped = load(gradient_ref) * factor
        new_first = 0.5 * load(first_ref) + 0.5 * clipped
        new_second = 0.6 * load(second_ref) + 0.4 * clipped * clipped
        first_hat = new_first * (1.0 / (1.0 - 0.5**5))
        second_hat = new_second * (1.0 / (1.0 - 0.6**5))
        updated = weight - rate * (first_hat / (jnp.sqrt(second_hat) + 1e-8) + 0.01 * weight)
        store(new_weight_ref, updated)
        store(new_first_ref, new_first)
        store(new_second_ref, new_second)
        low_ref[0, 0, place] = updated.reshape(count).astype(jnp.bfloat16)
        store(new_average_ref, 0.5 * load(average_ref) + 0.5 * updated)


CHUNK = 1024


def adam(first_index, shared, weight, gradient, first, second, average, steps=3):
    span = weight.shape[2]
    spec = pl.BlockSpec((1, 1, span // steps), lambda i: (0, 0, i))
    full = jax.ShapeDtypeStruct(weight.shape, jnp.float32)
    return pl.pallas_call(
        adam_kernel,
        grid=(steps,),
        in_specs=[
            pl.BlockSpec(memory_space=pltpu.SMEM),
            pl.BlockSpec((32, 640), lambda i: (0, 0)),
        ]
        + [spec] * 5,
        out_specs=[spec] * 5,
        out_shape=[full, full, full, jax.ShapeDtypeStruct(weight.shape, jnp.bfloat16), full],
        name="adam",
    )(first_index, shared, weight, gradient, first, second, average)


def placing(rows, columns, row_axis):
    narrow = lax.broadcasted_iota(jnp.int32, (rows, columns), row_axis)
    wide = lax.broadcasted_iota(jnp.int32, (rows, columns), 1 - row_axis)
    place = jnp.where(narrow < 16, narrow + 64, jnp.where(narrow < 32, narrow - 16, narrow + 160))
    return jnp.where(place == wide, 1.0, 0.0).astype(jnp.bfloat16)


def wide_rows(value):
    return jnp.concatenate((value, jnp.zeros((value.shape[0], 64), value.dtype)), 1)


def early_kernel(
    parts_ref, mid_ref, up_in_ref, hidden_ref, down_in_ref, context_ref, attn_in_ref, early_ref
):
    early_ref[0, 0:192] = dot(context_ref[0], attn_in_ref[...], TN)[:192].astype(jnp.bfloat16)
    early_ref[0, 192:960] = dot(mid_ref[...], up_in_ref[0], TN).astype(jnp.bfloat16)
    early_ref[0, 960:1728] = dot(hidden_ref[0], down_in_ref[...], TN).astype(jnp.bfloat16)
    early_ref[0, 1728:] = jnp.zeros((96, 768), jnp.bfloat16)


def early_grads(parts, mid, up_in, hidden, down_in, context, attn_in):
    positions = mid.shape[0]
    count = parts.shape[0]
    fixed = pl.BlockSpec((positions, 768), lambda i, p: (0, 0))
    chosen = pl.BlockSpec((1, positions, 768), lambda i, p: (p[i], 0, 0))
    return pl.pallas_call(
        early_kernel,
        grid_spec=pltpu.PrefetchScalarGridSpec(
            num_scalar_prefetch=1,
            grid=(count,),
            in_specs=[
                fixed,
                chosen,
                chosen,
                fixed,
                pl.BlockSpec((1, positions, 256), lambda i, p: (p[i], 0, 0)),
                fixed,
            ],
            out_specs=pl.BlockSpec((1, 1824, 768), lambda i, p: (i, 0, 0)),
        ),
        out_shape=outside((count, 1824, 768), jnp.bfloat16),
        compiler_params=pltpu.CompilerParams(vmem_limit_bytes=24 << 20),
        cost_estimate=COST,
        name="early_grads",
    )(parts, *kept_out(mid, up_in, hidden, down_in, context, attn_in))


def late_kernel(
    parts_ref,
    text_ref,
    qkv_in_ref,
    layout_ref,
    lqkv_in_ref,
    lcontext_ref,
    lattn_in_ref,
    lmid_ref,
    lup_in_ref,
    lhidden_ref,
    ldown_in_ref,
    late_ref,
    heads_ref,
    rows_ref,
    slots_ref,
    small_ref,
):
    heads_grad = dot(text_ref[...], qkv_in_ref[0], TN)
    for tile in range(6):
        heads_ref[tile] = heads_grad[:, 128 * tile : 128 * tile + 128]
    for slot in range(3):
        for step in range(4):
            piece = jnp.concatenate(
                [heads_ref[2 * slot + half, pl.ds(step, 192, stride=4), :] for half in range(2)], 1
            )
            late_ref[0, 192 * slot : 192 * slot + 192, 192 * step : 192 * step + 192] = piece[
                :, :192
            ].astype(jnp.bfloat16)

    slots_ref[...] = jnp.zeros_like(slots_ref)
    lqkv_grad = dot(layout_ref[...], lqkv_in_ref[0], TN)
    for slot in range(3):
        for half in range(2):
            at = 256 * slot + 128 * half
            rows_ref[half, 0:192] = lqkv_grad[:, at : at + 128]
            for step in range(16):
                row = 16 * (3 * step + slot)
                slots_ref[row : row + 12, 128 * half : 128 * half + 128] = rows_ref[
                    half, pl.ds(step, 12, stride=16), :
                ]
    placed = dot(slots_ref[...].astype(jnp.bfloat16), placing(256, 48, 1), NN)
    for slot in range(3):
        for step in range(16):
            at = 16 * (3 * step + slot)
            small_ref[12 * slot : 12 * slot + 12, 48 * step : 48 * step + 48] = placed[at : at + 12]

    def gather(first, count):
        for step in range(4):
            piece = jnp.concatenate(
                [rows_ref[half, pl.ds(step, count, stride=4), :] for half in range(2)], 1
            )
            small_ref[first : first + count, 192 * step : 192 * step + 192] = piece[:, :192]

    lout_grad = dot(lcontext_ref[0], lattn_in_ref[...], TN)
    for head, at in enumerate((64, 0, 192)):
        rows_ref[0, 16 * head : 16 * head + 16, :] = lout_grad[at : at + 16, 0:128]
        rows_ref[1, 16 * head : 16 * head + 16, 0:64] = lout_grad[at : at + 16, 128:192]
    gather(36, 12)
    for first, left, right in (
        (48, lmid_ref[...], lup_in_ref[0]),
        (96, lhidden_ref[0], ldown_in_ref[...]),
    ):
        grad = dot(left, right, TN)
        rows_ref[0, 0:192, :] = grad[:, 0:128]
        rows_ref[1, 0:192, 0:64] = grad[:, 128:192]
        gather(first, 48)
    late_ref[0, 576:720] = small_ref[...].astype(jnp.bfloat16)


def late_grads(parts, text, qkv_in, layout, lqkv_in, lcontext, lattn_in, lmid, lup_in, lhidden, ldown_in):
    positions = text.shape[0]
    count = parts.shape[0]

    def fixed(width):
        return pl.BlockSpec((positions, width), lambda i, p: (0, 0))

    def chosen(width):
        return pl.BlockSpec((1, positions, width), lambda i, p: (p[i], 0, 0))

    return pl.pallas_call(
        late_kernel,
        grid_spec=pltpu.PrefetchScalarGridSpec(
            num_scalar_prefetch=1,
            grid=(count,),
            in_specs=[
                fixed(768),
                chosen(768),
                fixed(192),
                chosen(768),
                chosen(256),
                fixed(192),
                fixed(192),
                chosen(192),
                chosen(192),
                fixed(192),
            ],
            out_specs=pl.BlockSpec((1, 720, 768), lambda i, p: (i, 0, 0)),
            scratch_shapes=[
                pltpu.VMEM((6, 768, 128), jnp.float32),
                pltpu.VMEM((2, 192, 128), jnp.float32),
                pltpu.VMEM((768, 256), jnp.float32),
                pltpu.VMEM((144, 768), jnp.float32),
            ],
        ),
        out_shape=outside((count, 720, 768), jnp.bfloat16),
        compiler_params=pltpu.CompilerParams(vmem_limit_bytes=26 << 20),
        cost_estimate=COST,
        name="late_grads",
    )(parts, *kept_out(text, qkv_in, layout, lqkv_in, lcontext, lattn_in, lmid, lup_in, lhidden, ldown_in))


TILES = 20
HEAD_PIECES = ((0, 0, 20, 0), (1, 1, 16, 20), (1, 0, 1, 36), (7, 11, 9, 37))
OUT_PIECES = ((1, 17, 3, 0), (2, 1, 9, 3))
UP_PIECES = ((2, 10, 10, 0), (3, 1, 19, 10), (4, 1, 19, 29))
DOWN_PIECES = ((5, 1, 19, 0), (6, 1, 19, 19), (7, 1, 10, 38))
OUT_SEAMS = ((2, 2),)
UP_SEAMS = ((3, 9), (4, 28), (5, 47))
DOWN_SEAMS = ((6, 18), (7, 37))


def start_piece(table_ref, sources, part, window, first, count, target, semaphore):
    row = part * 8 + window
    which, slot = table_ref[0, row], table_ref[1, row]

    def among(low, high):
        if high - low == 1:
            place = sources[low].at[slot, pl.ds(first, count)]
            pltpu.make_async_copy(place, target, semaphore).start()
            return
        middle = (low + high) // 2

        @pl.when(which < middle)
        def lower():
            among(low, middle)

        @pl.when(which >= middle)
        def upper():
            among(middle, high)

    among(0, len(sources))


def wait_piece(table_ref, sources, part, window, first, count, target, semaphore):
    pltpu.make_async_copy(sources[0].at[0, pl.ds(first, count)], target, semaphore).wait()


def unpack_kernel(
    table_ref, *refs
):
    sources = refs[:12]
    qkv_ref, lqkv_ref, lwo_ref, lw1_ref, lw2_ref, frames_ref, rows_ref, small_ref, semaphores = refs[12:]
    part = pl.program_id(0)

    def each(act, number):
        for index, (window, first, count, at) in enumerate(HEAD_PIECES):
            target = frames_ref.at[number, pl.ds(at, count)]
            act(table_ref, sources, number, window, first, count, target, semaphores.at[number, index])

    @pl.when(part == 0)
    def begin():
        for number in range(4):
            each(start_piece, number)

    each(wait_piece, part)
    frames_ref[part, 19] = frames_ref[part, 19] + frames_ref[part, 36]

    def spread(source_ref, first, count, stride, target_ref):
        for step in range(4):
            piece = wide_rows(source_ref[first : first + count, 192 * step : 192 * step + 192])
            target_ref[0, pl.ds(step, count, stride=stride), :] = piece[:, :128]
            target_ref[1, pl.ds(step, count, stride=stride), :] = piece[:, 128:]

    small_ref[...] = frames_ref[part, 37:46].reshape(144, 768).astype(jnp.float32)
    for slot in range(3):
        for step in range(4):
            piece = frames_ref[part, 12 * slot : 12 * slot + 12, :, 192 * step : 192 * step + 192]
            piece = wide_rows(piece.reshape(192, 192).astype(jnp.float32))
            rows_ref[0, pl.ds(step, 192, stride=4), :] = piece[:, :128]
            rows_ref[1, pl.ds(step, 192, stride=4), :] = piece[:, 128:]
        qkv_ref[0, :, 256 * slot : 256 * slot + 128] = rows_ref[0].astype(jnp.bfloat16)
        qkv_ref[0, :, 256 * slot + 128 : 256 * slot + 256] = rows_ref[1].astype(jnp.bfloat16)
    place = placing(48, 256, 0)
    narrow = jnp.concatenate(
        [small_ref[0:48, 48 * step : 48 * step + 48] for step in range(16)], 0
    )
    placed = dot(narrow.astype(jnp.bfloat16), place, NN)
    for slot in range(3):
        for step in range(16):
            piece = placed[48 * step + 12 * slot : 48 * step + 12 * slot + 12]
            rows_ref[0, pl.ds(step, 12, stride=16), :] = piece[:, :128]
            rows_ref[1, pl.ds(step, 12, stride=16), :] = piece[:, 128:]
        lqkv_ref[0, :, 256 * slot : 256 * slot + 128] = rows_ref[0, 0:192].astype(jnp.bfloat16)
        lqkv_ref[0, :, 256 * slot + 128 : 256 * slot + 256] = rows_ref[1, 0:192].astype(jnp.bfloat16)
    spread(small_ref, 36, 12, 4, rows_ref)
    lwo_ref[...] = jnp.zeros_like(lwo_ref)
    for head, at in enumerate((64, 0, 192)):
        for half, width in ((0, 128), (1, 64)):
            lwo_ref[0, at : at + 16, 128 * half : 128 * half + width] = rows_ref[
                half, 16 * head : 16 * head + 16, :width
            ].astype(jnp.bfloat16)
    for first, target_ref in ((48, lw1_ref), (96, lw2_ref)):
        spread(small_ref, first, 48, 4, rows_ref)
        target_ref[0, :, 0:128] = rows_ref[0, 0:192].astype(jnp.bfloat16)
        target_ref[0, :, 128:192] = rows_ref[1, 0:192, :64].astype(jnp.bfloat16)


def unpack(table, sources):
    shapes = ((768, 768), (192, 768), (256, 192), (192, 192), (192, 192))
    return pl.pallas_call(
        unpack_kernel,
        grid=(4,),
        in_specs=[pl.BlockSpec(memory_space=pltpu.SMEM)] + [pl.BlockSpec(memory_space=pl.ANY)] * 12,
        out_specs=[pl.BlockSpec((1,) + shape, lambda t: (t, 0, 0)) for shape in shapes],
        out_shape=[outside((4,) + shape, jnp.bfloat16) for shape in shapes],
        scratch_shapes=[
            pltpu.VMEM((4, 46, 16, 768), jnp.bfloat16),
            pltpu.VMEM((2, 768, 128), jnp.float32),
            pltpu.VMEM((144, 768), jnp.float32),
            pltpu.SemaphoreType.DMA((4, 4)),
        ],
        compiler_params=pltpu.CompilerParams(vmem_limit_bytes=20 << 20),
        cost_estimate=COST,
        name="unpack",
    )(table, *kept_out(*sources))


def gelu_parts(value):
    below = 0.5 + 0.5 * lax.erf(value * 0.5**0.5)
    decay = jnp.exp(value * value * -0.5)
    return value * below, below + value * decay * 0.3989422804014327


def normed_rows(value):
    mean = jnp.mean(value, -1, keepdims=True)
    centred = value - mean
    scale = lax.rsqrt(jnp.mean(centred * centred, -1, keepdims=True) + 1e-5)
    return centred * scale, scale


def norm_pull(incoming, normed, scale, gain):
    scaled = incoming * gain
    return scale * (
        scaled
        - jnp.mean(scaled, -1, keepdims=True)
        - normed * jnp.mean(scaled * normed, -1, keepdims=True)
    )


def column_sums(target_ref, *values):
    for row, value in enumerate(values):
        target_ref[row : row + 1] = jnp.sum(value, 0, keepdims=True)


def each_piece(act, table_ref, sources, matrix, part, target_ref, seams_ref, semaphores):
    index = matrix[2]
    for window, first, count, at in matrix[0]:
        target = target_ref.at[part, pl.ds(at, count)]
        act(table_ref, sources, part, window, first, count, target, semaphores.at[part, index])
        index += 1
    for number, (window, _) in enumerate(matrix[1]):
        target = seams_ref.at[part, pl.ds(matrix[3] + number, 1)]
        act(table_ref, sources, part, window, 0, 1, target, semaphores.at[part, index])
        index += 1


OUT_MATRIX = (OUT_PIECES, OUT_SEAMS, 0, 0)
UP_MATRIX = (UP_PIECES, UP_SEAMS, 3, 1)
DOWN_MATRIX = (DOWN_PIECES, DOWN_SEAMS, 9, 4)


def started(*args):
    def begin(part, carry):
        each_piece(start_piece, *args[:3], part, *args[3:])
        return carry

    lax.fori_loop(0, 4, begin, 0)


def awaited(table_ref, pieces_refs, matrix, part, target_ref, seams_ref, semaphores):
    each_piece(wait_piece, table_ref, pieces_refs, matrix, part, target_ref, seams_ref, semaphores)
    for number, (_, at) in enumerate(matrix[1]):
        target_ref[part, at] = target_ref[part, at] + seams_ref[part, matrix[3] + number]


def bring_parts(table_ref, pieces_refs, matrices, part, seams_ref, semaphores):
    @pl.when(part < 3)
    def ahead():
        for matrix, target_ref in matrices:
            each_piece(
                start_piece,
                table_ref,
                pieces_refs,
                matrix,
                part + 1,
                target_ref,
                seams_ref,
                semaphores,
            )

    for matrix, target_ref in matrices:
        awaited(table_ref, pieces_refs, matrix, part, target_ref, seams_ref, semaphores)


def forward_kernel(*refs):
    table_ref, pieces_refs, refs = refs[0], refs[1:17], refs[17:]
    inputs, outputs, scratch = refs[:18], refs[18:37], refs[37:]
    out_ref = outputs[18]
    out_scratch, up_scratch, down_scratch, seams_ref, semaphores = scratch[6:]
    part = pl.program_id(0)
    matrices = ((UP_MATRIX, up_scratch), (DOWN_MATRIX, down_scratch))

    @pl.when(part == 0)
    def begin():
        started(table_ref, pieces_refs, OUT_MATRIX, out_scratch, seams_ref, semaphores)
        for matrix, target_ref in matrices:
            each_piece(
                start_piece, table_ref, pieces_refs, matrix, 0, target_ref, seams_ref, semaphores
            )
        out_scratch[:, 12:16] = jnp.zeros((4, 4, 16, 768), jnp.bfloat16)
        for number in range(4):
            awaited(table_ref, pieces_refs, OUT_MATRIX, number, out_scratch, seams_ref, semaphores)
        out_ref[...] = out_scratch[...].reshape(4, 256, 768)

    bring_parts(table_ref, pieces_refs, matrices, part, seams_ref, semaphores)
    for stream in range(2):
        act_ref, context_ref, own_out_ref, own_up_ref, up_bias_ref, own_down_ref, rows_ref, cotangent_ref, _ = inputs[
            9 * stream : 9 * stream + 9
        ]
        (
            mid_low_ref,
            normed_ref,
            scale_ref,
            hidden_ref,
            slope_ref,
            final_ref,
            pre_ref,
            pre_low_ref,
            sums_ref,
        ) = outputs[9 * stream : 9 * stream + 9]
        mid_ref, total_ref, low_ref = scratch[3 * stream : 3 * stream + 3]

        @pl.when(part == 0)
        def attention_out():
            weights = out_ref if stream == 0 else own_out_ref
            attn = sum(dot(context_ref[number], weights[number], NN) for number in range(4))
            normed, scale = normed_rows(attn + rows_ref[2:3] + act_ref[...])
            mid = normed * rows_ref[3:4] + rows_ref[4:5]
            normed_ref[...] = normed
            scale_ref[...] = scale
            mid_ref[...] = mid
            low_ref[...] = mid.astype(jnp.bfloat16)
            mid_low_ref[...] = low_ref[...]

        if stream == 0:
            up, down = up_scratch[part].reshape(768, 768), down_scratch[part].reshape(768, 768)
        else:
            up, down = own_up_ref[0], own_down_ref[0]
        hidden, slope = gelu_parts(dot(low_ref[...], up, NN) + up_bias_ref[0])
        hidden = hidden.astype(jnp.bfloat16)
        hidden_ref[0] = hidden
        slope_ref[0] = slope.astype(jnp.bfloat16)
        product = dot(hidden, down, NN)

        @pl.when(part == 0)
        def first():
            total_ref[...] = product

        @pl.when(part > 0)
        def later():
            total_ref[...] = total_ref[...] + product

        @pl.when(part == 3)
        def last():
            gain = rows_ref[6:7]
            normed, scale = normed_rows(total_ref[...] + rows_ref[5:6] + mid_ref[...])
            final_ref[0] = (normed * gain + rows_ref[7:8]).astype(jnp.bfloat16)
            incoming = cotangent_ref[0].astype(jnp.float32)
            pre = norm_pull(incoming, normed, scale, gain)
            pre_ref[...] = pre
            pre_low_ref[...] = pre.astype(jnp.bfloat16)
            column_sums(sums_ref, pre, incoming * normed, incoming)


def backward_kernel(*refs):
    table_ref, pieces_refs, refs = refs[0], refs[1:17], refs[17:]
    inputs, outputs, scratch = refs[:18], refs[18:30], refs[30:]
    up_scratch, down_scratch, seams_ref, semaphores = scratch[2:]
    part = pl.program_id(0)
    matrices = ((DOWN_MATRIX, down_scratch), (UP_MATRIX, up_scratch))

    @pl.when(part == 0)
    def begin():
        for matrix, target_ref in matrices:
            each_piece(
                start_piece, table_ref, pieces_refs, matrix, 0, target_ref, seams_ref, semaphores
            )

    bring_parts(table_ref, pieces_refs, matrices, part, seams_ref, semaphores)
    for stream in range(2):
        pre_ref, pre_low_ref, slope_ref, normed_ref, scale_ref, rows_ref, out_ref, own_down_ref, own_up_ref = inputs[
            9 * stream : 9 * stream + 9
        ]
        up_in_ref, up_sum_ref, attn_ref, attn_low_ref, sums_ref, context_grad_ref = outputs[
            6 * stream : 6 * stream + 6
        ]
        total_ref = scratch[stream]
        if stream == 0:
            up, down = up_scratch[part].reshape(768, 768), down_scratch[part].reshape(768, 768)
        else:
            up, down = own_up_ref[0], own_down_ref[0]
        up_in = dot(pre_low_ref[...], down, NT) * slope_ref[0].astype(jnp.float32)
        up_in = up_in.astype(jnp.bfloat16)
        up_in_ref[0] = up_in
        up_sum_ref[0] = jnp.sum(up_in.astype(jnp.float32), 0, keepdims=True)
        back = dot(up_in, up, NT)

        @pl.when(part == 0)
        def first():
            total_ref[...] = back

        @pl.when(part > 0)
        def later():
            total_ref[...] = total_ref[...] + back

        @pl.when(part == 3)
        def last():
            incoming = total_ref[...] + pre_ref[...]
            normed = normed_ref[...]
            attn = norm_pull(incoming, normed, scale_ref[...], rows_ref[3:4])
            attn_low = attn.astype(jnp.bfloat16)
            attn_ref[...] = attn
            attn_low_ref[...] = attn_low
            column_sums(sums_ref, attn, incoming * normed, incoming)
            for number in range(4):
                context_grad_ref[number] = dot(attn_low, out_ref[number], NT).astype(jnp.bfloat16)


def whole(*shape):
    return pl.BlockSpec(shape, lambda t: (0,) * len(shape), pipeline_mode=pl.Buffered(1))


def result(*shape):
    return pl.BlockSpec(shape, lambda t: (0,) * len(shape))


def by_part(*shape):
    return pl.BlockSpec((1,) + shape, lambda t: (t,) + (0,) * len(shape))


PIECES_SPECS = [pl.BlockSpec(memory_space=pltpu.SMEM)] + [
    pl.BlockSpec(memory_space=pl.ANY)
] * 16


def feed_forward(table, pieces, text, layout):
    positions = text[0].shape[0]
    small = jnp.zeros((8, 128), jnp.float32)
    in_specs, operands, out_specs, out_shape, scratch = [], [], [], [], []
    for number, stream in enumerate((text, layout)):
        act, context, out, up, up_bias, down, rows, cotangent = stream
        width, hidden = act.shape[1], up_bias.shape[2]
        matrices = (out, up, down)
        specs = (whole(4, 256, width), by_part(width, hidden), by_part(hidden, width))
        if number == 0:
            matrices, specs = (small,) * 3, (whole(8, 128),) * 3
        in_specs += [
            whole(positions, width),
            whole(4, positions, 256),
            specs[0],
            specs[1],
            by_part(1, hidden),
            specs[2],
            whole(8, width),
            whole(1, positions, width),
            whole(8, 128),
        ]
        operands += [act, context, matrices[0], matrices[1], up_bias, matrices[2], rows, cotangent, small]
        out_specs += [
            result(positions, width),
            result(positions, width),
            result(positions, 1),
            by_part(positions, hidden),
            by_part(positions, hidden),
            result(1, positions, width),
            result(positions, width),
            result(positions, width),
            result(8, width),
        ]
        out_shape += [
            outside((positions, width), jnp.bfloat16),
            outside((positions, width), jnp.float32),
            outside((positions, 1), jnp.float32),
            outside((4, positions, hidden), jnp.bfloat16),
            outside((4, positions, hidden), jnp.bfloat16),
            outside((1, positions, width), jnp.bfloat16),
            outside((positions, width), jnp.float32),
            outside((positions, width), jnp.bfloat16),
            outside((8, width), jnp.float32),
        ]
        scratch += [
            pltpu.VMEM((positions, width), jnp.float32),
            pltpu.VMEM((positions, width), jnp.float32),
            pltpu.VMEM((positions, width), jnp.bfloat16),
        ]
    results = pl.pallas_call(
        forward_kernel,
        grid=(4,),
        in_specs=PIECES_SPECS + in_specs,
        out_specs=out_specs + [result(4, 256, 768)],
        out_shape=out_shape + [outside((4, 256, 768), jnp.bfloat16)],
        scratch_shapes=scratch
        + [
            pltpu.VMEM((4, 16, 16, 768), jnp.bfloat16),
            pltpu.VMEM((4, 48, 16, 768), jnp.bfloat16),
            pltpu.VMEM((4, 48, 16, 768), jnp.bfloat16),
            pltpu.VMEM((4, 6, 16, 768), jnp.bfloat16),
            pltpu.SemaphoreType.DMA((4, 14)),
        ],
        compiler_params=pltpu.CompilerParams(vmem_limit_bytes=56 << 20),
        cost_estimate=COST,
        name="feed_forward",
    )(table, *kept_out(*pieces), *kept_out(*operands))
    return results[:9], results[9:18], results[18]


def feed_back(table, pieces, text, layout):
    positions = text[0].shape[0]
    small = jnp.zeros((8, 128), jnp.float32)
    in_specs, operands, out_specs, out_shape, scratch = [], [], [], [], []
    for number, stream in enumerate((text, layout)):
        pre, pre_low, slope, normed, scale, rows, out, down, up = stream
        width, hidden = pre.shape[1], slope.shape[2]
        matrices, specs = (down, up), (by_part(hidden, width), by_part(width, hidden))
        if number == 0:
            matrices, specs = (small,) * 2, (whole(8, 128),) * 2
        in_specs += [
            whole(positions, width),
            whole(positions, width),
            by_part(positions, hidden),
            whole(positions, width),
            whole(positions, 1),
            whole(8, width),
            whole(4, 256, width),
            specs[0],
            specs[1],
        ]
        operands += [pre, pre_low, slope, normed, scale, rows, out, *matrices]
        out_specs += [
            by_part(positions, hidden),
            by_part(1, hidden),
            result(positions, width),
            result(positions, width),
            result(8, width),
            result(4, positions, 256),
        ]
        out_shape += [
            outside((4, positions, hidden), jnp.bfloat16),
            outside((4, 1, hidden), jnp.float32),
            outside((positions, width), jnp.float32),
            outside((positions, width), jnp.bfloat16),
            outside((8, width), jnp.float32),
            outside((4, positions, 256), jnp.bfloat16),
        ]
        scratch.append(pltpu.VMEM((positions, width), jnp.float32))
    results = pl.pallas_call(
        backward_kernel,
        grid=(4,),
        in_specs=PIECES_SPECS + in_specs,
        out_specs=out_specs,
        out_shape=out_shape,
        scratch_shapes=scratch
        + [
            pltpu.VMEM((4, 48, 16, 768), jnp.bfloat16),
            pltpu.VMEM((4, 48, 16, 768), jnp.bfloat16),
            pltpu.VMEM((4, 6, 16, 768), jnp.bfloat16),
            pltpu.SemaphoreType.DMA((4, 14)),
        ],
        compiler_params=pltpu.CompilerParams(vmem_limit_bytes=56 << 20),
        cost_estimate=COST,
        name="feed_back",
    )(table, *kept_out(*pieces), *kept_out(*operands))
    return results[:6], results[6:]


def sum_kernel(counts, table_ref, *refs):
    total = len(counts)
    sources, out_ref = refs[:total], refs[total]
    buffers, semaphores = refs[total + 1 : -1], refs[-1]
    entries = out_ref.shape[0]

    def copies(entry):
        found = []
        for number, (source, buffer) in enumerate(zip(sources, buffers)):
            at = 0
            for piece, count in enumerate(counts[number]):
                part, first = (table_ref[number, entry, piece, item] for item in range(2))
                found.append(
                    pltpu.make_async_copy(
                        source.at[part, pl.ds(first, count)],
                        buffer.at[entry, pl.ds(at, count)],
                        semaphores.at[number, entry, piece],
                    )
                )
                at += count
        return found

    pending = [copies(entry) for entry in range(entries)]
    for copy in sum(pending, []):
        copy.start()
    for entry in range(entries):
        for copy in pending[entry]:
            copy.wait()
        total_value = sum(buffer[entry].astype(jnp.float32) for buffer in buffers)
        out_ref[entry] = total_value.astype(jnp.bfloat16)


def sum_windows(*sources):
    entries = len(sources[0][1])
    counts = tuple(tuple(count for _, _, count in places[0]) for _, places in sources)
    widest = max(len(item) for item in counts)
    length = sum(counts[0])
    rows = []
    for _, places in sources:
        for entry in places:
            for index, first, _ in entry + [(0, 0, 0)] * (widest - len(entry)):
                rows += [jnp.asarray(index, jnp.int32), jnp.asarray(first, jnp.int32)]
    table = jnp.stack(rows).reshape(len(sources), entries, widest, 2)
    shape = (entries, length, 16, 768)
    size = entries * length * 16 * 768 * 2
    return pl.pallas_call(
        lambda *refs: sum_kernel(counts, *refs),
        in_specs=[pl.BlockSpec(memory_space=pltpu.SMEM)]
        + [pl.BlockSpec(memory_space=pl.ANY)] * len(sources),
        out_specs=pl.BlockSpec(memory_space=pltpu.VMEM),
        out_shape=outside(shape, jnp.bfloat16),
        scratch_shapes=[pltpu.VMEM(shape, jnp.bfloat16)] * len(sources)
        + [pltpu.SemaphoreType.DMA((len(sources), entries, widest))],
        compiler_params=pltpu.CompilerParams(vmem_limit_bytes=24 << 20),
        cost_estimate=pl.CostEstimate(
            flops=size, transcendentals=0, bytes_accessed=size * (len(sources) + 1)
        ),
        name="sum_windows",
    )(table, *(pltpu.with_memory_space_constraint(array, pltpu.HBM) for array, _ in sources))


INNER_PIECES = ((2, 21, 20), (40, 59, 20))
OUTER_PIECES = ((78, 97, 17), (95, 0, 3))
LATE_PIECES = ((0, 19, 26),)


def exchange_pairs(flip):
    pairs = []
    for device in range(32):
        z, x, y, core = device // 8, device // 4 % 2, device // 2 % 2, device % 2
        z, x, y, core = flip(z, x, y, core)
        pairs.append((device, z * 8 + x * 4 + y * 2 + core))
    return pairs


ROUNDS = (
    exchange_pairs(lambda z, x, y, core: (z, x, y, 1 - core)),
    exchange_pairs(lambda z, x, y, core: (z, x, 1 - y, core) if core else (z, 1 - x, y, core)),
    exchange_pairs(lambda z, x, y, core: (z, 1 - x, y, core) if core else (z, x, 1 - y, core)),
    exchange_pairs(lambda z, x, y, core: (z ^ 1, x, y, core) if core else (z ^ 2, x, y, core)),
    exchange_pairs(lambda z, x, y, core: (z ^ 2, x, y, core) if core else (z ^ 1, x, y, core)),
)


def last_pairs(*lists):
    return [
        (z * 8 + rest * 2 + core, to * 8 + rest * 2 + core)
        for core, pairs in enumerate(lists)
        for z, to in pairs
        for rest in range(4)
    ]


INWARD = last_pairs(((0, 1), (3, 2)), ((0, 2), (3, 1)))
OUTWARD = last_pairs(((1, 0), (2, 3)), ((2, 0), (1, 3)))


def swap(value, step):
    return lax.ppermute(value, ("dp", "tensor"), ROUNDS[step])


def after(value, *others):
    return lax.optimization_barrier((value, others))[0]


def picked(value, index, axis):
    return lax.dynamic_index_in_dim(value, index, axis, keepdims=False)


def total_low(*values):
    return sum(value.astype(jnp.float32) for value in values).astype(jnp.bfloat16)


def tiled(value):
    return value.reshape(2, -1, 16, UNIT)


def window_places(pieces, place, entry, other):
    z, x, y, core = place
    own_x, own_y = (1 - x, 1 - y) if other else (x, y)
    part = jnp.where(core == 0, entry, own_y)
    across = jnp.where(core == 0, own_x, entry)
    return [(part, jnp.where(across == 0, first, second), n) for first, second, n in pieces]


def first_sent(kept, received, pieces, place):
    places = [window_places(pieces, place, entry, True) for entry in range(2)]
    return sum_windows((tiled(kept), places), (tiled(received), places))


def second_sources(kept, received, second, pieces, place, own):
    z, x, y, core = place
    entry = jnp.where(core == 0, y, x)
    entry = entry if own else 1 - entry
    places = [window_places(pieces, place, entry, False)]
    return [
        (tiled(kept), places),
        (tiled(received), places),
        (second, [[(entry, 0, second.shape[1])]]),
    ]


def third_source(third):
    return (third[None], [[(0, 0, third.shape[0])]])


def inner_sources(kept, received, second, third, place, block):
    z, x, y, core = place
    entry = jnp.where(core == 0, y, x)
    part = jnp.where(core == 0, entry, y)
    across = jnp.where(core == 0, x, entry)
    (a, b, count), (c, d, _) = INNER_PIECES
    at = jnp.where(across == 0, jnp.where(block == 0, a, c), jnp.where(block == 0, b, d))
    places = [[(part, at, count)]]
    return [
        (tiled(kept), places),
        (tiled(received), places),
        (second, [[(entry, count * block, count)]]),
        (third[None], [[(0, count * block, count)]]),
    ]


def late_sides(value, place):
    z, x, y, core = place
    upper = jnp.where(core == 0, z // 2, z % 2)
    sent = lax.dynamic_slice_in_dim(value, 6 * (1 - upper), TILES)
    return sent, lax.dynamic_slice_in_dim(value, 6 * upper, TILES)


def along_z(value, pairs):
    return lax.ppermute(value, ("dp", "tensor"), pairs)


def gather_pieces(frame, place, prepared):
    z, x, y, core = place
    own = frame.reshape(TILES, 16, UNIT)

    def paired(value):
        return jnp.stack((value, swap(value, 1)))

    near = swap(own, 4)
    pairs = [paired(own)]
    outer = (z == 0) | (z == 3)
    far = swap(after(jnp.where(outer, own, near), pairs[0]), 3)
    rests = [swap(pairs[0], 2)]
    pairs.append(paired(near))
    last = swap(after(jnp.where(outer, near, own), far), 3)
    rests.append(swap(pairs[1], 2))
    pairs.append(paired(after(far, pairs[1], rests[0])))
    prepared = lax.optimization_barrier(prepared)
    rests.append(swap(after(pairs[2], prepared), 2))
    pairs.append(paired(after(last, pairs[2], rests[1])))
    pieces = []
    for step in range(3):
        pieces += [pairs[step], rests[step], swap(pairs[step], 0), swap(rests[step], 0)]
    rest = swap(pairs[3], 2)
    part = jnp.arange(32) // 8
    window = jnp.arange(32) % 8
    its_z, its_x, its_y, its_core = window // 2, window % 2, part // 2, part % 2
    off_x, off_y = its_x != x, its_y != y
    beside = jnp.where(its_core == 0, z ^ 1, z ^ 2)
    far_step = jnp.where((its_z == 0) | (its_z == 3), 2, 3)
    step = jnp.where(its_z == z, 0, jnp.where(its_z == beside, 1, far_step))
    which = 4 * step + 2 * (its_core != core) + jnp.where(its_core == 0, off_y, off_x)
    slot = jnp.where(its_core == 0, off_x, off_y)
    table = jnp.stack((which, slot)).astype(jnp.int32)
    return table, pieces, (pairs[3], rest), prepared


def rearranged(stack):
    def matrix(first, count, height):
        return stack[:, first : first + count].reshape(4, height, -1)

    gap = jnp.zeros((4, 768, 64), stack.dtype)
    heads = []
    for slot in range(3):
        heads += [matrix(192 * slot, 192, 768), gap]
    small = []
    for slot in range(3):
        columns = matrix(2304 + 12 * slot, 12, 192)
        small.append(spaced(columns.reshape(768, 48)).reshape(4, 192, 256))
    rows = matrix(2340, 12, 48).transpose(0, 2, 1)
    return (
        jnp.concatenate(heads, 2),
        jnp.concatenate(small, 2),
        spaced(rows.reshape(768, 48)).reshape(4, 192, 256).transpose(0, 2, 1),
        matrix(2352, 48, 192),
        matrix(2400, 48, 192),
    )


def stack_pieces(stack):
    frames = jnp.stack([stack[:, 304 * window : 304 * window + FRAME] for window in range(8)], 1)
    seam = (jnp.arange(FRAME)[:, None] >= 304) & (jnp.arange(8) < 7)[:, None, None]
    frames = jnp.where(seam, 0.0, frames).astype(stack.dtype).reshape(32, TILES, 16, UNIT)
    number = jnp.arange(32)
    return jnp.stack((number // 2, number % 2)).astype(jnp.int32), list(
        frames.reshape(16, 2, TILES, 16, UNIT)
    )


def spaced(vector):
    gap = jnp.zeros((vector.shape[0], 48), vector.dtype)
    first, second, third = vector[:, 0:16], vector[:, 16:32], vector[:, 32:48]
    return jnp.concatenate((second, gap, first, gap, gap, gap[:, :16], third, gap), 1)


def unspaced(value):
    return jnp.concatenate((value[:, 64:80], value[:, 0:16], value[:, 192:208]), 1).reshape(-1)


def shards(
    text_in,
    layout_in,
    lengths,
    text_mask,
    box_mask,
    text_cot,
    layout_cot,
    master,
    first_moment,
    second_moment,
    ema_weights,
    vectors,
    vector_first,
    vector_second,
    vector_ema,
):
    parts = lax.axis_size("tensor")
    dp_count = lax.axis_size("dp")
    tensor_index = lax.axis_index("tensor")
    dp_index = lax.axis_index("dp")
    span = master.shape[2]
    near = dp_count == 8 and parts == 4
    place = (dp_index // 2, dp_index % 2, tensor_index // 2, tensor_index % 2)
    shift = (2 * dp_index).reshape(1)
    all_parts = jnp.arange(parts, dtype=jnp.int32)
    own_parts = all_parts[::2] + place[3]
    other_parts = all_parts[::2] + 1 - place[3]
    biases = split_vector(vectors)
    length = lax.dynamic_slice_in_dim(lengths, tensor_index, 1)

    def product(spec, left, right):
        return jnp.einsum(spec, left, right, preferred_element_type=jnp.float32)

    def over_parts(spec, left, right):
        return sum(product(spec, left[part], right[part]) for part in range(parts))

    def summed(value):
        return jnp.sum(value, 0, dtype=jnp.float32)

    gap = jnp.zeros((parts, 64), jnp.float32)
    none = jnp.zeros((parts, 256), jnp.float32)
    qkv_bias = jnp.concatenate(
        (biases[0].reshape(parts, 192), gap, none, biases[1].reshape(parts, 192), gap), 1
    )
    lqkv_bias = jnp.concatenate(
        (spaced(biases[9].reshape(parts, 48)), none, spaced(biases[10].reshape(parts, 48))), 1
    )
    text_flag = (text_mask[0] > 0)[:, None]
    box_flag = (box_mask[0] > 0)[:, None]
    text_act = jnp.where(text_flag, biases[18], text_in[0].astype(jnp.float32))
    layout_act = jnp.where(box_flag, biases[19], layout_in[0].astype(jnp.float32))
    text_low = text_act.astype(jnp.bfloat16)
    layout_low = layout_act.astype(jnp.bfloat16)
    text_rows, layout_rows = vectors[:6144].reshape(8, D), vectors[9216:10752].reshape(8, L)
    up_bias, lup_bias = biases[8].reshape(parts, 1, -1), biases[17].reshape(parts, 1, -1)
    prepared = (
        length,
        qkv_bias,
        lqkv_bias,
        text_act,
        layout_act,
        text_low,
        layout_low,
        text_rows,
        layout_rows,
        up_bias,
        lup_bias,
        layout_cot,
    )
    if near:
        table, outer, inner, prepared = gather_pieces(
            cast_frame(shift, master), place, prepared
        )
        qkv_weight, lqkv_weight, lout_weight, lup_weight, ldown_weight = unpack(table, outer)
    else:
        wire = master.reshape(-1, 192).astype(jnp.bfloat16)
        stack = lax.all_gather(wire[None], ("tensor", "dp"), axis=0, tiled=True)
        stack = stack.reshape(parts, -1, UNIT)
        qkv_weight, lqkv_weight, lout_weight, lup_weight, ldown_weight = rearranged(stack)
        table, pieces = stack_pieces(stack)
    (
        length,
        qkv_bias,
        lqkv_bias,
        text_act,
        layout_act,
        text_low,
        layout_low,
        text_rows,
        layout_rows,
        up_bias,
        lup_bias,
        layout_cot,
    ) = prepared
    qkv = (product("sd,tde->tse", text_low, qkv_weight) + qkv_bias[:, None]).astype(jnp.bfloat16)
    lqkv = (product("sd,tde->tse", layout_low, lqkv_weight) + lqkv_bias[:, None]).astype(
        jnp.bfloat16
    )
    if near:
        pieces = outer + [*inner, swap(inner[0], 0), swap(after(inner[1], qkv), 0)]
    context, lcontext, log_total = attend(length, qkv, lqkv)
    text_ahead, layout_ahead, out_weight = feed_forward(
        table,
        pieces,
        (text_act, context, None, None, up_bias, None, text_rows, text_cot),
        (
            layout_act,
            lcontext,
            lout_weight,
            lup_weight,
            lup_bias,
            ldown_weight,
            layout_rows,
            layout_cot,
        ),
    )
    text_mid_low, text_normed, text_scale, text_hidden, text_slope, text_out = text_ahead[:6]
    text_pre, text_down_in, text_sums_two = text_ahead[6:]
    layout_mid_low, layout_normed, layout_scale, layout_hidden, layout_slope = layout_ahead[:5]
    layout_out, layout_pre, layout_down_in, layout_sums_two = layout_ahead[5:]
    text_behind, layout_behind = feed_back(
        table,
        pieces,
        (
            text_pre,
            text_down_in,
            text_slope,
            text_normed,
            text_scale,
            text_rows,
            out_weight,
            None,
            None,
        ),
        (
            layout_pre,
            layout_down_in,
            layout_slope,
            layout_normed,
            layout_scale,
            layout_rows,
            lout_weight,
            ldown_weight,
            lup_weight,
        ),
    )
    text_up_grad, text_up_sums, text_pre_one, text_attn_in, text_sums_one, context_grad = text_behind
    layout_up_grad, layout_up_sums, layout_pre_one = layout_behind[:3]
    layout_attn_in, layout_sums_one, lcontext_grad = layout_behind[3:]
    early_of = (text_mid_low, text_up_grad, text_hidden, text_down_in, context, text_attn_in)
    if near:
        early_sent = early_grads(other_parts, *early_of)
        early_received = swap(early_sent, 0)
        early_kept = early_grads(after(own_parts, early_sent), *early_of)
    else:
        early_all = early_grads(all_parts, *early_of)
    if near:
        early_received = after(early_received, early_kept)
        early = (early_kept, early_received)
        inner_sent = first_sent(*early, INNER_PIECES, place)
        inner_second = swap(inner_sent, 1)
        outer_sent = first_sent(*after(early, inner_sent), OUTER_PIECES, place)
        outer_second = swap(outer_sent, 1)
        context_grad = after(context_grad, outer_sent)
    qkv_in, lqkv_in = attend_back(
        length, qkv, lqkv, log_total, context, lcontext, context_grad, lcontext_grad
    )
    late_of = [
        text_low,
        qkv_in,
        layout_low,
        lqkv_in,
        lcontext,
        layout_attn_in,
        layout_mid_low,
        layout_up_grad,
        layout_hidden,
        layout_down_in,
    ]
    if near:
        late_sent = late_grads(other_parts, *late_of)
        late_received = swap(late_sent, 0)
        inner_second = after(inner_second, late_sent)
        inner_sent = sum_windows(*second_sources(*early, inner_second, INNER_PIECES, place, False))[0]
        inner_third = swap(inner_sent, 2)
        late_kept = late_grads(after(own_parts, inner_sent), *late_of)
        late = (late_kept, after(late_received, late_kept))
        late_sent = first_sent(*late, LATE_PIECES, place)
        late_second = swap(late_sent, 1)
        outer_second = after(outer_second, late_sent)
        outer_sent = sum_windows(*second_sources(*early, outer_second, OUTER_PIECES, place, False))[0]
        outer_third = swap(outer_sent, 2)
        high, low = place[0] // 2, place[0] % 2
        side = jnp.where(place[3] == 0, 1 - high, low)
        inner_third = after(inner_third, outer_sent)
        inner = (*early, inner_second, inner_third, place)
        inner_sent = sum_windows(*inner_sources(*inner, side))[0]
        inner_fourth = swap(inner_sent, 3)
        qkv_in = after(qkv_in, inner_sent)
        text_in_back = over_parts("se,de->sd", qkv_in, qkv_weight)
        outer_third = after(outer_third, text_in_back)
        outer_sum = sum_windows(
            *second_sources(*early, outer_second, OUTER_PIECES, place, True), third_source(outer_third)
        )[0]
        outer_fourth = swap(outer_sum, 3)
        late_second = after(late_second, outer_sum)
        late_sent = sum_windows(*second_sources(*late, late_second, LATE_PIECES, place, False))[0]
        late_third = swap(late_sent, 2)
        text_in_back, lqkv_in = after((text_in_back, lqkv_in), late_sent)
    else:
        late_all = late_grads(all_parts, *late_of)
        text_in_back = over_parts("se,de->sd", qkv_in, qkv_weight)
    text_full = text_pre_one + text_in_back
    layout_full = layout_pre_one + over_parts("se,de->sd", lqkv_in, lqkv_weight)
    text_in_grad = jnp.where(text_flag, 0.0, text_full)
    layout_in_grad = jnp.where(box_flag, 0.0, layout_full)
    text_embed_grad = summed(jnp.where(text_flag, text_full, 0.0))
    layout_embed_grad = summed(jnp.where(box_flag, layout_full, 0.0))
    qkv_sums = jnp.sum(qkv_in, 1, dtype=jnp.float32)
    lqkv_sums = jnp.sum(lqkv_in, 1, dtype=jnp.float32)
    vector_part = jnp.concatenate(
        [
            qkv_sums[:, 0:192].reshape(-1),
            qkv_sums[:, 512:704].reshape(-1),
            text_sums_one[:3].reshape(-1),
            text_sums_two[:3].reshape(-1),
            text_up_sums.reshape(-1),
            unspaced(lqkv_sums[:, 0:256]),
            unspaced(lqkv_sums[:, 512:768]),
            layout_sums_one[:3].reshape(-1),
            layout_sums_two[:3].reshape(-1),
            layout_up_sums.reshape(-1),
            text_embed_grad,
            layout_embed_grad,
        ]
    )
    if near:
        slices = vector_part.reshape(32, -1)
        vector_slice = summed(lax.all_to_all(slices, ("dp", "tensor"), 0, 0, tiled=True))
        inner_fourth = after(inner_fourth, vector_part)
        inner_kept = sum_windows(*inner_sources(*inner, 1 - side), third_source(inner_fourth))[0]
        inner_last = along_z(inner_kept, INWARD)
        late_third = after(late_third, inner_kept)
        late_sum = sum_windows(
            *second_sources(*late, late_second, LATE_PIECES, place, True), third_source(late_third)
        )[0]
        late_sent, late_kept = late_sides(late_sum, place)
        late_fourth = swap(late_sent, 3)
        outer_kept = total_low(outer_sum, after(outer_fourth, late_sent))
        outer_last = along_z(outer_kept, OUTWARD)
        late_kept = total_low(late_kept, after(late_fourth, outer_kept, vector_slice))
        late_last = along_z(late_kept, OUTWARD)
        span_grad, shared = finish(
            jnp.stack((2 * dp_index, dp_index)),
            jnp.pad(vector_slice, (0, 512 - vector_slice.shape[0])).reshape(1, 512),
            *(
                item.reshape(FRAME, UNIT)
                for item in (inner_kept, inner_last, outer_kept, outer_last, late_kept, late_last)
            ),
        )
        shared = lax.all_to_all(shared, ("dp", "tensor"), 0, 0, tiled=True)
        vector_grad = shared[:, : vector_slice.shape[0]].reshape(-1)
        matrix_square = jnp.sum(shared[:, 512:])
    else:
        flat_grad = jnp.concatenate(
            (late_all[:, :576], early_all[:, :1728], late_all[:, 576:]), 1
        ).reshape(parts * dp_count, -1, 192)
        span_grad = lax.psum_scatter(flat_grad, ("tensor", "dp"), scatter_dimension=0, tiled=True)
        span_grad = span_grad.astype(jnp.float32).reshape(master.shape)
        vector_grad = lax.psum(vector_part, ("dp", "tensor"))
        matrix_square = lax.psum(jnp.sum(span_grad * span_grad), ("dp", "tensor"))
    grad_norm = jnp.sqrt(matrix_square + jnp.sum(vector_grad * vector_grad))
    factor = clip_bound / jnp.maximum(grad_norm, clip_bound)
    if near:
        matrix_new = adam(
            (dp_index * span).reshape(1),
            shared,
            master,
            span_grad,
            first_moment,
            second_moment,
            ema_weights,
        )
        matrix_new = tuple(matrix_new)
    else:
        rates = lax.dynamic_slice_in_dim(rate_table(parts), dp_index * span, span)
        matrix_new = adam_update(
            master,
            span_grad,
            first_moment,
            second_moment,
            ema_weights,
            rates.reshape(master.shape),
            factor,
        )
    vector_new = adam_update(
        vectors, vector_grad, vector_first, vector_second, vector_ema, vector_rate, factor
    )
    return (
        (
            text_out,
            layout_out,
            text_in_grad[None],
            layout_in_grad[None],
            grad_norm,
        )
        + matrix_new
        + vector_new
    )


def solution(mesh):
    in_specs = (
        P(("dp", "tensor"), None, None),
        P(("dp", "tensor"), None, None),
        P("dp"),
        P(("dp", "tensor"), None),
        P(("dp", "tensor"), None),
        P(("dp", "tensor"), None, None),
        P(("dp", "tensor"), None, None),
        P("tensor", "dp", None),
        P("tensor", "dp", None),
        P("tensor", "dp", None),
        P("tensor", "dp", None),
        P(),
        P(),
        P(),
        P(),
    )
    out_specs = (
        P(("dp", "tensor"), None, None),
        P(("dp", "tensor"), None, None),
        P(("dp", "tensor"), None, None),
        P(("dp", "tensor"), None, None),
        P(),
        P("tensor", "dp", None),
        P("tensor", "dp", None),
        P("tensor", "dp", None),
        P("tensor", "dp", None),
        P("tensor", "dp", None),
        P(),
        P(),
        P(),
        P(),
        P(),
    )
    return jax.shard_map(shards, mesh=mesh, in_specs=in_specs, out_specs=out_specs, check_vma=False)
```

```python
from functools import partial
import math

import jax
import jax.numpy as jnp
from jax import lax
from jax.experimental import pallas as pl
from jax.experimental.pallas import tpu as pltpu
from jax.sharding import PartitionSpec as P

D = 768
HT = 64
FF = 3072
L = 192
HL = 16
LF = 768
STEP = 5


norm_eps = 1e-05
clip_bound = 1.0
first_decay = 0.5
second_decay = 0.6
adam_floor = 1e-08
weight_decay = 0.01
vector_rate = 0.5
average_keep = 0.5
masked_score = -1e30


def piece_table(parts):
    text_spread = 1.0 / math.sqrt(D)
    layout_spread = 1.0 / math.sqrt(L)
    return [
        (D, D // parts, text_spread),
        (D, D // parts, text_spread),
        (D, D // parts, text_spread),
        (D // parts, D, 8.0 * text_spread),
        (D, FF // parts, text_spread),
        (FF // parts, D, 1.0 / math.sqrt(FF)),
        (L, L // parts, layout_spread),
        (L, L // parts, layout_spread),
        (L, L // parts, layout_spread),
        (L // parts, L, 8.0 * layout_spread),
        (L, LF // parts, layout_spread),
        (LF // parts, L, 1.0 / math.sqrt(LF)),
    ]


def rate_table(parts):
    return jnp.concatenate(
        [
            jnp.full((height * width,), spread, jnp.float32)
            for height, width, spread in piece_table(parts)
        ]
    )


def split_vector(flat):
    pieces = []
    start = 0
    for width in [D] * 8 + [FF] + [L] * 8 + [LF] + [D, L]:
        pieces.append(flat[start : start + width])
        start = start + width
    return pieces


def project(acts, weight):
    return jnp.einsum("psd,de->pse", acts, weight, preferred_element_type=jnp.float32)


def project_back(incoming, weight):
    return jnp.einsum("pse,de->psd", incoming, weight, preferred_element_type=jnp.float32)


def weight_grad(acts, incoming):
    return jnp.einsum("psd,pse->de", acts, incoming, preferred_element_type=jnp.float32)


def norm_forward(value, gain, shift):
    mean = jnp.mean(value, -1, keepdims=True)
    centred = value - mean
    scale = lax.rsqrt(jnp.mean(centred * centred, -1, keepdims=True) + norm_eps)
    normed = centred * scale
    return (normed * gain + shift, normed, scale)


def norm_backward(incoming, normed, scale, gain):
    scaled = incoming * gain
    result = scale * (
        scaled
        - jnp.mean(scaled, -1, keepdims=True)
        - normed * jnp.mean(scaled * normed, -1, keepdims=True)
    )
    return (result, jnp.sum(incoming * normed, (0, 1)), jnp.sum(incoming, (0, 1)))


def gelu_back(value, incoming):
    unused, pull = jax.vjp(partial(jax.nn.gelu, approximate=False), value)
    return pull(incoming)[0]


def adam_update(weight, gradient, first, second, average, rate, factor):
    clipped = gradient * factor
    new_first = first_decay * first + (1.0 - first_decay) * clipped
    new_second = second_decay * second + (1.0 - second_decay) * clipped * clipped
    first_hat = new_first / (1.0 - first_decay**STEP)
    second_hat = new_second / (1.0 - second_decay**STEP)
    updated = weight - rate * (
        first_hat / (jnp.sqrt(second_hat) + adam_floor) + weight_decay * weight
    )
    return (
        updated,
        new_first,
        new_second,
        updated.astype(jnp.bfloat16),
        average_keep * average + (1.0 - average_keep) * updated,
    )


COST = pl.CostEstimate(flops=5 << 30, transcendentals=0, bytes_accessed=10 << 20)
NT = (((1,), (1,)), ((), ()))
NN = (((1,), (0,)), ((), ()))
TN = (((0,), (0,)), ((), ()))


def dot(left, right, dims):
    return lax.dot_general(left, right, dims, preferred_element_type=jnp.float32)


def kept_out(*values):
    return [pltpu.with_memory_space_constraint(value, pltpu.HBM) for value in values]


def outside(shape, dtype):
    return pltpu.HBM(shape, dtype)


def lane_of(shape):
    return lax.broadcasted_iota(jnp.int32, shape, len(shape) - 1)


def head_tiles(text_ref, layout_ref, slot, tile, high):
    first = slot * 256 + tile * 128
    text = text_ref[0, :, first : first + 128]
    layout = layout_ref[0, :, first : first + 128]
    low = lane_of(text.shape) < 64
    if high:
        return jnp.where(low, layout, text)
    return jnp.where(low, text, layout)


def own_lanes(shape, high):
    low = lane_of(shape) < 64
    return ~low if high else low


def scaled_query(query, high):
    own = own_lanes(query.shape, high)
    marker = 16 if high else 80
    scale = jnp.where(own, 0.125, 0.25)
    scaled = (query.astype(jnp.float32) * scale).astype(jnp.bfloat16)
    return jnp.where(lane_of(query.shape) == marker, jnp.bfloat16(1.0), scaled)


def masked_key(key, high, length):
    marker = 16 if high else 80
    beyond = lax.broadcasted_iota(jnp.int32, key.shape, 0) >= length
    column = jnp.where(beyond, jnp.float32(-1e30), jnp.float32(0.0)).astype(jnp.bfloat16)
    return jnp.where(lane_of(key.shape) == marker, column, key)


def attend_kernel(
    length_ref,
    text_in_ref,
    layout_in_ref,
    text_weight_ref,
    layout_weight_ref,
    text_bias_ref,
    layout_bias_ref,
    text_ref,
    layout_ref,
    context_ref,
    layout_context_ref,
    total_ref,
):
    length = length_ref[0]
    for in_ref, weight_ref, bias_ref, result_ref in (
        (text_in_ref, text_weight_ref, text_bias_ref, text_ref),
        (layout_in_ref, layout_weight_ref, layout_bias_ref, layout_ref),
    ):
        heads = dot(in_ref[...], weight_ref[0], NN) + bias_ref[0]
        result_ref[0] = heads.astype(jnp.bfloat16)
    found = []
    for head in range(3):
        tile, high = head // 2, head % 2 == 1
        query = scaled_query(head_tiles(text_ref, layout_ref, 0, tile, high), high)
        key = masked_key(head_tiles(text_ref, layout_ref, 1, tile, high), high, length)
        value = head_tiles(text_ref, layout_ref, 2, tile, high)
        scores = dot(key, query, NT)
        top = jnp.max(scores, 0, keepdims=True)
        raised = jnp.exp(scores - top)
        total = jnp.sum(raised, 0, keepdims=True)
        probs = (raised * (1.0 / total)).astype(jnp.bfloat16)
        total_ref[0, head : head + 1, :] = top + jnp.log(total)
        context = dot(value, probs, TN)
        found.append(context.T)
    low = lane_of(found[0].shape) < 64
    zero = jnp.zeros_like(found[0])
    context_ref[0, :, 0:128] = jnp.where(low, found[0], found[1]).astype(jnp.bfloat16)
    context_ref[0, :, 128:256] = jnp.where(low, found[2], zero).astype(jnp.bfloat16)
    layout_context_ref[0, :, 0:128] = jnp.where(low, found[1], found[0]).astype(jnp.bfloat16)
    layout_context_ref[0, :, 128:256] = jnp.where(low, zero, found[2]).astype(jnp.bfloat16)


def block(rows, width):
    return pl.BlockSpec((1, rows, width), lambda t: (t, 0, 0))


def attend(length, text, layout, text_weight, layout_weight, text_bias, layout_bias):
    positions, parts = text.shape[0], text_weight.shape[0]
    return pl.pallas_call(
        attend_kernel,
        grid=(parts,),
        in_specs=[
            pl.BlockSpec(memory_space=pltpu.SMEM),
            pl.BlockSpec((positions, 768), lambda t: (0, 0)),
            pl.BlockSpec((positions, 192), lambda t: (0, 0)),
            block(768, 768),
            block(192, 768),
            block(1, 768),
            block(1, 768),
        ],
        out_specs=[
            block(positions, 768),
            block(positions, 768),
            block(positions, 256),
            block(positions, 256),
            block(8, positions),
        ],
        out_shape=[
            outside((parts, positions, 768), jnp.bfloat16),
            outside((parts, positions, 768), jnp.bfloat16),
            outside((parts, positions, 256), jnp.bfloat16),
            outside((parts, positions, 256), jnp.bfloat16),
            outside((parts, 8, positions), jnp.float32),
        ],
        compiler_params=pltpu.CompilerParams(vmem_limit_bytes=32 << 20),
        cost_estimate=COST,
        name="attend",
    )(length, *kept_out(text, layout, text_weight, layout_weight, text_bias, layout_bias))


def attend_back_kernel(
    length_ref,
    text_ref,
    layout_ref,
    total_ref,
    context_ref,
    layout_context_ref,
    context_grad_ref,
    layout_context_grad_ref,
    text_grad_ref,
    layout_grad_ref,
):
    length = length_ref[0]
    grads = ([], [], [])
    for head in range(3):
        tile, high = head // 2, head % 2 == 1
        raw_query = head_tiles(text_ref, layout_ref, 0, tile, high)
        raw_key = head_tiles(text_ref, layout_ref, 1, tile, high)
        value = head_tiles(text_ref, layout_ref, 2, tile, high)
        incoming = head_tiles(context_grad_ref, layout_context_grad_ref, 0, tile, high)
        context = head_tiles(context_ref, layout_context_ref, 0, tile, high)
        own = own_lanes(value.shape, high)
        query = scaled_query(raw_query, high)
        key = masked_key(raw_key, high, length)
        product = (incoming.astype(jnp.float32) * context.astype(jnp.float32)).T
        start = 0 if high else 64
        layout_mean = jnp.sum(product[start : start + 16], 0, keepdims=True)
        joint_mean = jnp.sum(product, 0, keepdims=True)
        zero = jnp.zeros_like(value)
        probs = jnp.exp(dot(key, query, NT) - total_ref[0, head : head + 1, :])
        value_grad = dot(probs.astype(jnp.bfloat16), incoming, NN)
        joint = (probs * (dot(value, incoming, NT) - joint_mean)).astype(jnp.bfloat16)
        alone = (
            probs * (dot(jnp.where(own, zero, value), incoming, NT) - layout_mean)
        ).astype(jnp.bfloat16)
        key_grad = jnp.where(own, dot(joint, raw_query, NN) * 0.125, dot(alone, raw_query, NN) * 0.25)
        rows = lax.broadcasted_iota(jnp.int32, (128, value.shape[0]), 0) < 64
        if high:
            rows = ~rows
        query_grad = jnp.where(
            rows, dot(raw_key, joint, TN) * 0.125, dot(raw_key, alone, TN) * 0.25
        )
        grads[0].append(query_grad.T)
        grads[1].append(key_grad)
        grads[2].append(value_grad)
    low = lane_of(grads[0][0].shape) < 64
    zero = jnp.zeros_like(grads[0][0])
    for slot in range(3):
        first, second, third = grads[slot]
        at = slot * 256
        text_grad_ref[0, :, at : at + 128] = jnp.where(low, first, second).astype(jnp.bfloat16)
        text_grad_ref[0, :, at + 128 : at + 256] = jnp.where(low, third, zero).astype(jnp.bfloat16)
        layout_grad_ref[0, :, at : at + 128] = jnp.where(low, second, first).astype(jnp.bfloat16)
        layout_grad_ref[0, :, at + 128 : at + 256] = jnp.where(low, zero, third).astype(
            jnp.bfloat16
        )


def attend_back(length, text, layout, total, context, layout_context, grad, layout_grad):
    parts, positions, _ = text.shape
    return pl.pallas_call(
        attend_back_kernel,
        grid=(parts,),
        in_specs=[
            pl.BlockSpec(memory_space=pltpu.SMEM),
            block(positions, 768),
            block(positions, 768),
            block(8, positions),
            block(positions, 256),
            block(positions, 256),
            block(positions, 256),
            block(positions, 256),
        ],
        out_specs=[block(positions, 768), block(positions, 768)],
        out_shape=[
            outside((parts, positions, 768), jnp.bfloat16),
            outside((parts, positions, 768), jnp.bfloat16),
        ],
        compiler_params=pltpu.CompilerParams(vmem_limit_bytes=30 << 20),
        cost_estimate=COST,
        name="attend_back",
    )(length, *kept_out(text, layout, total, context, layout_context, grad, layout_grad))


SPAN = 235008
FRAME = 320
UNIT = 768


def cast_kernel(shift_ref, master_ref, frame_ref, flat_ref):
    whole = SPAN // 1024
    for step in range(whole):
        flat_ref[pl.ds(8 * step, 8), :] = master_ref[0, 0, pl.ds(1024 * step, 1024)].reshape(8, 128)
    flat_ref[pl.ds(8 * whole, 4), :] = master_ref[0, 0, pl.ds(1024 * whole, 512)].reshape(4, 128)
    for column in range(6):
        rows = flat_ref[pl.ds(column, 306, stride=6), :]
        rows = jnp.concatenate((rows, jnp.zeros((14, 128), jnp.float32)), 0)
        rows = pltpu.roll(rows, shift_ref[0], 0)
        frame_ref[0, :, column * 128 : column * 128 + 128] = rows.astype(jnp.bfloat16)


def cast_frame(shift, master):
    return pl.pallas_call(
        cast_kernel,
        in_specs=[pl.BlockSpec(memory_space=pltpu.SMEM), pl.BlockSpec(memory_space=pltpu.VMEM)],
        out_specs=pl.BlockSpec(memory_space=pltpu.VMEM),
        out_shape=jax.ShapeDtypeStruct((1, FRAME, UNIT), jnp.bfloat16),
        scratch_shapes=[pltpu.VMEM((1840, 128), jnp.float32)],
        name="cast_frame",
    )(shift, master)


def finish_kernel(
    place_ref,
    slice_ref,
    inner_ref,
    inner_last_ref,
    edge_ref,
    edge_last_ref,
    flat_out_ref,
    square_ref,
    flat_ref,
):
    shift, window = place_ref[0], place_ref[1]
    row = lax.broadcasted_iota(jnp.int32, (FRAME, 128), 0)
    inner = (window >= 2) & (window < 6)
    squares = jnp.zeros((8, 128), jnp.float32)
    for column in range(6):
        at = slice(column * 128, column * 128 + 128)
        rows = jnp.where(
            inner,
            inner_ref[:, at].astype(jnp.float32) + inner_last_ref[:, at].astype(jnp.float32),
            edge_ref[:, at].astype(jnp.float32) + edge_last_ref[:, at].astype(jnp.float32),
        )
        rows = pltpu.roll(rows, FRAME - shift, 0)
        flat_ref[pl.ds(column, 306, stride=6), :] = rows[:306]
        masked = jnp.where(row < 306, rows, 0.0)
        squares = squares + jnp.sum((masked * masked).reshape(40, 8, 128), 0)
    square_ref[:, :512] = jnp.broadcast_to(slice_ref[...], (32, 512))
    square_ref[:, 512:] = jnp.broadcast_to(jnp.sum(squares, 0, keepdims=True), (32, 128))
    whole = SPAN // 1024
    for step in range(whole):
        flat_out_ref[0, 0, pl.ds(1024 * step, 1024)] = flat_ref[pl.ds(8 * step, 8), :].reshape(1024)
    flat_out_ref[0, 0, pl.ds(1024 * whole, 512)] = flat_ref[pl.ds(8 * whole, 4), :].reshape(512)


def finish(place, *values):
    return pl.pallas_call(
        finish_kernel,
        in_specs=[pl.BlockSpec(memory_space=pltpu.SMEM)]
        + [pl.BlockSpec(memory_space=pltpu.VMEM)] * 5,
        out_specs=[pl.BlockSpec(memory_space=pltpu.VMEM)] * 2,
        out_shape=[
            jax.ShapeDtypeStruct((1, 1, SPAN), jnp.float32),
            jax.ShapeDtypeStruct((32, 640), jnp.float32),
        ],
        scratch_shapes=[pltpu.VMEM((1840, 128), jnp.float32)],
        name="finish",
    )(place, *values)


RATE_STEPS = (
    (0, 768.0**-0.5),
    (576, 8.0 * 768.0**-0.5),
    (768, 768.0**-0.5),
    (1536, 3072.0**-0.5),
    (2304, 192.0**-0.5),
    (2340, 8.0 * 192.0**-0.5),
    (2352, 192.0**-0.5),
    (2400, 768.0**-0.5),
)


def adam_kernel(
    first_index_ref,
    shared_ref,
    weight_ref,
    gradient_ref,
    first_ref,
    second_ref,
    average_ref,
    new_weight_ref,
    new_first_ref,
    new_second_ref,
    low_ref,
    new_average_ref,
):
    width = weight_ref.shape[2]
    start = first_index_ref[0] + pl.program_id(0) * width
    shared = shared_ref[...]
    squares = jnp.where(lax.broadcasted_iota(jnp.int32, shared.shape, 1) < 512, shared * shared, shared)
    squares = jnp.sum(jnp.sum(squares, 0, keepdims=True), 1, keepdims=True)
    factor = 1.0 / jnp.maximum(jnp.sqrt(squares), 1.0)
    for at in range(0, width, CHUNK):
        count = min(CHUNK, width - at)
        place = pl.ds(at, count)

        def load(ref):
            return ref[0, 0, place].reshape(count // 128, 128)

        def store(ref, value):
            ref[0, 0, place] = value.reshape(count)

        shape = (count // 128, 128)
        index = lax.broadcasted_iota(jnp.int32, shape, 0) * 128 + start + at
        rate = jnp.full(shape, RATE_STEPS[0][1], jnp.float32)
        for row, value in RATE_STEPS[1:]:
            rate = jnp.where(index >= row * UNIT, jnp.float32(value), rate)
        weight = load(weight_ref)
        clipped = load(gradient_ref) * factor
        new_first = 0.5 * load(first_ref) + 0.5 * clipped
        new_second = 0.6 * load(second_ref) + 0.4 * clipped * clipped
        first_hat = new_first * (1.0 / (1.0 - 0.5**5))
        second_hat = new_second * (1.0 / (1.0 - 0.6**5))
        updated = weight - rate * (first_hat / (jnp.sqrt(second_hat) + 1e-8) + 0.01 * weight)
        store(new_weight_ref, updated)
        store(new_first_ref, new_first)
        store(new_second_ref, new_second)
        low_ref[0, 0, place] = updated.reshape(count).astype(jnp.bfloat16)
        store(new_average_ref, 0.5 * load(average_ref) + 0.5 * updated)


CHUNK = 1024


def adam(first_index, shared, weight, gradient, first, second, average, steps=3):
    span = weight.shape[2]
    spec = pl.BlockSpec((1, 1, span // steps), lambda i: (0, 0, i))
    full = jax.ShapeDtypeStruct(weight.shape, jnp.float32)
    return pl.pallas_call(
        adam_kernel,
        grid=(steps,),
        in_specs=[
            pl.BlockSpec(memory_space=pltpu.SMEM),
            pl.BlockSpec((32, 640), lambda i: (0, 0)),
        ]
        + [spec] * 5,
        out_specs=[spec] * 5,
        out_shape=[full, full, full, jax.ShapeDtypeStruct(weight.shape, jnp.bfloat16), full],
        name="adam",
    )(first_index, shared, weight, gradient, first, second, average)


def placing(rows, columns, row_axis):
    narrow = lax.broadcasted_iota(jnp.int32, (rows, columns), row_axis)
    wide = lax.broadcasted_iota(jnp.int32, (rows, columns), 1 - row_axis)
    place = jnp.where(narrow < 16, narrow + 64, jnp.where(narrow < 32, narrow - 16, narrow + 160))
    return jnp.where(place == wide, 1.0, 0.0).astype(jnp.bfloat16)


def wide_rows(value):
    return jnp.concatenate((value, jnp.zeros((value.shape[0], 64), value.dtype)), 1)


def early_kernel(
    parts_ref, mid_ref, up_in_ref, hidden_ref, down_in_ref, context_ref, attn_in_ref, early_ref
):
    early_ref[0, 0:192] = dot(context_ref[0], attn_in_ref[...], TN)[:192].astype(jnp.bfloat16)
    early_ref[0, 192:960] = dot(mid_ref[...], up_in_ref[0], TN).astype(jnp.bfloat16)
    early_ref[0, 960:1728] = dot(hidden_ref[0], down_in_ref[...], TN).astype(jnp.bfloat16)
    early_ref[0, 1728:] = jnp.zeros((96, 768), jnp.bfloat16)


def early_grads(parts, mid, up_in, hidden, down_in, context, attn_in):
    positions = mid.shape[0]
    count = parts.shape[0]
    fixed = pl.BlockSpec((positions, 768), lambda i, p: (0, 0))
    chosen = pl.BlockSpec((1, positions, 768), lambda i, p: (p[i], 0, 0))
    return pl.pallas_call(
        early_kernel,
        grid_spec=pltpu.PrefetchScalarGridSpec(
            num_scalar_prefetch=1,
            grid=(count,),
            in_specs=[
                fixed,
                chosen,
                chosen,
                fixed,
                pl.BlockSpec((1, positions, 256), lambda i, p: (p[i], 0, 0)),
                fixed,
            ],
            out_specs=pl.BlockSpec((1, 1824, 768), lambda i, p: (i, 0, 0)),
        ),
        out_shape=outside((count, 1824, 768), jnp.bfloat16),
        compiler_params=pltpu.CompilerParams(vmem_limit_bytes=24 << 20),
        cost_estimate=COST,
        name="early_grads",
    )(parts, *kept_out(mid, up_in, hidden, down_in, context, attn_in))


def late_kernel(
    parts_ref,
    text_ref,
    qkv_in_ref,
    layout_ref,
    lqkv_in_ref,
    lcontext_ref,
    lattn_in_ref,
    lmid_ref,
    lup_in_ref,
    lhidden_ref,
    ldown_in_ref,
    late_ref,
    heads_ref,
    rows_ref,
    slots_ref,
    small_ref,
):
    heads_grad = dot(text_ref[...], qkv_in_ref[0], TN)
    for tile in range(6):
        heads_ref[tile] = heads_grad[:, 128 * tile : 128 * tile + 128]
    for slot in range(3):
        for step in range(4):
            piece = jnp.concatenate(
                [heads_ref[2 * slot + half, pl.ds(step, 192, stride=4), :] for half in range(2)], 1
            )
            late_ref[0, 192 * slot : 192 * slot + 192, 192 * step : 192 * step + 192] = piece[
                :, :192
            ].astype(jnp.bfloat16)

    slots_ref[...] = jnp.zeros_like(slots_ref)
    lqkv_grad = dot(layout_ref[...], lqkv_in_ref[0], TN)
    for slot in range(3):
        for half in range(2):
            at = 256 * slot + 128 * half
            rows_ref[half, 0:192] = lqkv_grad[:, at : at + 128]
            for step in range(16):
                row = 16 * (3 * step + slot)
                slots_ref[row : row + 12, 128 * half : 128 * half + 128] = rows_ref[
                    half, pl.ds(step, 12, stride=16), :
                ]
    placed = dot(slots_ref[...].astype(jnp.bfloat16), placing(256, 48, 1), NN)
    for slot in range(3):
        for step in range(16):
            at = 16 * (3 * step + slot)
            small_ref[12 * slot : 12 * slot + 12, 48 * step : 48 * step + 48] = placed[at : at + 12]

    def gather(first, count):
        for step in range(4):
            piece = jnp.concatenate(
                [rows_ref[half, pl.ds(step, count, stride=4), :] for half in range(2)], 1
            )
            small_ref[first : first + count, 192 * step : 192 * step + 192] = piece[:, :192]

    lout_grad = dot(lcontext_ref[0], lattn_in_ref[...], TN)
    for head, at in enumerate((64, 0, 192)):
        rows_ref[0, 16 * head : 16 * head + 16, :] = lout_grad[at : at + 16, 0:128]
        rows_ref[1, 16 * head : 16 * head + 16, 0:64] = lout_grad[at : at + 16, 128:192]
    gather(36, 12)
    for first, left, right in (
        (48, lmid_ref[...], lup_in_ref[0]),
        (96, lhidden_ref[0], ldown_in_ref[...]),
    ):
        grad = dot(left, right, TN)
        rows_ref[0, 0:192, :] = grad[:, 0:128]
        rows_ref[1, 0:192, 0:64] = grad[:, 128:192]
        gather(first, 48)
    late_ref[0, 576:720] = small_ref[...].astype(jnp.bfloat16)


def late_grads(parts, text, qkv_in, layout, lqkv_in, lcontext, lattn_in, lmid, lup_in, lhidden, ldown_in):
    positions = text.shape[0]
    count = parts.shape[0]

    def fixed(width):
        return pl.BlockSpec((positions, width), lambda i, p: (0, 0))

    def chosen(width):
        return pl.BlockSpec((1, positions, width), lambda i, p: (p[i], 0, 0))

    return pl.pallas_call(
        late_kernel,
        grid_spec=pltpu.PrefetchScalarGridSpec(
            num_scalar_prefetch=1,
            grid=(count,),
            in_specs=[
                fixed(768),
                chosen(768),
                fixed(192),
                chosen(768),
                chosen(256),
                fixed(192),
                fixed(192),
                chosen(192),
                chosen(192),
                fixed(192),
            ],
            out_specs=pl.BlockSpec((1, 720, 768), lambda i, p: (i, 0, 0)),
            scratch_shapes=[
                pltpu.VMEM((6, 768, 128), jnp.float32),
                pltpu.VMEM((2, 192, 128), jnp.float32),
                pltpu.VMEM((768, 256), jnp.float32),
                pltpu.VMEM((144, 768), jnp.float32),
            ],
        ),
        out_shape=outside((count, 720, 768), jnp.bfloat16),
        compiler_params=pltpu.CompilerParams(vmem_limit_bytes=26 << 20),
        cost_estimate=COST,
        name="late_grads",
    )(parts, *kept_out(text, qkv_in, layout, lqkv_in, lcontext, lattn_in, lmid, lup_in, lhidden, ldown_in))


TILES = 20
HEAD_PIECES = ((0, 0, 20, 0), (1, 1, 16, 20), (1, 0, 1, 36), (7, 11, 9, 37))
OUT_PIECES = ((1, 17, 3, 0), (2, 1, 9, 3))
UP_PIECES = ((2, 10, 10, 0), (3, 1, 19, 10), (4, 1, 19, 29))
DOWN_PIECES = ((5, 1, 19, 0), (6, 1, 19, 19), (7, 1, 10, 38))
OUT_SEAMS = ((2, 2),)
UP_SEAMS = ((3, 9), (4, 28), (5, 47))
DOWN_SEAMS = ((6, 18), (7, 37))


def start_piece(table_ref, sources, part, window, first, count, target, semaphore):
    row = part * 8 + window
    which, slot = table_ref[0, row], table_ref[1, row]

    def among(low, high):
        if high - low == 1:
            place = sources[low].at[slot, pl.ds(first, count)]
            pltpu.make_async_copy(place, target, semaphore).start()
            return
        middle = (low + high) // 2

        @pl.when(which < middle)
        def lower():
            among(low, middle)

        @pl.when(which >= middle)
        def upper():
            among(middle, high)

    among(0, len(sources))


def wait_piece(table_ref, sources, part, window, first, count, target, semaphore):
    pltpu.make_async_copy(sources[0].at[0, pl.ds(first, count)], target, semaphore).wait()


def unpack_kernel(
    table_ref, *refs
):
    sources = refs[:12]
    qkv_ref, lqkv_ref, lwo_ref, lw1_ref, lw2_ref, frames_ref, rows_ref, small_ref, semaphores = refs[12:]
    part = pl.program_id(0)

    def each(act, number):
        for index, (window, first, count, at) in enumerate(HEAD_PIECES):
            target = frames_ref.at[number, pl.ds(at, count)]
            act(table_ref, sources, number, window, first, count, target, semaphores.at[number, index])

    @pl.when(part == 0)
    def begin():
        for number in range(4):
            each(start_piece, number)

    each(wait_piece, part)
    frames_ref[part, 19] = frames_ref[part, 19] + frames_ref[part, 36]

    def spread(source_ref, first, count, stride, target_ref):
        for step in range(4):
            piece = wide_rows(source_ref[first : first + count, 192 * step : 192 * step + 192])
            target_ref[0, pl.ds(step, count, stride=stride), :] = piece[:, :128]
            target_ref[1, pl.ds(step, count, stride=stride), :] = piece[:, 128:]

    small_ref[...] = frames_ref[part, 37:46].reshape(144, 768).astype(jnp.float32)
    for slot in range(3):
        for step in range(4):
            piece = frames_ref[part, 12 * slot : 12 * slot + 12, :, 192 * step : 192 * step + 192]
            piece = wide_rows(piece.reshape(192, 192).astype(jnp.float32))
            rows_ref[0, pl.ds(step, 192, stride=4), :] = piece[:, :128]
            rows_ref[1, pl.ds(step, 192, stride=4), :] = piece[:, 128:]
        qkv_ref[0, :, 256 * slot : 256 * slot + 128] = rows_ref[0].astype(jnp.bfloat16)
        qkv_ref[0, :, 256 * slot + 128 : 256 * slot + 256] = rows_ref[1].astype(jnp.bfloat16)
    place = placing(48, 256, 0)
    narrow = jnp.concatenate(
        [small_ref[0:48, 48 * step : 48 * step + 48] for step in range(16)], 0
    )
    placed = dot(narrow.astype(jnp.bfloat16), place, NN)
    for slot in range(3):
        for step in range(16):
            piece = placed[48 * step + 12 * slot : 48 * step + 12 * slot + 12]
            rows_ref[0, pl.ds(step, 12, stride=16), :] = piece[:, :128]
            rows_ref[1, pl.ds(step, 12, stride=16), :] = piece[:, 128:]
        lqkv_ref[0, :, 256 * slot : 256 * slot + 128] = rows_ref[0, 0:192].astype(jnp.bfloat16)
        lqkv_ref[0, :, 256 * slot + 128 : 256 * slot + 256] = rows_ref[1, 0:192].astype(jnp.bfloat16)
    spread(small_ref, 36, 12, 4, rows_ref)
    lwo_ref[...] = jnp.zeros_like(lwo_ref)
    for head, at in enumerate((64, 0, 192)):
        for half, width in ((0, 128), (1, 64)):
            lwo_ref[0, at : at + 16, 128 * half : 128 * half + width] = rows_ref[
                half, 16 * head : 16 * head + 16, :width
            ].astype(jnp.bfloat16)
    for first, target_ref in ((48, lw1_ref), (96, lw2_ref)):
        spread(small_ref, first, 48, 4, rows_ref)
        target_ref[0, :, 0:128] = rows_ref[0, 0:192].astype(jnp.bfloat16)
        target_ref[0, :, 128:192] = rows_ref[1, 0:192, :64].astype(jnp.bfloat16)


def unpack(table, sources):
    shapes = ((768, 768), (192, 768), (256, 192), (192, 192), (192, 192))
    return pl.pallas_call(
        unpack_kernel,
        grid=(4,),
        in_specs=[pl.BlockSpec(memory_space=pltpu.SMEM)] + [pl.BlockSpec(memory_space=pl.ANY)] * 12,
        out_specs=[pl.BlockSpec((1,) + shape, lambda t: (t, 0, 0)) for shape in shapes],
        out_shape=[outside((4,) + shape, jnp.bfloat16) for shape in shapes],
        scratch_shapes=[
            pltpu.VMEM((4, 46, 16, 768), jnp.bfloat16),
            pltpu.VMEM((2, 768, 128), jnp.float32),
            pltpu.VMEM((144, 768), jnp.float32),
            pltpu.SemaphoreType.DMA((4, 4)),
        ],
        compiler_params=pltpu.CompilerParams(vmem_limit_bytes=20 << 20),
        cost_estimate=COST,
        name="unpack",
    )(table, *kept_out(*sources))


def gelu_parts(value):
    below = 0.5 + 0.5 * lax.erf(value * 0.5**0.5)
    decay = jnp.exp(value * value * -0.5)
    return value * below, below + value * decay * 0.3989422804014327


def normed_rows(value):
    mean = jnp.mean(value, -1, keepdims=True)
    centred = value - mean
    scale = lax.rsqrt(jnp.mean(centred * centred, -1, keepdims=True) + 1e-5)
    return centred * scale, scale


def norm_pull(incoming, normed, scale, gain):
    scaled = incoming * gain
    return scale * (
        scaled
        - jnp.mean(scaled, -1, keepdims=True)
        - normed * jnp.mean(scaled * normed, -1, keepdims=True)
    )


def column_sums(target_ref, *values):
    for row, value in enumerate(values):
        target_ref[row : row + 1] = jnp.sum(value, 0, keepdims=True)


def each_piece(act, table_ref, sources, matrix, part, target_ref, seams_ref, semaphores):
    index = matrix[2]
    for window, first, count, at in matrix[0]:
        target = target_ref.at[part, pl.ds(at, count)]
        act(table_ref, sources, part, window, first, count, target, semaphores.at[part, index])
        index += 1
    for number, (window, _) in enumerate(matrix[1]):
        target = seams_ref.at[part, pl.ds(matrix[3] + number, 1)]
        act(table_ref, sources, part, window, 0, 1, target, semaphores.at[part, index])
        index += 1


OUT_MATRIX = (OUT_PIECES, OUT_SEAMS, 0, 0)
UP_MATRIX = (UP_PIECES, UP_SEAMS, 3, 1)
DOWN_MATRIX = (DOWN_PIECES, DOWN_SEAMS, 9, 4)


def started(*args):
    def begin(part, carry):
        each_piece(start_piece, *args[:3], part, *args[3:])
        return carry

    lax.fori_loop(0, 4, begin, 0)


def awaited(table_ref, pieces_refs, matrix, part, target_ref, seams_ref, semaphores):
    each_piece(wait_piece, table_ref, pieces_refs, matrix, part, target_ref, seams_ref, semaphores)
    for number, (_, at) in enumerate(matrix[1]):
        target_ref[part, at] = target_ref[part, at] + seams_ref[part, matrix[3] + number]


def bring_parts(table_ref, pieces_refs, matrices, part, seams_ref, semaphores):
    def ahead(number, carry):
        for matrix, target_ref in matrices:
            each_piece(
                start_piece,
                table_ref,
                pieces_refs,
                matrix,
                number,
                target_ref,
                seams_ref,
                semaphores,
            )
        return carry

    first = jnp.where(part == 0, 0, part + 1)
    lax.fori_loop(first, jnp.minimum(part + 2, 4), ahead, 0)
    for matrix, target_ref in matrices:
        awaited(table_ref, pieces_refs, matrix, part, target_ref, seams_ref, semaphores)


def forward_kernel(*refs):
    table_ref, pieces_refs, refs = refs[0], refs[1:17], refs[17:]
    inputs, outputs, scratch = refs[:18], refs[18:37], refs[37:]
    out_ref = outputs[18]
    out_scratch, up_scratch, down_scratch, seams_ref, semaphores = scratch[6:]
    part = pl.program_id(0)
    matrices = ((UP_MATRIX, up_scratch), (DOWN_MATRIX, down_scratch))

    @pl.when(part == 0)
    def begin():
        started(table_ref, pieces_refs, OUT_MATRIX, out_scratch, seams_ref, semaphores)
        out_scratch[:, 12:16] = jnp.zeros((4, 4, 16, 768), jnp.bfloat16)
        for number in range(4):
            awaited(table_ref, pieces_refs, OUT_MATRIX, number, out_scratch, seams_ref, semaphores)
        out_ref[...] = out_scratch[...].reshape(4, 256, 768)

    bring_parts(table_ref, pieces_refs, matrices, part, seams_ref, semaphores)
    for stream in range(2):
        act_ref, context_ref, own_out_ref, own_up_ref, up_bias_ref, own_down_ref, rows_ref, cotangent_ref, _ = inputs[
            9 * stream : 9 * stream + 9
        ]
        (
            mid_low_ref,
            normed_ref,
            scale_ref,
            hidden_ref,
            slope_ref,
            final_ref,
            pre_ref,
            pre_low_ref,
            sums_ref,
        ) = outputs[9 * stream : 9 * stream + 9]
        mid_ref, total_ref, low_ref = scratch[3 * stream : 3 * stream + 3]

        @pl.when(part == 0)
        def attention_out():
            weights = out_ref if stream == 0 else own_out_ref
            attn = sum(dot(context_ref[number], weights[number], NN) for number in range(4))
            normed, scale = normed_rows(attn + rows_ref[2:3] + act_ref[...])
            mid = normed * rows_ref[3:4] + rows_ref[4:5]
            normed_ref[...] = normed
            scale_ref[...] = scale
            mid_ref[...] = mid
            low_ref[...] = mid.astype(jnp.bfloat16)
            mid_low_ref[...] = low_ref[...]

        if stream == 0:
            up, down = up_scratch[part].reshape(768, 768), down_scratch[part].reshape(768, 768)
        else:
            up, down = own_up_ref[0], own_down_ref[0]
        hidden, slope = gelu_parts(dot(low_ref[...], up, NN) + up_bias_ref[0])
        hidden = hidden.astype(jnp.bfloat16)
        hidden_ref[0] = hidden
        slope_ref[0] = slope.astype(jnp.bfloat16)
        product = dot(hidden, down, NN)

        @pl.when(part == 0)
        def first():
            total_ref[...] = product

        @pl.when(part > 0)
        def later():
            total_ref[...] = total_ref[...] + product

        @pl.when(part == 3)
        def last():
            gain = rows_ref[6:7]
            normed, scale = normed_rows(total_ref[...] + rows_ref[5:6] + mid_ref[...])
            final_ref[0] = (normed * gain + rows_ref[7:8]).astype(jnp.bfloat16)
            incoming = cotangent_ref[0].astype(jnp.float32)
            pre = norm_pull(incoming, normed, scale, gain)
            pre_ref[...] = pre
            pre_low_ref[...] = pre.astype(jnp.bfloat16)
            column_sums(sums_ref, pre, incoming * normed, incoming)


def backward_kernel(*refs):
    table_ref, pieces_refs, refs = refs[0], refs[1:17], refs[17:]
    inputs, outputs, scratch = refs[:18], refs[18:30], refs[30:]
    up_scratch, down_scratch, seams_ref, semaphores = scratch[2:]
    part = pl.program_id(0)
    matrices = ((DOWN_MATRIX, down_scratch), (UP_MATRIX, up_scratch))

    bring_parts(table_ref, pieces_refs, matrices, part, seams_ref, semaphores)
    for stream in range(2):
        pre_ref, pre_low_ref, slope_ref, normed_ref, scale_ref, rows_ref, out_ref, own_down_ref, own_up_ref = inputs[
            9 * stream : 9 * stream + 9
        ]
        up_in_ref, up_sum_ref, attn_ref, attn_low_ref, sums_ref, context_grad_ref = outputs[
            6 * stream : 6 * stream + 6
        ]
        total_ref = scratch[stream]
        if stream == 0:
            up, down = up_scratch[part].reshape(768, 768), down_scratch[part].reshape(768, 768)
        else:
            up, down = own_up_ref[0], own_down_ref[0]
        up_in = dot(pre_low_ref[...], down, NT) * slope_ref[0].astype(jnp.float32)
        up_in = up_in.astype(jnp.bfloat16)
        up_in_ref[0] = up_in
        up_sum_ref[0] = jnp.sum(up_in.astype(jnp.float32), 0, keepdims=True)
        back = dot(up_in, up, NT)

        @pl.when(part == 0)
        def first():
            total_ref[...] = back

        @pl.when(part > 0)
        def later():
            total_ref[...] = total_ref[...] + back

        @pl.when(part == 3)
        def last():
            incoming = total_ref[...] + pre_ref[...]
            normed = normed_ref[...]
            attn = norm_pull(incoming, normed, scale_ref[...], rows_ref[3:4])
            attn_low = attn.astype(jnp.bfloat16)
            attn_ref[...] = attn
            attn_low_ref[...] = attn_low
            column_sums(sums_ref, attn, incoming * normed, incoming)
            for number in range(4):
                context_grad_ref[number] = dot(attn_low, out_ref[number], NT).astype(jnp.bfloat16)


def whole(*shape):
    return pl.BlockSpec(shape, lambda t: (0,) * len(shape), pipeline_mode=pl.Buffered(1))


def result(*shape):
    return pl.BlockSpec(shape, lambda t: (0,) * len(shape))


def by_part(*shape):
    return pl.BlockSpec((1,) + shape, lambda t: (t,) + (0,) * len(shape))


PIECES_SPECS = [pl.BlockSpec(memory_space=pltpu.SMEM)] + [
    pl.BlockSpec(memory_space=pl.ANY)
] * 16


def feed_forward(table, pieces, text, layout):
    positions = text[0].shape[0]
    small = jnp.zeros((8, 128), jnp.float32)
    in_specs, operands, out_specs, out_shape, scratch = [], [], [], [], []
    for number, stream in enumerate((text, layout)):
        act, context, out, up, up_bias, down, rows, cotangent = stream
        width, hidden = act.shape[1], up_bias.shape[2]
        matrices = (out, up, down)
        specs = (whole(4, 256, width), by_part(width, hidden), by_part(hidden, width))
        if number == 0:
            matrices, specs = (small,) * 3, (whole(8, 128),) * 3
        in_specs += [
            whole(positions, width),
            whole(4, positions, 256),
            specs[0],
            specs[1],
            by_part(1, hidden),
            specs[2],
            whole(8, width),
            whole(1, positions, width),
            whole(8, 128),
        ]
        operands += [act, context, matrices[0], matrices[1], up_bias, matrices[2], rows, cotangent, small]
        out_specs += [
            result(positions, width),
            result(positions, width),
            result(positions, 1),
            by_part(positions, hidden),
            by_part(positions, hidden),
            result(1, positions, width),
            result(positions, width),
            result(positions, width),
            result(8, width),
        ]
        out_shape += [
            outside((positions, width), jnp.bfloat16),
            outside((positions, width), jnp.float32),
            outside((positions, 1), jnp.float32),
            outside((4, positions, hidden), jnp.bfloat16),
            outside((4, positions, hidden), jnp.bfloat16),
            outside((1, positions, width), jnp.bfloat16),
            outside((positions, width), jnp.float32),
            outside((positions, width), jnp.bfloat16),
            outside((8, width), jnp.float32),
        ]
        scratch += [
            pltpu.VMEM((positions, width), jnp.float32),
            pltpu.VMEM((positions, width), jnp.float32),
            pltpu.VMEM((positions, width), jnp.bfloat16),
        ]
    results = pl.pallas_call(
        forward_kernel,
        grid=(4,),
        in_specs=PIECES_SPECS + in_specs,
        out_specs=out_specs + [result(4, 256, 768)],
        out_shape=out_shape + [outside((4, 256, 768), jnp.bfloat16)],
        scratch_shapes=scratch
        + [
            pltpu.VMEM((4, 16, 16, 768), jnp.bfloat16),
            pltpu.VMEM((4, 48, 16, 768), jnp.bfloat16),
            pltpu.VMEM((4, 48, 16, 768), jnp.bfloat16),
            pltpu.VMEM((4, 6, 16, 768), jnp.bfloat16),
            pltpu.SemaphoreType.DMA((4, 14)),
        ],
        compiler_params=pltpu.CompilerParams(vmem_limit_bytes=56 << 20),
        cost_estimate=COST,
        name="feed_forward",
    )(table, *kept_out(*pieces), *kept_out(*operands))
    return results[:9], results[9:18], results[18]


def feed_back(table, pieces, text, layout):
    positions = text[0].shape[0]
    small = jnp.zeros((8, 128), jnp.float32)
    in_specs, operands, out_specs, out_shape, scratch = [], [], [], [], []
    for number, stream in enumerate((text, layout)):
        pre, pre_low, slope, normed, scale, rows, out, down, up = stream
        width, hidden = pre.shape[1], slope.shape[2]
        matrices, specs = (down, up), (by_part(hidden, width), by_part(width, hidden))
        if number == 0:
            matrices, specs = (small,) * 2, (whole(8, 128),) * 2
        in_specs += [
            whole(positions, width),
            whole(positions, width),
            by_part(positions, hidden),
            whole(positions, width),
            whole(positions, 1),
            whole(8, width),
            whole(4, 256, width),
            specs[0],
            specs[1],
        ]
        operands += [pre, pre_low, slope, normed, scale, rows, out, *matrices]
        out_specs += [
            by_part(positions, hidden),
            by_part(1, hidden),
            result(positions, width),
            result(positions, width),
            result(8, width),
            result(4, positions, 256),
        ]
        out_shape += [
            outside((4, positions, hidden), jnp.bfloat16),
            outside((4, 1, hidden), jnp.float32),
            outside((positions, width), jnp.float32),
            outside((positions, width), jnp.bfloat16),
            outside((8, width), jnp.float32),
            outside((4, positions, 256), jnp.bfloat16),
        ]
        scratch.append(pltpu.VMEM((positions, width), jnp.float32))
    results = pl.pallas_call(
        backward_kernel,
        grid=(4,),
        in_specs=PIECES_SPECS + in_specs,
        out_specs=out_specs,
        out_shape=out_shape,
        scratch_shapes=scratch
        + [
            pltpu.VMEM((4, 48, 16, 768), jnp.bfloat16),
            pltpu.VMEM((4, 48, 16, 768), jnp.bfloat16),
            pltpu.VMEM((4, 6, 16, 768), jnp.bfloat16),
            pltpu.SemaphoreType.DMA((4, 14)),
        ],
        compiler_params=pltpu.CompilerParams(vmem_limit_bytes=56 << 20),
        cost_estimate=COST,
        name="feed_back",
    )(table, *kept_out(*pieces), *kept_out(*operands))
    return results[:6], results[6:]


def sum_kernel(counts, table_ref, *refs):
    total = len(counts)
    sources, out_ref = refs[:total], refs[total]
    buffers, semaphores = refs[total + 1 : -1], refs[-1]
    entries = out_ref.shape[0]

    def copies(entry):
        found = []
        for number, (source, buffer) in enumerate(zip(sources, buffers)):
            at = 0
            for piece, count in enumerate(counts[number]):
                part, first = (table_ref[number, entry, piece, item] for item in range(2))
                found.append(
                    pltpu.make_async_copy(
                        source.at[part, pl.ds(first, count)],
                        buffer.at[entry, pl.ds(at, count)],
                        semaphores.at[number, entry, piece],
                    )
                )
                at += count
        return found

    pending = [copies(entry) for entry in range(entries)]
    for copy in sum(pending, []):
        copy.start()
    for entry in range(entries):
        for copy in pending[entry]:
            copy.wait()
        length = out_ref.shape[1]
        step = 4 if length % 4 == 0 else 2

        def add(number, carry):
            tiles = pl.ds(number * step, step)
            total_value = sum(buffer[entry, tiles].astype(jnp.float32) for buffer in buffers)
            out_ref[entry, tiles] = total_value.astype(jnp.bfloat16)
            return carry

        lax.fori_loop(0, length // step, add, 0)


def sum_windows(*sources):
    entries = len(sources[0][1])
    counts = tuple(tuple(count for _, _, count in places[0]) for _, places in sources)
    widest = max(len(item) for item in counts)
    length = sum(counts[0])
    rows = []
    for _, places in sources:
        for entry in places:
            for index, first, _ in entry + [(0, 0, 0)] * (widest - len(entry)):
                rows += [jnp.asarray(index, jnp.int32), jnp.asarray(first, jnp.int32)]
    table = jnp.stack(rows).reshape(len(sources), entries, widest, 2)
    shape = (entries, length, 16, 768)
    size = entries * length * 16 * 768 * 2
    return pl.pallas_call(
        lambda *refs: sum_kernel(counts, *refs),
        in_specs=[pl.BlockSpec(memory_space=pltpu.SMEM)]
        + [pl.BlockSpec(memory_space=pl.ANY)] * len(sources),
        out_specs=pl.BlockSpec(memory_space=pltpu.VMEM),
        out_shape=outside(shape, jnp.bfloat16),
        scratch_shapes=[pltpu.VMEM(shape, jnp.bfloat16)] * len(sources)
        + [pltpu.SemaphoreType.DMA((len(sources), entries, widest))],
        compiler_params=pltpu.CompilerParams(vmem_limit_bytes=24 << 20),
        cost_estimate=pl.CostEstimate(
            flops=size, transcendentals=0, bytes_accessed=size * (len(sources) + 1)
        ),
        name="sum_windows",
    )(table, *(pltpu.with_memory_space_constraint(array, pltpu.HBM) for array, _ in sources))


INNER_PIECES = ((2, 21, 20), (40, 59, 20))
OUTER_PIECES = ((78, 97, 17), (95, 0, 3))
LATE_PIECES = ((0, 19, 26),)


def exchange_pairs(flip):
    pairs = []
    for device in range(32):
        z, x, y, core = device // 8, device // 4 % 2, device // 2 % 2, device % 2
        z, x, y, core = flip(z, x, y, core)
        pairs.append((device, z * 8 + x * 4 + y * 2 + core))
    return pairs


ROUNDS = (
    exchange_pairs(lambda z, x, y, core: (z, x, y, 1 - core)),
    exchange_pairs(lambda z, x, y, core: (z, x, 1 - y, core) if core else (z, 1 - x, y, core)),
    exchange_pairs(lambda z, x, y, core: (z, 1 - x, y, core) if core else (z, x, 1 - y, core)),
    exchange_pairs(lambda z, x, y, core: (z ^ 1, x, y, core) if core else (z ^ 2, x, y, core)),
    exchange_pairs(lambda z, x, y, core: (z ^ 2, x, y, core) if core else (z ^ 1, x, y, core)),
)


def last_pairs(*lists):
    return [
        (z * 8 + rest * 2 + core, to * 8 + rest * 2 + core)
        for core, pairs in enumerate(lists)
        for z, to in pairs
        for rest in range(4)
    ]


INWARD = last_pairs(((0, 1), (3, 2)), ((0, 2), (3, 1)))
OUTWARD = last_pairs(((1, 0), (2, 3)), ((2, 0), (1, 3)))


def swap(value, step):
    return lax.ppermute(value, ("dp", "tensor"), ROUNDS[step])


def after(value, *others):
    return lax.optimization_barrier((value, others))[0]


def picked(value, index, axis):
    return lax.dynamic_index_in_dim(value, index, axis, keepdims=False)


def total_low(*values):
    return sum(value.astype(jnp.float32) for value in values).astype(jnp.bfloat16)


def tiled(value):
    return value.reshape(2, -1, 16, UNIT)


def window_places(pieces, place, entry, other):
    z, x, y, core = place
    own_x, own_y = (1 - x, 1 - y) if other else (x, y)
    part = jnp.where(core == 0, entry, own_y)
    across = jnp.where(core == 0, own_x, entry)
    return [(part, jnp.where(across == 0, first, second), n) for first, second, n in pieces]


def first_sent(kept, received, pieces, place):
    places = [window_places(pieces, place, entry, True) for entry in range(2)]
    return sum_windows((tiled(kept), places), (tiled(received), places))


def second_sources(kept, received, second, pieces, place, own):
    z, x, y, core = place
    entry = jnp.where(core == 0, y, x)
    entry = entry if own else 1 - entry
    places = [window_places(pieces, place, entry, False)]
    return [
        (tiled(kept), places),
        (tiled(received), places),
        (second, [[(entry, 0, second.shape[1])]]),
    ]


def third_source(third):
    return (third[None], [[(0, 0, third.shape[0])]])


def inner_sources(kept, received, second, third, place, block):
    z, x, y, core = place
    entry = jnp.where(core == 0, y, x)
    part = jnp.where(core == 0, entry, y)
    across = jnp.where(core == 0, x, entry)
    (a, b, count), (c, d, _) = INNER_PIECES
    at = jnp.where(across == 0, jnp.where(block == 0, a, c), jnp.where(block == 0, b, d))
    places = [[(part, at, count)]]
    return [
        (tiled(kept), places),
        (tiled(received), places),
        (second, [[(entry, count * block, count)]]),
        (third[None], [[(0, count * block, count)]]),
    ]


def edge_sides(late, outer, place):
    z, x, y, core = place
    upper = jnp.where(core == 0, z // 2, z % 2) == 1
    tile = jnp.arange(TILES)[:, None, None]
    first = jnp.where((x == 0) | (tile < 17), late[:TILES], outer)
    last = jnp.where((x == 0) | (tile < 11), outer, late[6:])
    return jnp.where(upper, first, last), jnp.where(upper, last, first)


def along_z(value, pairs):
    return lax.ppermute(value, ("dp", "tensor"), pairs)


def gather_pieces(frame, place, prepared):
    z, x, y, core = place
    own = frame.reshape(TILES, 16, UNIT)

    def paired(value):
        return jnp.stack((value, swap(value, 1)))

    near = swap(own, 4)
    pairs = [paired(own)]
    outer = (z == 0) | (z == 3)
    far = swap(after(jnp.where(outer, own, near), pairs[0]), 3)
    rests = [swap(pairs[0], 2)]
    pairs.append(paired(near))
    last = swap(after(jnp.where(outer, near, own), far), 3)
    rests.append(swap(pairs[1], 2))
    pairs.append(paired(after(far, pairs[1], rests[0])))
    prepared = lax.optimization_barrier(prepared)
    rests.append(swap(after(pairs[2], prepared), 2))
    pairs.append(paired(after(last, pairs[2], rests[1])))
    pieces = []
    for step in range(3):
        pieces += [pairs[step], rests[step], swap(pairs[step], 0), swap(rests[step], 0)]
    rest = swap(pairs[3], 2)
    part = jnp.arange(32) // 8
    window = jnp.arange(32) % 8
    its_z, its_x, its_y, its_core = window // 2, window % 2, part // 2, part % 2
    off_x, off_y = its_x != x, its_y != y
    beside = jnp.where(its_core == 0, z ^ 1, z ^ 2)
    far_step = jnp.where((its_z == 0) | (its_z == 3), 2, 3)
    step = jnp.where(its_z == z, 0, jnp.where(its_z == beside, 1, far_step))
    which = 4 * step + 2 * (its_core != core) + jnp.where(its_core == 0, off_y, off_x)
    slot = jnp.where(its_core == 0, off_x, off_y)
    table = jnp.stack((which, slot)).astype(jnp.int32)
    return table, pieces, (pairs[3], rest), prepared


def rearranged(stack):
    def matrix(first, count, height):
        return stack[:, first : first + count].reshape(4, height, -1)

    gap = jnp.zeros((4, 768, 64), stack.dtype)
    heads = []
    for slot in range(3):
        heads += [matrix(192 * slot, 192, 768), gap]
    small = []
    for slot in range(3):
        columns = matrix(2304 + 12 * slot, 12, 192)
        small.append(spaced(columns.reshape(768, 48)).reshape(4, 192, 256))
    rows = matrix(2340, 12, 48).transpose(0, 2, 1)
    return (
        jnp.concatenate(heads, 2),
        jnp.concatenate(small, 2),
        spaced(rows.reshape(768, 48)).reshape(4, 192, 256).transpose(0, 2, 1),
        matrix(2352, 48, 192),
        matrix(2400, 48, 192),
    )


def stack_pieces(stack):
    frames = jnp.stack([stack[:, 304 * window : 304 * window + FRAME] for window in range(8)], 1)
    seam = (jnp.arange(FRAME)[:, None] >= 304) & (jnp.arange(8) < 7)[:, None, None]
    frames = jnp.where(seam, 0.0, frames).astype(stack.dtype).reshape(32, TILES, 16, UNIT)
    number = jnp.arange(32)
    return jnp.stack((number // 2, number % 2)).astype(jnp.int32), list(
        frames.reshape(16, 2, TILES, 16, UNIT)
    )


def spaced(vector):
    gap = jnp.zeros((vector.shape[0], 48), vector.dtype)
    first, second, third = vector[:, 0:16], vector[:, 16:32], vector[:, 32:48]
    return jnp.concatenate((second, gap, first, gap, gap, gap[:, :16], third, gap), 1)


def unspaced(value):
    return jnp.concatenate((value[:, 64:80], value[:, 0:16], value[:, 192:208]), 1).reshape(-1)


def shards(
    text_in,
    layout_in,
    lengths,
    text_mask,
    box_mask,
    text_cot,
    layout_cot,
    master,
    first_moment,
    second_moment,
    ema_weights,
    vectors,
    vector_first,
    vector_second,
    vector_ema,
):
    parts = lax.axis_size("tensor")
    dp_count = lax.axis_size("dp")
    tensor_index = lax.axis_index("tensor")
    dp_index = lax.axis_index("dp")
    span = master.shape[2]
    near = dp_count == 8 and parts == 4
    place = (dp_index // 2, dp_index % 2, tensor_index // 2, tensor_index % 2)
    shift = (2 * dp_index).reshape(1)
    all_parts = jnp.arange(parts, dtype=jnp.int32)
    own_parts = all_parts[::2] + place[3]
    other_parts = all_parts[::2] + 1 - place[3]
    biases = split_vector(vectors)
    length = lax.dynamic_slice_in_dim(lengths, tensor_index, 1)

    def product(spec, left, right):
        return jnp.einsum(spec, left, right, preferred_element_type=jnp.float32)

    def over_parts(spec, left, right):
        return sum(product(spec, left[part], right[part]) for part in range(parts))

    def summed(value):
        return jnp.sum(value, 0, dtype=jnp.float32)

    gap = jnp.zeros((parts, 64), jnp.float32)
    none = jnp.zeros((parts, 256), jnp.float32)
    qkv_bias = jnp.concatenate(
        (biases[0].reshape(parts, 192), gap, none, biases[1].reshape(parts, 192), gap), 1
    )
    lqkv_bias = jnp.concatenate(
        (spaced(biases[9].reshape(parts, 48)), none, spaced(biases[10].reshape(parts, 48))), 1
    )
    text_flag = (text_mask[0] > 0)[:, None]
    box_flag = (box_mask[0] > 0)[:, None]
    text_act = jnp.where(text_flag, biases[18], text_in[0].astype(jnp.float32))
    layout_act = jnp.where(box_flag, biases[19], layout_in[0].astype(jnp.float32))
    text_low = text_act.astype(jnp.bfloat16)
    layout_low = layout_act.astype(jnp.bfloat16)
    text_rows, layout_rows = vectors[:6144].reshape(8, D), vectors[9216:10752].reshape(8, L)
    up_bias, lup_bias = biases[8].reshape(parts, 1, -1), biases[17].reshape(parts, 1, -1)
    prepared = (
        length,
        qkv_bias,
        lqkv_bias,
        text_act,
        layout_act,
        text_low,
        layout_low,
        text_rows,
        layout_rows,
        up_bias,
        lup_bias,
        layout_cot,
    )
    if near:
        table, outer, inner, prepared = gather_pieces(
            cast_frame(shift, master), place, prepared
        )
        qkv_weight, lqkv_weight, lout_weight, lup_weight, ldown_weight = unpack(table, outer)
    else:
        wire = master.reshape(-1, 192).astype(jnp.bfloat16)
        stack = lax.all_gather(wire[None], ("tensor", "dp"), axis=0, tiled=True)
        stack = stack.reshape(parts, -1, UNIT)
        qkv_weight, lqkv_weight, lout_weight, lup_weight, ldown_weight = rearranged(stack)
        table, pieces = stack_pieces(stack)
    (
        length,
        qkv_bias,
        lqkv_bias,
        text_act,
        layout_act,
        text_low,
        layout_low,
        text_rows,
        layout_rows,
        up_bias,
        lup_bias,
        layout_cot,
    ) = prepared
    if near:
        pieces = outer + [*inner, swap(inner[0], 0), swap(after(inner[1], qkv_weight), 0)]
    qkv, lqkv, context, lcontext, log_total = attend(
        length,
        text_low,
        layout_low,
        qkv_weight,
        lqkv_weight,
        qkv_bias[:, None],
        lqkv_bias[:, None],
    )
    text_ahead, layout_ahead, out_weight = feed_forward(
        table,
        pieces,
        (text_act, context, None, None, up_bias, None, text_rows, text_cot),
        (
            layout_act,
            lcontext,
            lout_weight,
            lup_weight,
            lup_bias,
            ldown_weight,
            layout_rows,
            layout_cot,
        ),
    )
    text_mid_low, text_normed, text_scale, text_hidden, text_slope, text_out = text_ahead[:6]
    text_pre, text_down_in, text_sums_two = text_ahead[6:]
    layout_mid_low, layout_normed, layout_scale, layout_hidden, layout_slope = layout_ahead[:5]
    layout_out, layout_pre, layout_down_in, layout_sums_two = layout_ahead[5:]
    text_behind, layout_behind = feed_back(
        table,
        pieces,
        (
            text_pre,
            text_down_in,
            text_slope,
            text_normed,
            text_scale,
            text_rows,
            out_weight,
            None,
            None,
        ),
        (
            layout_pre,
            layout_down_in,
            layout_slope,
            layout_normed,
            layout_scale,
            layout_rows,
            lout_weight,
            ldown_weight,
            lup_weight,
        ),
    )
    text_up_grad, text_up_sums, text_pre_one, text_attn_in, text_sums_one, context_grad = text_behind
    layout_up_grad, layout_up_sums, layout_pre_one = layout_behind[:3]
    layout_attn_in, layout_sums_one, lcontext_grad = layout_behind[3:]
    early_of = (text_mid_low, text_up_grad, text_hidden, text_down_in, context, text_attn_in)
    if near:
        early_sent = early_grads(other_parts, *early_of)
        early_received = swap(early_sent, 0)
        early_kept = early_grads(after(own_parts, early_sent), *early_of)
    else:
        early_all = early_grads(all_parts, *early_of)
    if near:
        early_received = after(early_received, early_kept)
        early = (early_kept, early_received)
        inner_sent = first_sent(*early, INNER_PIECES, place)
        inner_second = swap(inner_sent, 1)
        outer_sent = first_sent(*after(early, inner_sent), OUTER_PIECES, place)
        outer_second = swap(outer_sent, 1)
        context_grad = after(context_grad, outer_sent)
    qkv_in, lqkv_in = attend_back(
        length, qkv, lqkv, log_total, context, lcontext, context_grad, lcontext_grad
    )
    late_of = [
        text_low,
        qkv_in,
        layout_low,
        lqkv_in,
        lcontext,
        layout_attn_in,
        layout_mid_low,
        layout_up_grad,
        layout_hidden,
        layout_down_in,
    ]
    if near:
        late_sent = late_grads(other_parts, *late_of)
        late_received = swap(late_sent, 0)
        inner_second = after(inner_second, late_sent)
        inner_sent = sum_windows(*second_sources(*early, inner_second, INNER_PIECES, place, False))[0]
        inner_third = swap(inner_sent, 2)
        late_kept = late_grads(after(own_parts, inner_sent), *late_of)
        late = (late_kept, after(late_received, late_kept))
        late_sent = first_sent(*late, LATE_PIECES, place)
        late_second = swap(late_sent, 1)
        outer_second = after(outer_second, late_sent)
        outer_sent = sum_windows(*second_sources(*early, outer_second, OUTER_PIECES, place, False))[0]
        outer_third = swap(outer_sent, 2)
        high, low = place[0] // 2, place[0] % 2
        side = jnp.where(place[3] == 0, 1 - high, low)
        inner_third = after(inner_third, outer_sent)
        inner = (*early, inner_second, inner_third, place)
        inner_sent = sum_windows(*inner_sources(*inner, side))[0]
        inner_fourth = swap(inner_sent, 3)
        qkv_in = after(qkv_in, inner_sent)
        text_in_back = over_parts("se,de->sd", qkv_in, qkv_weight)
        outer_third = after(outer_third, text_in_back)
        outer_sum = sum_windows(
            *second_sources(*early, outer_second, OUTER_PIECES, place, True), third_source(outer_third)
        )[0]
        late_second = after(late_second, outer_sum)
        late_sent = sum_windows(*second_sources(*late, late_second, LATE_PIECES, place, False))[0]
        late_third = swap(late_sent, 2)
        text_in_back, lqkv_in = after((text_in_back, lqkv_in), late_sent)
    else:
        late_all = late_grads(all_parts, *late_of)
        text_in_back = over_parts("se,de->sd", qkv_in, qkv_weight)
    text_full = text_pre_one + text_in_back
    layout_full = layout_pre_one + over_parts("se,de->sd", lqkv_in, lqkv_weight)
    text_in_grad = jnp.where(text_flag, 0.0, text_full)
    layout_in_grad = jnp.where(box_flag, 0.0, layout_full)
    text_embed_grad = summed(jnp.where(text_flag, text_full, 0.0))
    layout_embed_grad = summed(jnp.where(box_flag, layout_full, 0.0))
    qkv_sums = jnp.sum(qkv_in, 1, dtype=jnp.float32)
    lqkv_sums = jnp.sum(lqkv_in, 1, dtype=jnp.float32)
    vector_part = jnp.concatenate(
        [
            qkv_sums[:, 0:192].reshape(-1),
            qkv_sums[:, 512:704].reshape(-1),
            text_sums_one[:3].reshape(-1),
            text_sums_two[:3].reshape(-1),
            text_up_sums.reshape(-1),
            unspaced(lqkv_sums[:, 0:256]),
            unspaced(lqkv_sums[:, 512:768]),
            layout_sums_one[:3].reshape(-1),
            layout_sums_two[:3].reshape(-1),
            layout_up_sums.reshape(-1),
            text_embed_grad,
            layout_embed_grad,
        ]
    )
    if near:
        slices = vector_part.reshape(32, -1)
        vector_slice = summed(lax.all_to_all(slices, ("dp", "tensor"), 0, 0, tiled=True))
        inner_fourth = after(inner_fourth, vector_part)
        inner_kept = sum_windows(*inner_sources(*inner, 1 - side), third_source(inner_fourth))[0]
        inner_last = along_z(inner_kept, INWARD)
        late_third = after(late_third, inner_kept)
        late_sum = sum_windows(
            *second_sources(*late, late_second, LATE_PIECES, place, True), third_source(late_third)
        )[0]
        edge_sent, edge_kept = edge_sides(late_sum, outer_sum, place)
        edge_fourth = swap(edge_sent, 3)
        edge_kept = total_low(edge_kept, edge_fourth)
        edge_last = along_z(edge_kept, OUTWARD)
        span_grad, shared = finish(
            jnp.stack((2 * dp_index, dp_index)),
            jnp.pad(vector_slice, (0, 512 - vector_slice.shape[0])).reshape(1, 512),
            *(
                item.reshape(FRAME, UNIT)
                for item in (inner_kept, inner_last, edge_kept, edge_last)
            ),
        )
        shared = lax.all_to_all(shared, ("dp", "tensor"), 0, 0, tiled=True)
        vector_grad = shared[:, : vector_slice.shape[0]].reshape(-1)
        matrix_square = jnp.sum(shared[:, 512:])
    else:
        flat_grad = jnp.concatenate(
            (late_all[:, :576], early_all[:, :1728], late_all[:, 576:]), 1
        ).reshape(parts * dp_count, -1, 192)
        span_grad = lax.psum_scatter(flat_grad, ("tensor", "dp"), scatter_dimension=0, tiled=True)
        span_grad = span_grad.astype(jnp.float32).reshape(master.shape)
        vector_grad = lax.psum(vector_part, ("dp", "tensor"))
        matrix_square = lax.psum(jnp.sum(span_grad * span_grad), ("dp", "tensor"))
    grad_norm = jnp.sqrt(matrix_square + jnp.sum(vector_grad * vector_grad))
    factor = clip_bound / jnp.maximum(grad_norm, clip_bound)
    if near:
        matrix_new = adam(
            (dp_index * span).reshape(1),
            shared,
            master,
            span_grad,
            first_moment,
            second_moment,
            ema_weights,
        )
        matrix_new = tuple(matrix_new)
    else:
        rates = lax.dynamic_slice_in_dim(rate_table(parts), dp_index * span, span)
        matrix_new = adam_update(
            master,
            span_grad,
            first_moment,
            second_moment,
            ema_weights,
            rates.reshape(master.shape),
            factor,
        )
    vector_new = adam_update(
        vectors, vector_grad, vector_first, vector_second, vector_ema, vector_rate, factor
    )
    return (
        (
            text_out,
            layout_out,
            text_in_grad[None],
            layout_in_grad[None],
            grad_norm,
        )
        + matrix_new
        + vector_new
    )


def solution(mesh):
    in_specs = (
        P(("dp", "tensor"), None, None),
        P(("dp", "tensor"), None, None),
        P("dp"),
        P(("dp", "tensor"), None),
        P(("dp", "tensor"), None),
        P(("dp", "tensor"), None, None),
        P(("dp", "tensor"), None, None),
        P("tensor", "dp", None),
        P("tensor", "dp", None),
        P("tensor", "dp", None),
        P("tensor", "dp", None),
        P(),
        P(),
        P(),
        P(),
    )
    out_specs = (
        P(("dp", "tensor"), None, None),
        P(("dp", "tensor"), None, None),
        P(("dp", "tensor"), None, None),
        P(("dp", "tensor"), None, None),
        P(),
        P("tensor", "dp", None),
        P("tensor", "dp", None),
        P("tensor", "dp", None),
        P("tensor", "dp", None),
        P("tensor", "dp", None),
        P(),
        P(),
        P(),
        P(),
        P(),
    )
    return jax.shard_map(shards, mesh=mesh, in_specs=in_specs, out_specs=out_specs, check_vma=False)
```
